32 devices in a mesh: fsdp: 8 (over z, core), tp: 4 (over y, x).
Axes of the slice: x: 2, y: 2, z: 4, core: 2. Of those that a mesh axis runs over, the one named last changes fastest.
Arguments:
- layer_input: bfloat16 [8192, 2048], P(('fsdp', 'tp')), may hold values from -6 to 6
- cotangent: bfloat16 [8192, 2048], P(('fsdp', 'tp')), may hold values from -6 to 6
- segment_ids: int32 [8192], P('fsdp'), may hold values from 0 to 12, as said below
- path_positions: int32 [8192], P('fsdp'), may hold values from 0 to 383, as said below
- ancestor_masks: int32 [8, 13, 13], P('fsdp'), may hold values from 0 to 1, as said below
- attn_gain: bfloat16 [2048], P('fsdp'), may hold values from 0.5 to 1.5
- query_weight: bfloat16 [2048, 2048], P('fsdp', 'tp'), may hold values from -0.125 to 0.125
- key_weight: bfloat16 [2048, 512], P('fsdp', 'tp'), may hold values from -0.125 to 0.125
- value_weight: bfloat16 [2048, 512], P('fsdp', 'tp'), may hold values from -0.125 to 0.125
- out_weight: bfloat16 [2048, 2048], P('tp', 'fsdp'), may hold values from -1.5 to 1.5
- mlp_gain: bfloat16 [2048], P('fsdp'), may hold values from 0.5 to 1.5
- gate_weight: bfloat16 [2048, 8192], P('fsdp', 'tp'), may hold values from -0.125 to 0.125
- up_weight: bfloat16 [2048, 8192], P('fsdp', 'tp'), may hold values from -0.125 to 0.125
- down_weight: bfloat16 [8192, 2048], P('tp', 'fsdp'), may hold values from -0.0625 to 0.0625
Outputs:
- output: bfloat16 [8192, 2048], P(('fsdp', 'tp'))
- input_grad: float32 [8192, 2048], P(('fsdp', 'tp'))
- attn_gain_grad: float32 [2048], P('fsdp')
- query_grad: float32 [2048, 2048], P('fsdp', 'tp')
- key_grad: float32 [2048, 512], P('fsdp', 'tp')
- value_grad: float32 [2048, 512], P('fsdp', 'tp')
- out_grad: float32 [2048, 2048], P('tp', 'fsdp')
- mlp_gain_grad: float32 [2048], P('fsdp')
- gate_grad: float32 [2048, 8192], P('fsdp', 'tp')
- up_grad: float32 [2048, 8192], P('fsdp', 'tp')
- down_grad: float32 [8192, 2048], P('tp', 'fsdp')
The draws below stay inside these ranges and needn't reach their ends.
Inputs may be any that keep to these rules, and one draw needn't show every extreme that they name: `segment_ids`: in each tree the trunk, segment 0, fills the first 256 rows; segments 1 to 4 are branches and the rest leaves, each filling one aligned run of 64 rows, in any order. `path_positions`: trunk rows count from 0; a branch's rows from 256, a leaf's from (5) * 64. `ancestor_masks`: the trunk is the parent of every branch, each branch the parent of two leaves; a segment counts as its own ancestor.
All inputs are finite; a program needn't handle non-finite values.
Results may differ from the reference program's by a relative error of at most 0.019.
Values may be sent and summed in bfloat16 or wider, within the bound.
A program may use at most 320 MiB of HBM per device.

```python
import math
import jax
import jax.numpy as jnp
import numpy as np
from jax import lax

D = 2048
H = 32
KV = 8
HD = 64
FF = 8192
SEG = 64
TRUNK_BLK = 4
BRANCHES = 4
LEAVES = 8
SEGS = 13
TREE = 1024
TREES = 8
TOKENS = 8192


def tree_layout(key):
    block_count = TRUNK_BLK + BRANCHES + LEAVES

    def one_tree(tree_index):
        tree_key = jax.random.fold_in(jax.random.fold_in(key, 901), tree_index)
        order = jax.random.permutation(jax.random.fold_in(tree_key, 1), BRANCHES + LEAVES)
        leaf_order = jax.random.permutation(jax.random.fold_in(tree_key, 2), LEAVES)
        block_segment = jnp.concatenate([jnp.zeros((TRUNK_BLK,), jnp.int32), (order + 1).astype(jnp.int32)])
        depth_start = jnp.where(block_segment <= BRANCHES, TRUNK_BLK * SEG, (TRUNK_BLK + 1) * SEG)
        block_start = jnp.where(block_segment == 0, jnp.arange(block_count, dtype=jnp.int32) * SEG, depth_start)
        token_segment = jnp.repeat(block_segment, SEG, total_repeat_length=TREE)
        within = jnp.tile(jnp.arange(SEG, dtype=jnp.int32), block_count)
        token_position = jnp.repeat(block_start, SEG, total_repeat_length=TREE) + within
        parent = jnp.concatenate([jnp.zeros((1 + BRANCHES,), jnp.int32), (1 + leaf_order // 2).astype(jnp.int32)])
        segment_range = jnp.arange(SEGS, dtype=jnp.int32)
        ancestor = (segment_range[:, None] == segment_range[None, :]) | (segment_range[None, :] == 0) | (parent[:, None] == segment_range[None, :])
        return (token_segment.astype(jnp.int32), token_position.astype(jnp.int32), ancestor.astype(jnp.int32))
    return jax.vmap(one_tree)(jnp.arange(TREES, dtype=jnp.int32))


def draw_segment_ids(key, part):
    return tree_layout(key)[0].reshape(TREES * TREE)


def draw_path_positions(key, part):
    return tree_layout(key)[1].reshape(TREES * TREE)


def draw_ancestor_masks(key, part):
    return tree_layout(key)[2]


def raised(values, own_key, source, target, parts, factor):
    def block_of(position):
        return (jnp.arange(values.shape[position]) // (values.shape[position] // parts)).reshape((-1,) + (1,) * (values.ndim - 1 - position))

    first = jax.random.permutation(own_key, parts)[block_of(target)]
    other_side = (block_of(target) + parts // 2) % parts
    return jnp.where((block_of(source) == first) | (block_of(source) == other_side), factor * values, values)


def steps_of(rng, dims, cuts, least, high):
    gain = 1.0
    for axis_at, parts in cuts:
        heights = jax.random.uniform(jax.random.fold_in(jax.random.fold_in(rng, 6), axis_at), (parts,), jnp.float32, least / len(cuts), high / len(cuts))
        gain = gain * jnp.repeat(jnp.exp(heights), dims[axis_at] // parts).reshape((-1,) + (1,) * (len(dims) - 1 - axis_at))
    return gain


def scatter_about(own_key, extent, width, most, shards=(), held_as=jnp.bfloat16):
    entries = jax.random.normal(own_key, extent, jnp.float32) * width
    if len(shards) > 0:
        entries = steps_of(own_key, extent, shards, -0.22, 0.18) * entries
    return jnp.clip(entries, min=-most, max=most).astype(held_as)


def bell_draw_with(stream_key, shape, scale, most, split, heavy, held_as=jnp.bfloat16):
    values = scale * jax.random.normal(stream_key, shape, jnp.float32)
    if split:
        values = values * steps_of(stream_key, shape, split, -0.22, 0.18)
    return jnp.clip(raised(values, jax.random.fold_in(stream_key, 3), *heavy), -most, most).astype(held_as)


def setup_inputs(seed: int = 0) -> dict:
    keys = jax.random.split(jax.random.key(seed), 15)
    return {
        "layer_input": scatter_about(keys[0], (TOKENS, D), 1.0, 6.0, ((0, 32),)),
        "cotangent": bell_draw_with(keys[1], (TOKENS, D), 1.0, 6.0, ((0, 32),), (0, 1, 32, 2.75)),
        "segment_ids": draw_segment_ids(jax.random.fold_in(keys[14], 71), 0),
        "path_positions": draw_path_positions(jax.random.fold_in(keys[14], 71), 0),
        "ancestor_masks": draw_ancestor_masks(jax.random.fold_in(keys[14], 71), 0),
        "attn_gain": jnp.clip(1.0 + 0.1 * jax.random.normal(keys[5], (D,), jnp.float32), 0.5, 1.5).astype(jnp.bfloat16),
        "query_weight": scatter_about(keys[6], (D, H * HD), D ** -0.5, 0.125, ((0, 8), (1, 4))),
        "key_weight": scatter_about(keys[7], (D, KV * HD), D ** -0.5, 0.125, ((0, 8), (1, 4))),
        "value_weight": scatter_about(keys[8], (D, KV * HD), D ** -0.5, 0.125, ((0, 8), (1, 4))),
        "out_weight": scatter_about(keys[9], (H * HD, D), (max(D // 128, 2)) ** -0.5, 1.5, ((0, 4), (1, 8))),
        "mlp_gain": jnp.clip(1.0 + 0.1 * jax.random.normal(keys[10], (D,), jnp.float32), 0.5, 1.5).astype(jnp.bfloat16),
        "gate_weight": scatter_about(keys[11], (D, FF), D ** -0.5, 0.125, ((0, 8), (1, 4))),
        "up_weight": scatter_about(keys[12], (D, FF), D ** -0.5, 0.125, ((0, 8), (1, 4))),
        "down_weight": scatter_about(keys[13], (FF, D), FF ** -0.5, 0.0625, ((0, 4), (1, 8))),
    }


EPSILON = 1e-05

@jax.custom_vjp
def low(v):
    return lax.optimization_barrier(v.astype(jnp.bfloat16)).astype(jnp.float32)

@jax.custom_vjp
def low_back(v):
    return v

def low_keep(v):
    return (low(v), None)

def low_pass(kept, grad):
    return (grad,)

def back_keep(v):
    return (v, None)

def back_low(kept, grad):
    return (low(grad),)
low.defvjp(low_keep, low_pass)
low_back.defvjp(back_keep, back_low)

def inverse_freq(head_size):
    base_freq = 1.0 / 500000.0 ** (np.arange(0, head_size, 2) / head_size)
    wavelen = 2.0 * math.pi / base_freq
    smooth = (8192.0 / wavelen - 1.0) / 3.0
    blended = (1.0 - smooth) * base_freq / 32.0 + smooth * base_freq
    scaled = np.where(wavelen > 8192.0, base_freq / 32.0, np.where(wavelen < 2048.0, base_freq, blended))
    return scaled.astype(np.float32)

def rope_tables(positions, head_size):
    freqs = jnp.asarray(inverse_freq(head_size))
    angles = positions.astype(jnp.float32)[:, None] * freqs[None, :]
    angles = jnp.concatenate([angles, angles], axis=-1)
    return (jnp.cos(angles), jnp.sin(angles))

def rotate_half(values):
    half_size = values.shape[-1] // 2
    return jnp.concatenate([-values[..., half_size:], values[..., :half_size]], axis=-1)

def apply_rope(values, cosine_table, sine_table):
    return values * cosine_table[:, None, :] + rotate_half(values) * sine_table[:, None, :]

def rms_scale(row_values):
    return lax.rsqrt(lax.optimization_barrier(jnp.mean(row_values * row_values, axis=-1, keepdims=True)) + EPSILON)

def matmul(left, right):
    return jnp.dot(left, right, precision=lax.Precision.HIGHEST, preferred_element_type=jnp.float32)

def head_group(query_group, key_head, value_head, allowed, score_scale):
    raw_scores = jnp.einsum('igd,jd->gij', query_group, key_head, precision=lax.Precision.HIGHEST) * score_scale
    scores = low_back(raw_scores)
    masked = jnp.where(allowed[None], scores, -1e+30)
    row_max = lax.optimization_barrier(jnp.max(masked, axis=-1, keepdims=True))
    exponent = jnp.exp(masked - row_max)
    weights_soft = exponent / lax.optimization_barrier(jnp.sum(exponent, axis=-1, keepdims=True))
    probs_low = low(weights_soft)
    mixture = jnp.einsum('gij,jd->igd', probs_low, value_head, precision=lax.Precision.HIGHEST)
    return low(low_back(mixture))

def tree_forward(tree_rows, params, allowed, cosine_table, sine_table):
    attn_gain, query_weight, key_weight, value_weight, out_weight, mlp_gain, gate_weight, up_weight, down_weight = params
    row_count = tree_rows.shape[0]
    first_normed = low(tree_rows * rms_scale(tree_rows) * attn_gain)
    queries = low(apply_rope(low_back(matmul(first_normed, query_weight)).reshape(row_count, H, HD), cosine_table, sine_table))
    key_rows = low(apply_rope(low_back(matmul(first_normed, key_weight)).reshape(row_count, KV, HD), cosine_table, sine_table))
    value_rows = low(low_back(matmul(first_normed, value_weight))).reshape(row_count, KV, HD)
    grouped = queries.reshape(row_count, KV, H // KV, HD).transpose(1, 0, 2, 3)
    score_scale = HD ** (-0.5)
    attend = jax.checkpoint(lambda member: head_group(member[0], member[1], member[2], allowed, score_scale))
    mixture = lax.map(attend, (grouped, key_rows.transpose(1, 0, 2), value_rows.transpose(1, 0, 2)))
    attended = mixture.transpose(1, 0, 2, 3).reshape(row_count, H * HD)
    residual = tree_rows + low_back(matmul(attended, out_weight))
    second_normed = low(residual * rms_scale(residual) * mlp_gain)
    gate_proj = low_back(matmul(second_normed, gate_weight))
    up_proj = low_back(matmul(second_normed, up_weight))
    hidden = low(jax.nn.silu(gate_proj) * up_proj)
    return residual + low_back(matmul(hidden, down_weight))

def reference(layer_input, cotangent, segment_ids, path_positions, ancestor_masks, attn_gain, query_weight, key_weight, value_weight, out_weight, mlp_gain, gate_weight, up_weight, down_weight):
    params = (attn_gain.astype(jnp.float32), query_weight.astype(jnp.float32), key_weight.astype(jnp.float32), value_weight.astype(jnp.float32), out_weight.astype(jnp.float32), mlp_gain.astype(jnp.float32), gate_weight.astype(jnp.float32), up_weight.astype(jnp.float32), down_weight.astype(jnp.float32))
    tree_inputs = layer_input.astype(jnp.float32).reshape(TREES, TREE, D)
    tree_cotangent = cotangent.astype(jnp.float32).reshape(TREES, TREE, D)
    tree_segments = segment_ids.reshape(TREES, TREE)
    tree_positions = path_positions.reshape(TREES, TREE)
    row_index = jnp.arange(TREE)

    def one_tree(totals, member):
        inputs_tree, cot_tree, seg_tree, pos_tree, anc_tree = member
        same_segment = seg_tree[:, None] == seg_tree[None, :]
        reach = anc_tree[seg_tree[:, None], seg_tree[None, :]] == 1
        allowed = reach & (~same_segment | (row_index[None, :] <= row_index[:, None]))
        cosine_table, sine_table = rope_tables(pos_tree, HD)

        def forward(tree_rows, weight_list):
            return tree_forward(tree_rows, weight_list, allowed, cosine_table, sine_table)
        result, pullback = jax.vjp(forward, inputs_tree, params)
        rows_grad, param_grads = pullback(cot_tree)
        totals = tuple((running + fresh for running, fresh in zip(totals, param_grads)))
        return (totals, (result.astype(jnp.bfloat16), rows_grad))
    zeros_init = tuple((jnp.zeros_like(param) for param in params))
    totals, stacked = lax.scan(one_tree, zeros_init, (tree_inputs, tree_cotangent, tree_segments, tree_positions, ancestor_masks))
    output = stacked[0].reshape(TOKENS, D)
    input_grad = stacked[1].reshape(TOKENS, D)
    return (output, input_grad, totals[0], totals[1], totals[2], totals[3], totals[4], totals[5], totals[6], totals[7], totals[8])
```

```python
import functools
import math

import jax
import jax.numpy as jnp
import numpy as np
from jax import lax
from jax.experimental import pallas as pl
from jax.experimental.pallas import tpu as pltpu
from jax.sharding import PartitionSpec as P

HD = 64
SEGS = 13
SEG = 64
TRUNK = 256
BRANCHES = 4
EPSILON = 1e-05
PARTS = (3, 3, 2)
HOPS = 1
NEG = -1e30
BF = jnp.bfloat16
F32 = jnp.float32


def inverse_freq(head_size):
    base_freq = 1.0 / 500000.0 ** (np.arange(0, head_size, 2) / head_size)
    wavelen = 2.0 * math.pi / base_freq
    smooth = (8192.0 / wavelen - 1.0) / 3.0
    blended = (1.0 - smooth) * base_freq / 32.0 + smooth * base_freq
    scaled = np.where(
        wavelen > 8192.0, base_freq / 32.0, np.where(wavelen < 2048.0, base_freq, blended)
    )
    return scaled.astype(np.float32)


def dot_nn(left, right):
    return lax.dot_general(
        left, right, (((1,), (0,)), ((), ())), preferred_element_type=F32
    )


def dot_nt(left, right):
    return lax.dot_general(
        left, right, (((1,), (1,)), ((), ())), preferred_element_type=F32
    )


def dot_tn(left, right):
    return lax.dot_general(
        left, right, (((0,), (0,)), ((), ())), preferred_element_type=F32
    )


def rope_lanes(values, cosine, signed_sine, low_half):
    rolled = jnp.where(low_half, pltpu.roll(values, 96, 1), pltpu.roll(values, 32, 1))
    return values * cosine + rolled * signed_sine


def rope_lanes_back(grads, cosine, signed_sine, low_half):
    scaled = grads * signed_sine
    rolled = jnp.where(low_half, pltpu.roll(scaled, 96, 1), pltpu.roll(scaled, 32, 1))
    return grads * cosine + rolled


def low_half_mask(rows):
    lane = lax.broadcasted_iota(jnp.int32, (rows, 128), 1)
    return lax.rem(lane, HD) < HD // 2


def parent_block(mask_ref, seg_ref, segment, block_count):
    parent = jnp.int32(0)
    for branch in range(1, BRANCHES + 1):
        parent = parent + branch * mask_ref[segment * SEGS + branch]
    parent = jnp.where(segment > BRANCHES, parent, segment)
    found = jnp.int32(0)
    for block in range(block_count):
        found = found + block * (seg_ref[block] == parent).astype(jnp.int32)
    return found


def block_mask(has_parent, members):
    shape = (members * SEG, 2 * SEG)
    row = lax.rem(lax.broadcasted_iota(jnp.int32, shape, 0), SEG)
    col = lax.broadcasted_iota(jnp.int32, shape, 1)
    return ((col < SEG) & has_parent) | ((col >= SEG) & (col - SEG <= row))


def trunk_mask(index, members):
    shape = (members * SEG, TRUNK)
    row = lax.rem(lax.broadcasted_iota(jnp.int32, shape, 0), SEG) + index * SEG
    col = lax.broadcasted_iota(jnp.int32, shape, 1)
    return col <= row


def softmax_rows(scores):
    row_max = jnp.max(scores, axis=-1, keepdims=True)
    exponent = jnp.exp(scores - row_max)
    return exponent / jnp.sum(exponent, axis=-1, keepdims=True)


def attn_fwd_kernel(
    heads, groups, mask_ref, seg_ref, base_ref, pre_ref, cos_ref, sin_ref,
    att_ref, q_ref, k_ref, v_ref,
):
    rows = pre_ref.shape[0]
    blocks = rows // SEG
    members = heads // groups
    score_scale = HD ** (-0.5)
    low_half = low_half_mask(rows)
    cosine = cos_ref[...]
    sine = sin_ref[...]
    q_width = heads * HD
    kv_width = groups * HD

    def put_heads(dest, first, wide, count):
        for half in range(count):
            head = first + half
            part = wide[:, half * HD : (half + 1) * HD].reshape(blocks, SEG, HD)
            group, member = head // members, head % members
            dest[group, :, member * SEG : (member + 1) * SEG, :] = part

    for pair in range(q_width // 128):
        lanes = pre_ref[:, pair * 128 : (pair + 1) * 128]
        put_heads(q_ref, 2 * pair, rope_lanes(lanes, cosine, sine, low_half).astype(BF), 2)
    if kv_width % 128 == 0:
        for pair in range(kv_width // 128):
            at = q_width + pair * 128
            wide = rope_lanes(pre_ref[:, at : at + 128], cosine, sine, low_half).astype(BF)
            at = q_width + kv_width + pair * 128
            plain = pre_ref[:, at : at + 128].astype(BF)
            for half in range(2):
                k_ref[2 * pair + half] = wide[:, half * HD : (half + 1) * HD]
                v_ref[2 * pair + half] = plain[:, half * HD : (half + 1) * HD]
    else:
        both = pre_ref[:, q_width : q_width + 128]
        k_ref[0] = rope_lanes(both, cosine, sine, low_half).astype(BF)[:, :HD]
        v_ref[0] = both.astype(BF)[:, HD:]

    base = base_ref[0]
    trunk_block = base // SEG
    trunk_rows = pl.ds(pl.multiple_of(base, TRUNK), TRUNK)

    def store(group, block, mixed):
        at = pl.ds(pl.multiple_of(block * SEG, SEG), SEG)
        for member in range(members):
            head = group * members + member
            att_ref[at, head * HD : (head + 1) * HD] = mixed[
                member * SEG : (member + 1) * SEG
            ].astype(BF)

    for group in range(groups):
        def one_block(block, carry):
            inside = block - trunk_block
            is_trunk = (inside >= 0) & (inside < TRUNK // SEG)

            @pl.when(is_trunk)
            def _():
                queries = q_ref[group, block]
                scores = dot_nt(queries, k_ref[group, trunk_rows, :]) * score_scale
                scores = jnp.where(trunk_mask(inside, members), scores, NEG)
                probs = softmax_rows(scores).astype(BF)
                store(group, block, dot_nn(probs, v_ref[group, trunk_rows, :]))

            @pl.when(jnp.logical_not(is_trunk))
            def _():
                segment = seg_ref[block]
                parent = parent_block(mask_ref, seg_ref, segment, blocks)
                up = pl.ds(pl.multiple_of(parent * SEG, SEG), SEG)
                own = pl.ds(pl.multiple_of(block * SEG, SEG), SEG)
                queries = q_ref[group, block]
                keys = jnp.concatenate(
                    [k_ref[group, trunk_rows, :], k_ref[group, up, :], k_ref[group, own, :]], axis=0
                )
                vals = jnp.concatenate(
                    [v_ref[group, trunk_rows, :], v_ref[group, up, :], v_ref[group, own, :]], axis=0
                )
                scores = dot_nt(queries, keys) * score_scale
                tail = jnp.where(
                    block_mask(segment > BRANCHES, members), scores[:, TRUNK:], NEG
                )
                scores = jnp.concatenate([scores[:, :TRUNK], tail], axis=1)
                probs = softmax_rows(scores).astype(BF)
                store(group, block, dot_nn(probs, vals))

            return carry

        lax.fori_loop(0, blocks, one_block, 0)


def attn_bwd_kernel(
    heads, groups, mask_ref, seg_ref, base_ref, q_ref, k_ref, v_ref, grad_ref, cos_ref, sin_ref,
    out_ref, g_ref, dq_ref, dk_ref, dv_ref,
):
    rows = grad_ref.shape[0]
    blocks = rows // SEG
    members = heads // groups
    score_scale = HD ** (-0.5)
    low_half = low_half_mask(rows)
    cosine = cos_ref[...]
    sine = sin_ref[...]
    q_width = heads * HD
    kv_width = groups * HD
    for head in range(heads):
        part = grad_ref[:, head * HD : (head + 1) * HD].reshape(blocks, SEG, HD)
        group, member = head // members, head % members
        g_ref[group, :, member * SEG : (member + 1) * SEG, :] = part
    dk_ref[...] = jnp.zeros_like(dk_ref)
    dv_ref[...] = jnp.zeros_like(dv_ref)
    base = base_ref[0]
    trunk_block = base // SEG
    trunk_rows = pl.ds(pl.multiple_of(base, TRUNK), TRUNK)

    def store(group, block, d_query):
        at = pl.ds(pl.multiple_of(block * SEG, SEG), SEG)
        for member in range(members):
            head = group * members + member
            dq_ref[at, head * HD : (head + 1) * HD] = d_query[member * SEG : (member + 1) * SEG]

    for group in range(groups):
        lanes = slice(group * HD, (group + 1) * HD)

        def grads(queries, out_grads, keys, vals, scores):
            probs = softmax_rows(scores)
            prob_back = dot_nt(out_grads, vals)
            delta = jnp.sum(probs * prob_back, axis=-1, keepdims=True)
            score_back = (probs * (prob_back - delta)).astype(BF)
            d_query = dot_nn(score_back, keys) * score_scale
            d_key = dot_tn(score_back, queries) * score_scale
            d_val = dot_tn(probs.astype(BF), out_grads)
            return d_query, d_key, d_val

        def one_block(block, carry):
            inside = block - trunk_block
            is_trunk = (inside >= 0) & (inside < TRUNK // SEG)

            @pl.when(is_trunk)
            def _():
                queries = q_ref[group, block]
                keys = k_ref[group, trunk_rows, :]
                scores = dot_nt(queries, keys) * score_scale
                scores = jnp.where(trunk_mask(inside, members), scores, NEG)
                d_query, d_key, d_val = grads(
                    queries, g_ref[group, block], keys, v_ref[group, trunk_rows, :], scores
                )
                store(group, block, d_query)
                dk_ref[trunk_rows, lanes] += d_key
                dv_ref[trunk_rows, lanes] += d_val

            @pl.when(jnp.logical_not(is_trunk))
            def _():
                segment = seg_ref[block]
                parent = parent_block(mask_ref, seg_ref, segment, blocks)
                up = pl.ds(pl.multiple_of(parent * SEG, SEG), SEG)
                own = pl.ds(pl.multiple_of(block * SEG, SEG), SEG)
                queries = q_ref[group, block]
                keys = jnp.concatenate(
                    [k_ref[group, trunk_rows, :], k_ref[group, up, :], k_ref[group, own, :]], axis=0
                )
                vals = jnp.concatenate(
                    [v_ref[group, trunk_rows, :], v_ref[group, up, :], v_ref[group, own, :]], axis=0
                )
                scores = dot_nt(queries, keys) * score_scale
                tail = jnp.where(
                    block_mask(segment > BRANCHES, members), scores[:, TRUNK:], NEG
                )
                scores = jnp.concatenate([scores[:, :TRUNK], tail], axis=1)
                d_query, d_key, d_val = grads(queries, g_ref[group, block], keys, vals, scores)
                store(group, block, d_query)
                for ref, val in ((dk_ref, d_key), (dv_ref, d_val)):
                    ref[trunk_rows, lanes] += val[:TRUNK]
                    ref[up, lanes] += val[TRUNK : TRUNK + SEG]
                    ref[own, lanes] += val[TRUNK + SEG :]

            return carry

        lax.fori_loop(0, blocks, one_block, 0)
    for pair in range(q_width // 128):
        at = slice(pair * 128, (pair + 1) * 128)
        out_ref[:, at] = rope_lanes_back(dq_ref[:, at], cosine, sine, low_half).astype(BF)
    if kv_width % 128 == 0:
        for pair in range(kv_width // 128):
            at = slice(pair * 128, (pair + 1) * 128)
            turned = rope_lanes_back(dk_ref[:, at], cosine, sine, low_half)
            out_ref[:, q_width + pair * 128 : q_width + (pair + 1) * 128] = turned.astype(BF)
            first = q_width + kv_width + pair * 128
            out_ref[:, first : first + 128] = dv_ref[:, at].astype(BF)
    else:
        wide = jnp.concatenate([dk_ref[...], dv_ref[...]], axis=1)
        turned = rope_lanes_back(wide, cosine, sine, low_half)
        lane = lax.broadcasted_iota(jnp.int32, (rows, 128), 1)
        out_ref[:, q_width : q_width + 128] = jnp.where(lane < HD, turned, wide).astype(BF)


SMEM = pl.BlockSpec(memory_space=pltpu.SMEM)
VMEM = pl.BlockSpec(memory_space=pltpu.VMEM)


def attention_forward(heads, groups, masks, segs, base, pre, cosine, sine):
    rows = pre.shape[0]
    members = heads // groups
    blocks = rows // SEG
    return pl.pallas_call(
        functools.partial(attn_fwd_kernel, heads, groups),
        name="attn_fwd",
        out_shape=(
            jax.ShapeDtypeStruct((rows, heads * HD), BF),
            jax.ShapeDtypeStruct((groups, blocks, members * SEG, HD), BF),
            jax.ShapeDtypeStruct((groups, rows, HD), BF),
            jax.ShapeDtypeStruct((groups, rows, HD), BF),
        ),
        in_specs=[SMEM, SMEM, SMEM, VMEM, VMEM, VMEM],
        out_specs=(VMEM, VMEM, VMEM, VMEM),
        compiler_params=pltpu.CompilerParams(vmem_limit_bytes=40 << 20),
        cost_estimate=pl.CostEstimate(
            flops=8_000_000_000, bytes_accessed=8_000_000, transcendentals=3_000_000
        ),
    )(masks, segs, base, pre, cosine, sine)


def attention_backward(heads, groups, masks, segs, base, queries, keys, vals, grads, cosine, sine):
    rows = grads.shape[0]
    members = heads // groups
    blocks = rows // SEG
    return pl.pallas_call(
        functools.partial(attn_bwd_kernel, heads, groups),
        name="attn_bwd",
        out_shape=jax.ShapeDtypeStruct((rows, (heads + 2 * groups) * HD), BF),
        in_specs=[SMEM, SMEM, SMEM, VMEM, VMEM, VMEM, VMEM, VMEM, VMEM],
        out_specs=VMEM,
        scratch_shapes=[
            pltpu.VMEM((groups, blocks, members * SEG, HD), BF),
            pltpu.VMEM((rows, heads * HD), F32),
            pltpu.VMEM((rows, groups * HD), F32),
            pltpu.VMEM((rows, groups * HD), F32),
        ],
        compiler_params=pltpu.CompilerParams(vmem_limit_bytes=40 << 20),
        cost_estimate=pl.CostEstimate(
            flops=20_000_000_000, bytes_accessed=8_000_000, transcendentals=3_000_000
        ),
    )(masks, segs, base, queries, keys, vals, grads, cosine, sine)


def chunk_kernel(steps, slabs, halves, added, last, order_ref, *refs):
    rows_ref, cot_ref, full_ref, rows_turned_ref, cot_turned_ref = refs[:5]
    refs = refs[5:]
    if added:
        (back_in_ref, out_in_ref), refs = refs[:2], refs[2:]
    grad_refs, refs = refs[:halves], refs[halves:]
    back_ref, out_ref, pair_ref, hidden_ref = refs
    step = pl.program_id(0)
    chunk = hidden_ref.shape[1]
    tile = chunk // steps
    height = rows_turned_ref.shape[0]

    for at in range(steps):

        @pl.when(step == at)
        def _():
            cut = slice(at * tile, (at + 1) * tile)
            gate = dot_nn(rows_ref[...], full_ref[:, cut])
            up = dot_nn(rows_ref[...], full_ref[:, chunk + at * tile : chunk + (at + 1) * tile])
            back = dot_nn(
                cot_ref[...], full_ref[:, 2 * chunk + at * tile : 2 * chunk + (at + 1) * tile]
            )
            sigmoid = 1.0 / (1.0 + jnp.exp(-gate))
            silu = gate * sigmoid
            hidden_ref[:, cut] = (silu * up).astype(BF)
            pair_ref[:, cut] = (back * up * sigmoid * (1.0 + gate * (1.0 - sigmoid))).astype(BF)
            pair_ref[:, chunk + at * tile : chunk + (at + 1) * tile] = (back * silu).astype(BF)

    def write(grad_ref):
        grad = jnp.concatenate(
            [
                dot_nn(rows_turned_ref[...], pair_ref[...]).astype(BF),
                dot_nn(cot_turned_ref[...], hidden_ref[...]).astype(BF),
            ],
            axis=1,
        )
        grad_ref[...] = grad.reshape(grad_ref.shape)

    @pl.when(step >= steps)
    def _():
        slab = pl.ds(pl.multiple_of(order_ref[step - steps] * height, height), height)
        back = dot_nt(pair_ref[...], full_ref[slab, : 2 * chunk])
        out = dot_nt(hidden_ref[...], full_ref[slab, 2 * chunk :])
        back = back_in_ref[...] + back if added else back
        out = out_in_ref[...] + out if added else out
        back_ref[...] = back.astype(back_ref.dtype)
        out_ref[...] = out.astype(out_ref.dtype)
        if halves == 1:
            write(grad_refs[0])

    if halves == 2:

        @pl.when((step >= steps) & (step < steps + slabs // 2))
        def _():
            write(grad_refs[0])

        @pl.when(step >= steps + slabs // 2)
        def _():
            write(grad_refs[1])


def chunk_pass(order, halves, rows, cot, full, rows_turned, cot_turned, sums, last):
    count, depth = rows.shape
    width = full.shape[1]
    chunk = width // 3
    slabs = order.shape[0]
    height = depth // slabs
    steps = max(1, chunk // 256)
    added = sums is not None
    whole = pl.BlockSpec(memory_space=pltpu.VMEM)

    def place(i):
        return jnp.maximum(i - steps, 0)

    turned = pl.BlockSpec((height, count), lambda i, order: (order[place(i)], 0))
    column = pl.BlockSpec((count, height), lambda i, order: (0, order[place(i)]))
    if halves == 2:
        half = slabs // 2
        grad_shapes = [jax.ShapeDtypeStruct((half, height, width), BF)] * 2
        grad_specs = [
            pl.BlockSpec(
                (1, height, width), lambda i, order: (jnp.minimum(place(i), half - 1), 0, 0)
            ),
            pl.BlockSpec(
                (1, height, width), lambda i, order: (jnp.maximum(place(i) - half, 0), 0, 0)
            ),
        ]
    else:
        grad_shapes = [jax.ShapeDtypeStruct((depth, width), BF)]
        grad_specs = [pl.BlockSpec((height, width), lambda i, order: (order[place(i)], 0))]
    total = jax.ShapeDtypeStruct((count, depth), BF if last else F32)
    return pl.pallas_call(
        functools.partial(chunk_kernel, steps, slabs, halves, added, last),
        name="chunk_pass",
        out_shape=(*grad_shapes, total, total),
        grid_spec=pltpu.PrefetchScalarGridSpec(
            num_scalar_prefetch=1,
            grid=(steps + slabs,),
            in_specs=[whole, whole, whole, turned, turned] + [column] * (2 if added else 0),
            out_specs=(*grad_specs, column, column),
            scratch_shapes=[
                pltpu.VMEM((count, 2 * chunk), BF),
                pltpu.VMEM((count, chunk), BF),
            ],
        ),
        input_output_aliases={6: halves, 7: halves + 1} if added and not last else {},
        compiler_params=pltpu.CompilerParams(vmem_limit_bytes=56 << 20),
        cost_estimate=pl.CostEstimate(
            flops=6 * count * depth * width,
            bytes_accessed=8 * count * depth + 4 * depth * width + 16 * count * depth,
            transcendentals=count * chunk,
        ),
    )(order, rows, cot, full, rows_turned, cot_turned, *(sums if added else ()))


def pair_kernel(left_ref, first_ref, other_ref, second_ref, out_ref):
    width = first_ref.shape[1]
    out_ref[:, :width] = dot_tn(left_ref[...], first_ref[...]).astype(BF)
    out_ref[:, width:] = dot_tn(other_ref[...], second_ref[...]).astype(BF)


def pair_grads(left, first, other, second):
    count, depth = left.shape
    width = first.shape[1] + second.shape[1]
    height = 256
    whole = pl.BlockSpec(memory_space=pltpu.VMEM)
    column = pl.BlockSpec((count, height), lambda i: (0, i))
    return pl.pallas_call(
        pair_kernel,
        name="pair_grads",
        out_shape=jax.ShapeDtypeStruct((depth, width), BF),
        grid=(depth // height,),
        in_specs=[column, whole, column, whole],
        out_specs=pl.BlockSpec((height, width), lambda i: (i, 0)),
        compiler_params=pltpu.CompilerParams(vmem_limit_bytes=32 << 20),
        cost_estimate=pl.CostEstimate(
            flops=2 * count * depth * width,
            bytes_accessed=4 * count * depth + 2 * depth * width,
            transcendentals=0,
        ),
    )(left, first, other, second)


def on_z(pairs):
    return [(2 * a + core, 2 * b + core) for a, b in pairs for core in range(2)]


UP = [on_z([(z, z + 1) for z in range(count)]) for count in (1, 2, 3)]
DOWN = [on_z([(3 - z, 2 - z) for z in range(count)]) for count in (1, 2, 3)]
CORES = [(i, i ^ 1) for i in range(8)]
X_SWAP = [(i, i ^ 1) for i in range(4)]
Y_SWAP = [(i, i ^ 2) for i in range(4)]


def by_fsdp(value, pairs):
    return lax.ppermute(value, "fsdp", pairs)


def by_tp(value, pairs):
    return lax.ppermute(value, "tp", pairs)


def after(value, *earlier):
    return lax.optimization_barrier((value, *earlier))[0]


class Line:
    by_hops = True
    slabs = 8

    def __init__(self):
        place = lax.axis_index("fsdp")
        z, core = place // 2, place % 2
        self.rank = lax.axis_index("tp")
        self.order = jnp.stack(
            [((z + 4 - slot) % 4) * 2 + (core ^ other) for other in (1, 0) for slot in range(4)]
        ).astype(jnp.int32)

    def row_order(self, values):
        count = values.shape[0] // 4
        return jnp.concatenate(
            [lax.dynamic_slice_in_dim(values, (self.rank ^ p) * count, count, 0) for p in range(4)]
        )

    def trunk_base(self):
        return self.rank * TRUNK

    def sum_slabs(self, away, own):
        sums = own.astype(F32) + by_fsdp(away, CORES).astype(F32)
        low = sums.astype(BF)
        up = by_fsdp(low[1], UP[0])
        down = by_fsdp(low[3], DOWN[0])
        middle = (sums[2] + up.astype(F32) + down.astype(F32)).astype(BF)
        marks = [low, middle]
        up = by_fsdp(middle, UP[1])
        down = by_fsdp(middle, DOWN[1])
        up = (sums[3] + up.astype(F32)).astype(BF)
        down = (sums[1] + down.astype(F32)).astype(BF)
        marks.append(up)
        marks.append(down)
        up = by_fsdp(up, UP[2])
        down = by_fsdp(down, DOWN[2])
        return sums[0] + up.astype(F32) + down.astype(F32), marks

    def gather_rows(self, rows):
        half = rows.shape[0] // 2
        beside = by_tp(rows, X_SWAP)
        above = by_tp(rows, Y_SWAP)
        return jnp.concatenate(
            [rows, beside, above, by_tp(beside[:half], Y_SWAP), by_tp(above[half:], X_SWAP)]
        )

    def scatter_rows(self, partial):
        count = partial.shape[0] // 4
        half = count // 2
        own = partial[:count].astype(F32)
        beside = partial[count : 2 * count]
        above = partial[2 * count : 3 * count]
        far = partial[3 * count :].astype(BF)
        first = by_tp(far[:half], X_SWAP).astype(F32)
        second = by_tp(far[half:], Y_SWAP).astype(F32)
        above = jnp.concatenate([above[:half] + first, above[half:].astype(F32)]).astype(BF)
        beside = jnp.concatenate([beside[:half].astype(F32), beside[half:] + second]).astype(BF)
        return own + by_tp(beside, X_SWAP).astype(F32) + by_tp(above, Y_SWAP).astype(F32)


class Plain:
    by_hops = False
    slabs = 8

    def row_order(self, values):
        return values

    def trunk_base(self):
        return jnp.int32(0)

    def gather_rows(self, rows):
        return lax.all_gather(rows, "tp", axis=0, tiled=True)

    def scatter_rows(self, partial):
        return lax.psum_scatter(partial.astype(F32), "tp", scatter_dimension=0, tiled=True)


def gather_slabs(shard):
    return lax.all_gather(shard, "fsdp", axis=0, tiled=True)


def scatter_slabs(grads):
    return lax.psum_scatter(grads, "fsdp", scatter_dimension=0, tiled=True).astype(F32)


def rms_scale(row_values):
    return lax.rsqrt(jnp.mean(row_values * row_values, axis=-1, keepdims=True) + EPSILON)


def norm_back(row_values, row_scale, gain_values, grad_out):
    scaled_grad = grad_out * gain_values
    return row_scale * scaled_grad - row_values * row_scale**3 * jnp.mean(
        scaled_grad * row_values, axis=-1, keepdims=True
    )


def body(
    make_links,
    layer_input,
    cotangent,
    segment_ids,
    path_positions,
    ancestor_masks,
    attn_gain,
    query_weight,
    key_weight,
    value_weight,
    out_weight,
    mlp_gain,
    gate_weight,
    up_weight,
    down_weight,
):
    links = make_links()
    heads = query_weight.shape[1] // HD
    groups = key_weight.shape[1] // HD
    q_width, kv_width = heads * HD, groups * HD
    qkv_width = q_width + 2 * kv_width
    units = gate_weight.shape[1]
    edges = [units * sum(PARTS[:i]) // sum(PARTS) for i in range(len(PARTS) + 1)]

    gain_rows = gather_slabs(jnp.stack([attn_gain, mlp_gain], axis=1)).astype(F32)
    first_gain, second_gain = gain_rows[:, 0][None, :], gain_rows[:, 1][None, :]
    own_qkv = jnp.concatenate([query_weight, key_weight, value_weight], axis=1)
    attn_full = gather_slabs(jnp.concatenate([own_qkv, out_weight.T], axis=1))
    qkv_full, out_full = attn_full[:, :qkv_width], attn_full[:, qkv_width:]
    own_down = down_weight.T
    mlp_full = []
    for first, last in zip(edges[:-1], edges[1:]):
        cut = slice(first, last)
        mlp_full.append(
            gather_slabs(
                jnp.concatenate([gate_weight[:, cut], up_weight[:, cut], own_down[:, cut]], axis=1)
            )
        )

    positions = links.row_order(path_positions)
    angles = positions.astype(F32)[:, None] * jnp.asarray(inverse_freq(HD))[None, :]
    cosine, sine = jnp.cos(angles), jnp.sin(angles)
    cosine = jnp.concatenate([cosine] * 4, axis=1)
    sine = jnp.concatenate([-sine, sine] * 2, axis=1)
    segs = links.row_order(segment_ids)[::SEG]
    masks = ancestor_masks.reshape(SEGS * SEGS)
    base = jnp.reshape(links.trunk_base(), (1,)).astype(jnp.int32)

    inputs = layer_input.astype(F32)
    first_scale = rms_scale(inputs)
    first_normed = links.gather_rows((inputs * first_scale * first_gain).astype(BF))

    qkv_pre = dot_nn(first_normed, qkv_full)
    cot_all = links.gather_rows(after(cotangent, qkv_pre))
    attended, queries, keys, vals = attention_forward(
        heads, groups, masks, segs, base, qkv_pre, cosine, sine
    )
    residual = inputs + links.scatter_rows(dot_nt(attended, out_full))
    second_scale = rms_scale(residual)
    cot_turned = cot_all.T
    second_rows = (residual * second_scale * second_gain).astype(BF)
    second_normed = links.gather_rows(after(second_rows, cot_turned))

    second_turned = second_normed.T
    sums = None
    mlp_sums = []
    later = []
    for index, full in enumerate(mlp_full):
        halves = 2 if index < HOPS and links.by_hops else 1
        if later:
            full = after(full, later.pop(0))
        *grads, back_sum, out_sum = chunk_pass(
            links.order if halves == 2 else jnp.arange(links.slabs, dtype=jnp.int32),
            halves,
            second_normed,
            cot_all,
            full,
            second_turned,
            cot_turned,
            sums,
            index == len(mlp_full) - 1,
        )
        sums = (back_sum, out_sum)
        if halves == 2:
            part, later = links.sum_slabs(*grads)
        else:
            part = scatter_slabs(grads[0])
        mlp_sums.append(part)
    if later:
        back_sum = after(back_sum, *later)
    second_back = links.scatter_rows(back_sum)
    cot_float = cotangent.astype(F32)
    residual_back = cot_float + norm_back(residual, second_scale, second_gain, second_back)
    branch_back = links.gather_rows(residual_back.astype(BF))
    attended_back = dot_nn(branch_back, out_full).astype(BF)
    output = (residual + links.scatter_rows(out_sum)).astype(BF)
    qkv_back = attention_backward(
        heads, groups, masks, segs, base, queries, keys, vals, attended_back, cosine, sine
    )
    first_back = links.scatter_rows(dot_nt(qkv_back, qkv_full))
    attn_grads = pair_grads(first_normed, after(qkv_back, *mlp_sums), branch_back, attended)
    attn_sum = scatter_slabs(attn_grads)
    qkv_sum = attn_sum[:, :qkv_width]
    input_grad = residual_back + norm_back(inputs, first_scale, first_gain, first_back)

    thirds = [
        [part[:, at * part.shape[1] // 3 : (at + 1) * part.shape[1] // 3] for part in mlp_sums]
        for at in range(3)
    ]
    gate_sum, up_sum = jnp.concatenate(thirds[0], axis=1), jnp.concatenate(thirds[1], axis=1)
    down_sum = jnp.concatenate(thirds[2], axis=1).T
    attn_part = jnp.sum(own_qkv.astype(F32) * qkv_sum, axis=1)
    mlp_part = jnp.sum(
        gate_weight.astype(F32) * gate_sum + up_weight.astype(F32) * up_sum, axis=1
    )
    attn_total, mlp_total = lax.psum((attn_part, mlp_part), "tp")
    return (
        output,
        input_grad,
        attn_total / attn_gain.astype(F32),
        qkv_sum[:, :q_width],
        qkv_sum[:, q_width : q_width + kv_width],
        qkv_sum[:, q_width + kv_width :],
        attn_sum[:, qkv_width:].T,
        mlp_total / mlp_gain.astype(F32),
        gate_sum,
        up_sum,
        down_sum,
    )


def solution(mesh):
    fits = mesh.shape["fsdp"] == 8 and mesh.shape["tp"] == 4
    return jax.shard_map(
        functools.partial(body, Line if fits else Plain),
        mesh=mesh,
        in_specs=(
            P(("fsdp", "tp"), None),
            P(("fsdp", "tp"), None),
            P("fsdp"),
            P("fsdp"),
            P("fsdp", None, None),
            P("fsdp"),
            P("fsdp", "tp"),
            P("fsdp", "tp"),
            P("fsdp", "tp"),
            P("tp", "fsdp"),
            P("fsdp"),
            P("fsdp", "tp"),
            P("fsdp", "tp"),
            P("tp", "fsdp"),
        ),
        out_specs=(
            P(("fsdp", "tp"), None),
            P(("fsdp", "tp"), None),
            P("fsdp"),
            P("fsdp", "tp"),
            P("fsdp", "tp"),
            P("fsdp", "tp"),
            P("tp", "fsdp"),
            P("fsdp"),
            P("fsdp", "tp"),
            P("fsdp", "tp"),
            P("tp", "fsdp"),
        ),
        check_vma=False,
    )
```

```python
import functools
import math

import jax
import jax.numpy as jnp
import numpy as np
from jax import lax
from jax.experimental import pallas as pl
from jax.experimental.pallas import tpu as pltpu
from jax.sharding import PartitionSpec as P

HD = 64
SEGS = 13
SEG = 64
TRUNK = 256
BRANCHES = 4
EPSILON = 1e-05
PARTS = (3, 3, 2)
EARLY = 1
NEG = -1e30
BF = jnp.bfloat16
F32 = jnp.float32


def inverse_freq(head_size):
    base_freq = 1.0 / 500000.0 ** (np.arange(0, head_size, 2) / head_size)
    wavelen = 2.0 * math.pi / base_freq
    smooth = (8192.0 / wavelen - 1.0) / 3.0
    blended = (1.0 - smooth) * base_freq / 32.0 + smooth * base_freq
    scaled = np.where(
        wavelen > 8192.0, base_freq / 32.0, np.where(wavelen < 2048.0, base_freq, blended)
    )
    return scaled.astype(np.float32)


def dot_nn(left, right):
    return lax.dot_general(
        left, right, (((1,), (0,)), ((), ())), preferred_element_type=F32
    )


def dot_nt(left, right):
    return lax.dot_general(
        left, right, (((1,), (1,)), ((), ())), preferred_element_type=F32
    )


def dot_tn(left, right):
    return lax.dot_general(
        left, right, (((0,), (0,)), ((), ())), preferred_element_type=F32
    )


def rope_lanes(values, cosine, signed_sine, low_half):
    rolled = jnp.where(low_half, pltpu.roll(values, 96, 1), pltpu.roll(values, 32, 1))
    return values * cosine + rolled * signed_sine


def rope_lanes_back(grads, cosine, signed_sine, low_half):
    scaled = grads * signed_sine
    rolled = jnp.where(low_half, pltpu.roll(scaled, 96, 1), pltpu.roll(scaled, 32, 1))
    return grads * cosine + rolled


def low_half_mask(rows):
    lane = lax.broadcasted_iota(jnp.int32, (rows, 128), 1)
    return lax.rem(lane, HD) < HD // 2


def parent_block(mask_ref, seg_ref, segment, block_count):
    parent = jnp.int32(0)
    for branch in range(1, BRANCHES + 1):
        parent = parent + branch * mask_ref[segment * SEGS + branch]
    parent = jnp.where(segment > BRANCHES, parent, segment)
    found = jnp.int32(0)
    for block in range(block_count):
        found = found + block * (seg_ref[block] == parent).astype(jnp.int32)
    return found


def block_mask(has_parent, members):
    shape = (members * SEG, 2 * SEG)
    row = lax.rem(lax.broadcasted_iota(jnp.int32, shape, 0), SEG)
    col = lax.broadcasted_iota(jnp.int32, shape, 1)
    return ((col < SEG) & has_parent) | ((col >= SEG) & (col - SEG <= row))


def trunk_mask(index, members):
    shape = (members * SEG, TRUNK)
    row = lax.rem(lax.broadcasted_iota(jnp.int32, shape, 0), SEG) + index * SEG
    col = lax.broadcasted_iota(jnp.int32, shape, 1)
    return col <= row


def softmax_rows(scores):
    row_max = jnp.max(scores, axis=-1, keepdims=True)
    exponent = jnp.exp(scores - row_max)
    return exponent / jnp.sum(exponent, axis=-1, keepdims=True)


def attn_fwd_kernel(
    heads, groups, mask_ref, seg_ref, base_ref, pre_ref, cos_ref, sin_ref,
    att_ref, q_ref, k_ref, v_ref,
):
    rows = pre_ref.shape[0]
    blocks = rows // SEG
    members = heads // groups
    score_scale = HD ** (-0.5)
    low_half = low_half_mask(rows)
    cosine = cos_ref[...]
    sine = sin_ref[...]
    q_width = heads * HD
    kv_width = groups * HD

    def put_heads(dest, first, wide, count):
        for half in range(count):
            head = first + half
            part = wide[:, half * HD : (half + 1) * HD].reshape(blocks, SEG, HD)
            group, member = head // members, head % members
            dest[group, :, member * SEG : (member + 1) * SEG, :] = part

    for pair in range(q_width // 128):
        lanes = pre_ref[:, pair * 128 : (pair + 1) * 128]
        put_heads(q_ref, 2 * pair, rope_lanes(lanes, cosine, sine, low_half).astype(BF), 2)
    if kv_width % 128 == 0:
        for pair in range(kv_width // 128):
            at = q_width + pair * 128
            wide = rope_lanes(pre_ref[:, at : at + 128], cosine, sine, low_half).astype(BF)
            at = q_width + kv_width + pair * 128
            plain = pre_ref[:, at : at + 128].astype(BF)
            for half in range(2):
                k_ref[2 * pair + half] = wide[:, half * HD : (half + 1) * HD]
                v_ref[2 * pair + half] = plain[:, half * HD : (half + 1) * HD]
    else:
        both = pre_ref[:, q_width : q_width + 128]
        k_ref[0] = rope_lanes(both, cosine, sine, low_half).astype(BF)[:, :HD]
        v_ref[0] = both.astype(BF)[:, HD:]

    base = base_ref[0]
    trunk_block = base // SEG
    trunk_rows = pl.ds(pl.multiple_of(base, TRUNK), TRUNK)

    def store(group, block, mixed):
        at = pl.ds(pl.multiple_of(block * SEG, SEG), SEG)
        for member in range(members):
            head = group * members + member
            att_ref[at, head * HD : (head + 1) * HD] = mixed[
                member * SEG : (member + 1) * SEG
            ].astype(BF)

    for group in range(groups):
        def one_block(block, carry):
            inside = block - trunk_block
            is_trunk = (inside >= 0) & (inside < TRUNK // SEG)

            @pl.when(is_trunk)
            def _():
                queries = q_ref[group, block]
                scores = dot_nt(queries, k_ref[group, trunk_rows, :]) * score_scale
                scores = jnp.where(trunk_mask(inside, members), scores, NEG)
                probs = softmax_rows(scores).astype(BF)
                store(group, block, dot_nn(probs, v_ref[group, trunk_rows, :]))

            @pl.when(jnp.logical_not(is_trunk))
            def _():
                segment = seg_ref[block]
                parent = parent_block(mask_ref, seg_ref, segment, blocks)
                up = pl.ds(pl.multiple_of(parent * SEG, SEG), SEG)
                own = pl.ds(pl.multiple_of(block * SEG, SEG), SEG)
                queries = q_ref[group, block]
                keys = jnp.concatenate(
                    [k_ref[group, trunk_rows, :], k_ref[group, up, :], k_ref[group, own, :]], axis=0
                )
                vals = jnp.concatenate(
                    [v_ref[group, trunk_rows, :], v_ref[group, up, :], v_ref[group, own, :]], axis=0
                )
                scores = dot_nt(queries, keys) * score_scale
                tail = jnp.where(
                    block_mask(segment > BRANCHES, members), scores[:, TRUNK:], NEG
                )
                scores = jnp.concatenate([scores[:, :TRUNK], tail], axis=1)
                probs = softmax_rows(scores).astype(BF)
                store(group, block, dot_nn(probs, vals))

            return carry

        lax.fori_loop(0, blocks, one_block, 0)


def attn_bwd_kernel(
    heads, groups, mask_ref, seg_ref, base_ref, q_ref, k_ref, v_ref, grad_ref, cos_ref, sin_ref,
    out_ref, g_ref, dq_ref, dk_ref, dv_ref,
):
    rows = grad_ref.shape[0]
    blocks = rows // SEG
    members = heads // groups
    score_scale = HD ** (-0.5)
    low_half = low_half_mask(rows)
    cosine = cos_ref[...]
    sine = sin_ref[...]
    q_width = heads * HD
    kv_width = groups * HD
    for head in range(heads):
        part = grad_ref[:, head * HD : (head + 1) * HD].reshape(blocks, SEG, HD)
        group, member = head // members, head % members
        g_ref[group, :, member * SEG : (member + 1) * SEG, :] = part
    dk_ref[...] = jnp.zeros_like(dk_ref)
    dv_ref[...] = jnp.zeros_like(dv_ref)
    base = base_ref[0]
    trunk_block = base // SEG
    trunk_rows = pl.ds(pl.multiple_of(base, TRUNK), TRUNK)

    def store(group, block, d_query):
        at = pl.ds(pl.multiple_of(block * SEG, SEG), SEG)
        for member in range(members):
            head = group * members + member
            dq_ref[at, head * HD : (head + 1) * HD] = d_query[member * SEG : (member + 1) * SEG]

    for group in range(groups):
        lanes = slice(group * HD, (group + 1) * HD)

        def grads(queries, out_grads, keys, vals, scores):
            probs = softmax_rows(scores)
            prob_back = dot_nt(out_grads, vals)
            delta = jnp.sum(probs * prob_back, axis=-1, keepdims=True)
            score_back = (probs * (prob_back - delta)).astype(BF)
            d_query = dot_nn(score_back, keys) * score_scale
            d_key = dot_tn(score_back, queries) * score_scale
            d_val = dot_tn(probs.astype(BF), out_grads)
            return d_query, d_key, d_val

        def one_block(block, carry):
            inside = block - trunk_block
            is_trunk = (inside >= 0) & (inside < TRUNK // SEG)

            @pl.when(is_trunk)
            def _():
                queries = q_ref[group, block]
                keys = k_ref[group, trunk_rows, :]
                scores = dot_nt(queries, keys) * score_scale
                scores = jnp.where(trunk_mask(inside, members), scores, NEG)
                d_query, d_key, d_val = grads(
                    queries, g_ref[group, block], keys, v_ref[group, trunk_rows, :], scores
                )
                store(group, block, d_query)
                dk_ref[trunk_rows, lanes] += d_key
                dv_ref[trunk_rows, lanes] += d_val

            @pl.when(jnp.logical_not(is_trunk))
            def _():
                segment = seg_ref[block]
                parent = parent_block(mask_ref, seg_ref, segment, blocks)
                up = pl.ds(pl.multiple_of(parent * SEG, SEG), SEG)
                own = pl.ds(pl.multiple_of(block * SEG, SEG), SEG)
                queries = q_ref[group, block]
                keys = jnp.concatenate(
                    [k_ref[group, trunk_rows, :], k_ref[group, up, :], k_ref[group, own, :]], axis=0
                )
                vals = jnp.concatenate(
                    [v_ref[group, trunk_rows, :], v_ref[group, up, :], v_ref[group, own, :]], axis=0
                )
                scores = dot_nt(queries, keys) * score_scale
                tail = jnp.where(
                    block_mask(segment > BRANCHES, members), scores[:, TRUNK:], NEG
                )
                scores = jnp.concatenate([scores[:, :TRUNK], tail], axis=1)
                d_query, d_key, d_val = grads(queries, g_ref[group, block], keys, vals, scores)
                store(group, block, d_query)
                for ref, val in ((dk_ref, d_key), (dv_ref, d_val)):
                    ref[trunk_rows, lanes] += val[:TRUNK]
                    ref[up, lanes] += val[TRUNK : TRUNK + SEG]
                    ref[own, lanes] += val[TRUNK + SEG :]

            return carry

        lax.fori_loop(0, blocks, one_block, 0)
    for pair in range(q_width // 128):
        at = slice(pair * 128, (pair + 1) * 128)
        out_ref[:, at] = rope_lanes_back(dq_ref[:, at], cosine, sine, low_half).astype(BF)
    if kv_width % 128 == 0:
        for pair in range(kv_width // 128):
            at = slice(pair * 128, (pair + 1) * 128)
            turned = rope_lanes_back(dk_ref[:, at], cosine, sine, low_half)
            out_ref[:, q_width + pair * 128 : q_width + (pair + 1) * 128] = turned.astype(BF)
            first = q_width + kv_width + pair * 128
            out_ref[:, first : first + 128] = dv_ref[:, at].astype(BF)
    else:
        wide = jnp.concatenate([dk_ref[...], dv_ref[...]], axis=1)
        turned = rope_lanes_back(wide, cosine, sine, low_half)
        lane = lax.broadcasted_iota(jnp.int32, (rows, 128), 1)
        out_ref[:, q_width : q_width + 128] = jnp.where(lane < HD, turned, wide).astype(BF)


LIGHT = pl.CostEstimate(flops=1000, bytes_accessed=1000, transcendentals=0)
SMEM = pl.BlockSpec(memory_space=pltpu.SMEM)
VMEM = pl.BlockSpec(memory_space=pltpu.VMEM)


def attention_forward(heads, groups, masks, segs, base, pre, cosine, sine):
    rows = pre.shape[0]
    members = heads // groups
    blocks = rows // SEG
    return pl.pallas_call(
        functools.partial(attn_fwd_kernel, heads, groups),
        name="attn_fwd",
        out_shape=(
            jax.ShapeDtypeStruct((rows, heads * HD), BF),
            jax.ShapeDtypeStruct((groups, blocks, members * SEG, HD), BF),
            jax.ShapeDtypeStruct((groups, rows, HD), BF),
            jax.ShapeDtypeStruct((groups, rows, HD), BF),
        ),
        in_specs=[SMEM, SMEM, SMEM, VMEM, VMEM, VMEM],
        out_specs=(VMEM, VMEM, VMEM, VMEM),
        compiler_params=pltpu.CompilerParams(vmem_limit_bytes=40 << 20),
        cost_estimate=LIGHT,
    )(masks, segs, base, pre, cosine, sine)


def attention_backward(heads, groups, masks, segs, base, queries, keys, vals, grads, cosine, sine):
    rows = grads.shape[0]
    members = heads // groups
    blocks = rows // SEG
    return pl.pallas_call(
        functools.partial(attn_bwd_kernel, heads, groups),
        name="attn_bwd",
        out_shape=jax.ShapeDtypeStruct((rows, (heads + 2 * groups) * HD), BF),
        in_specs=[SMEM, SMEM, SMEM, VMEM, VMEM, VMEM, VMEM, VMEM, VMEM],
        out_specs=VMEM,
        scratch_shapes=[
            pltpu.VMEM((groups, blocks, members * SEG, HD), BF),
            pltpu.VMEM((rows, heads * HD), F32),
            pltpu.VMEM((rows, groups * HD), F32),
            pltpu.VMEM((rows, groups * HD), F32),
        ],
        compiler_params=pltpu.CompilerParams(vmem_limit_bytes=40 << 20),
        cost_estimate=LIGHT,
    )(masks, segs, base, queries, keys, vals, grads, cosine, sine)


MESH = pl.DeviceIdType.MESH


def swap_peers():
    rank = lax.axis_index("tp")
    place = lax.axis_index("fsdp")
    return [(place, rank + 1 - 2 * (rank % 2)), (place, (rank + 2) % 4)]


def greet(peers):
    barrier = pltpu.get_barrier_semaphore()
    for peer in peers:
        pl.semaphore_signal(barrier, inc=1, device_id=peer, device_id_type=MESH)
    pl.semaphore_wait(barrier, len(peers))


def send(source, target, send_sem, recv_sem, peer):
    copy = pltpu.make_async_remote_copy(
        src_ref=source,
        dst_ref=target,
        send_sem=send_sem,
        recv_sem=recv_sem,
        device_id=peer,
        device_id_type=MESH,
    )
    copy.start()
    return copy


def line_peers():
    place = lax.axis_index("fsdp")
    rank = lax.axis_index("tp")
    z, core = place // 2, place % 2
    up, down = (z + 1) % 4, (z + 3) % 4
    return z, core, [(2 * z + 1 - core, rank), (2 * up + core, rank), (2 * down + core, rank)]


def far_copies(far_ref, far_recv, send_sem, recv_sem, z, peers):
    heading = z // 2
    place = lax.axis_index("fsdp")
    target = (place + 2 - 4 * heading, lax.axis_index("tp"))
    return pltpu.make_async_remote_copy(
        src_ref=far_ref,
        dst_ref=far_recv.at[heading],
        send_sem=send_sem,
        recv_sem=recv_sem.at[heading],
        device_id=target,
        device_id_type=MESH,
    )


def far_add(pair_ref, far_recv, recv_sem, z, peers):
    @pl.when((z == 1) | (z == 2))
    def _():
        for heading in range(2):
            pltpu.make_async_remote_copy(
                src_ref=far_recv.at[heading],
                dst_ref=far_recv.at[heading],
                send_sem=recv_sem.at[heading],
                recv_sem=recv_sem.at[heading],
                device_id=peers[0],
                device_id_type=MESH,
            ).wait_recv()
        pair_ref[0] = (pair_ref[0].astype(F32) + far_recv[1].astype(F32)).astype(BF)
        pair_ref[1] = (pair_ref[1].astype(F32) + far_recv[0].astype(F32)).astype(BF)


def near_copies(pair_ref, near_recv, send_sem, recv_sem, peers):
    return [
        pltpu.make_async_remote_copy(
            src_ref=pair_ref.at[at],
            dst_ref=near_recv.at[at],
            send_sem=send_sem.at[at],
            recv_sem=recv_sem.at[at],
            device_id=peers[2 - at],
            device_id_type=MESH,
        )
        for at in range(2)
    ]


class Hops:
    def __init__(self, slabs_ref, total_ref, pair_ref, slab_ref, far_recv, near_recv, sends, recvs, loads):
        self.z, _, self.line = line_peers()
        self.total_ref, self.pair_ref, self.slab_ref = total_ref, pair_ref, slab_ref
        self.far_recv, self.near_recv, self.recvs = far_recv, near_recv, recvs
        self.far = far_copies(
            slabs_ref.at[0], far_recv, sends.at[0, 0], recvs.at[0], self.z, self.line
        )
        self.loads = [
            pltpu.make_async_copy(slabs_ref.at[1 + at], pair_ref.at[at], loads.at[at])
            for at in range(2)
        ] + [pltpu.make_async_copy(slabs_ref.at[3], slab_ref, loads.at[2])]
        self.near = near_copies(pair_ref, near_recv, sends.at[1], recvs.at[1], self.line)

    def begin(self):
        self.far.start()
        for load in self.loads:
            load.start()

    def onward(self):
        for load in self.loads:
            load.wait()
        self.far.wait_send()
        far_add(self.pair_ref, self.far_recv, self.recvs.at[0], self.z, self.line)
        for copy in self.near:
            copy.start()

    def finish(self):
        for copy in self.near:
            copy.wait()
        self.total_ref[...] = (
            self.slab_ref[...].astype(F32)
            + self.near_recv[0].astype(F32)
            + self.near_recv[1].astype(F32)
        )


def hop_scratch(height, width):
    return [
        pltpu.VMEM((2, height, width), BF),
        pltpu.VMEM((height, width), BF),
        pltpu.VMEM((2, height, width), BF),
        pltpu.VMEM((2, height, width), BF),
        pltpu.SemaphoreType.DMA((2, 2)),
        pltpu.SemaphoreType.DMA((2, 2)),
        pltpu.SemaphoreType.DMA((3,)),
    ]


SLOTS = (2, 1, 3, 0)


def chunk_kernel(cfg, *refs):
    steps, slabs, first, last, cores, job, owners = cfg
    refs = list(refs)
    take = lambda count: [refs.pop(0) for _ in range(count)]
    rows_ref, cot_ref, full_ref = take(3)
    if not first:
        back_in_ref, out_in_ref = take(2)
    if job == "far":
        (slabs_ref,) = take(1)
    if job == "near":
        slabs_ref, moved_ref = take(2)
    if owners:
        (residual_ref,) = take(1)
    grad_ref, back_ref, out_ref = take(3)
    if job == "far":
        (moved_ref,) = take(1)
    if job == "near":
        (total_ref,) = take(1)
    pair_ref, hidden_ref = take(2)
    if cores:
        mine_ref, theirs_ref, core_send, core_recv = take(4)
    if job:
        job_recv, job_send_sem, job_recv_sem, load_sem = take(4)
    if job == "near":
        (slab_ref,) = take(1)
    if owners:
        part_ref, owned_ref, owner_send, owner_recv = take(4)

    step = pl.program_id(0)
    end = steps + slabs - 1
    chunk = hidden_ref.shape[1]
    tile = chunk // steps
    height = rows_ref.shape[1] // slabs
    if cores or job:
        z, core, peers = line_peers()
        far = None
        if job == "far":
            loads = [
                pltpu.make_async_copy(slabs_ref.at[1 + at], moved_ref.at[at], load_sem.at[at])
                for at in range(2)
            ]
            far = far_copies(slabs_ref.at[0], job_recv, job_send_sem.at[0], job_recv_sem, z, peers)
        if job == "near":
            loads = [pltpu.make_async_copy(slabs_ref.at[3], slab_ref, load_sem.at[0])]
            near = near_copies(moved_ref, job_recv, job_send_sem, job_recv_sem, peers)

        if owners:
            fsdp, rank = lax.axis_index("fsdp"), lax.axis_index("tp")
            beside = rank + 1 - 2 * (rank % 2)
            row_peers = [(fsdp, beside), (fsdp, (rank + 2) % 4), (fsdp, 3 - rank)]

            def to_owner(piece, columns):
                return pltpu.make_async_remote_copy(
                    src_ref=part_ref.at[piece, :, columns],
                    dst_ref=owned_ref.at[piece - 1, :, columns],
                    send_sem=owner_send.at[piece - 1],
                    recv_sem=owner_recv.at[piece - 1],
                    device_id=row_peers[piece - 1],
                    device_id_type=MESH,
                )

        @pl.when(step == 0)
        def _():
            greet(peers + (row_peers if owners else []))
            if job == "far":
                far.start()
            if job == "near":
                for copy in near:
                    copy.start()
            if job:
                for load in loads:
                    load.start()

    for at in range(steps):

        @pl.when(step == at)
        def _():
            cut = slice(at * tile, (at + 1) * tile)
            gate = dot_nn(rows_ref[...], full_ref[:, cut])
            up = dot_nn(rows_ref[...], full_ref[:, chunk + at * tile : chunk + (at + 1) * tile])
            back = dot_nn(
                cot_ref[...], full_ref[:, 2 * chunk + at * tile : 2 * chunk + (at + 1) * tile]
            )
            sigmoid = 1.0 / (1.0 + jnp.exp(-gate))
            silu = gate * sigmoid
            hidden_ref[:, cut] = (silu * up).astype(BF)
            pair_ref[:, cut] = (back * up * sigmoid * (1.0 + gate * (1.0 - sigmoid))).astype(BF)
            pair_ref[:, chunk + at * tile : chunk + (at + 1) * tile] = (back * silu).astype(BF)

    def write(slab, target_ref, added_ref):
        at = pl.ds(pl.multiple_of(slab * height, height), height)
        grad = dot_tn(rows_ref[:, at], pair_ref[...])
        more = dot_tn(cot_ref[:, at], hidden_ref[...])
        if added_ref is not None:
            grad = grad.astype(BF).astype(F32) + added_ref[:, : 2 * chunk].astype(F32)
            more = more.astype(BF).astype(F32) + added_ref[:, 2 * chunk :].astype(F32)
        target_ref[:, : 2 * chunk] = grad.astype(BF)
        target_ref[:, 2 * chunk :] = more.astype(BF)

    @pl.when(step >= steps)
    def _():
        slab = pl.ds(pl.multiple_of((step - steps) * height, height), height)
        back = dot_nt(pair_ref[...], full_ref[slab, : 2 * chunk])
        out = dot_nt(hidden_ref[...], full_ref[slab, 2 * chunk :])
        back = back if first else back_in_ref[...] + back
        out = out if first else out_in_ref[...] + out
        back_ref[...] = back.astype(back_ref.dtype)
        if owners:
            columns = pl.ds(pl.multiple_of((step - steps) * height, height), height)
            part_ref[:, :, columns] = out.astype(BF).reshape(4, -1, height)
            for piece in (3, 1, 2):
                to_owner(piece, columns).start()
        else:
            out_ref[...] = out.astype(out_ref.dtype)
        if not cores:
            write(step - steps, grad_ref, None)

    if cores:
        copies = [
            pltpu.make_async_remote_copy(
                src_ref=mine_ref.at[at % 2],
                dst_ref=theirs_ref.at[at],
                send_sem=core_send.at[at],
                recv_sem=core_recv.at[at],
                device_id=peers[0],
                device_id_type=MESH,
            )
            for at in range(4)
        ]
        for at, slot in enumerate(SLOTS):
            chip = (z + 4 - slot) % 4

            @pl.when(step == steps + at)
            def _():
                if at >= 2:
                    copies[at - 2].wait_send()
                write(2 * chip + 1 - core, mine_ref.at[at % 2], None)
                copies[at].start()

            @pl.when(step == steps + 4 + at)
            def _():
                copies[at].wait_recv()
                write(2 * chip + core, grad_ref.at[0], theirs_ref.at[at])

        @pl.when(step == end)
        def _():
            copies[2].wait_send()
            copies[3].wait_send()

    if job == "far":

        @pl.when(step == end)
        def _():
            for load in loads:
                load.wait()
            far.wait_send()
            far_add(moved_ref, job_recv, job_recv_sem, z, peers)

    if job == "near":

        @pl.when(step == end)
        def _():
            loads[0].wait()
            for copy in near:
                copy.wait()
            total_ref[...] = (
                slab_ref[...].astype(F32) + job_recv[0].astype(F32) + job_recv[1].astype(F32)
            )


    if owners:

        @pl.when(step == end)
        def _():
            for piece in (1, 2, 3):
                to_owner(piece, slice(None)).wait()
            total = residual_ref[...] + part_ref[0].astype(F32)
            for piece in range(3):
                total = total + owned_ref[piece].astype(F32)
            out_ref[...] = total.astype(BF)


def chunk_pass(rows, cot, full, at, width, sums, last, cores=False, job=None, operands=(), number=None, residual=None):
    count, depth = rows.shape
    chunk = width // 3
    slabs = 8
    height = depth // slabs
    steps = max(1, chunk // 256)
    first = sums is None
    whole = pl.BlockSpec(memory_space=pltpu.VMEM)
    anywhere = pl.BlockSpec(memory_space=pl.ANY)
    weights = pl.BlockSpec((depth, width), lambda i: (0, at), pipeline_mode=pl.Buffered(1))

    def place(i):
        return jnp.maximum(i - steps, 0)

    column = pl.BlockSpec((count, height), lambda i: (0, place(i)))
    total = jax.ShapeDtypeStruct((count, depth), BF if last else F32)
    if cores:
        grad_shape = jax.ShapeDtypeStruct((4, height, width), BF)
        grad_spec = pl.BlockSpec((1, height, width), lambda i: (jnp.maximum(place(i) - 4, 0), 0, 0))
    else:
        grad_shape = jax.ShapeDtypeStruct((depth, width), BF)
        grad_spec = pl.BlockSpec((height, width), lambda i: (place(i), 0))
    out_shapes, out_specs = [grad_shape, total, total], [grad_spec, column, column]
    in_specs = [whole, whole, weights] + ([] if first else [column, column])
    scratch = [pltpu.VMEM((count, 2 * chunk), BF), pltpu.VMEM((count, chunk), BF)]
    dma = pltpu.SemaphoreType.DMA
    if cores:
        scratch += [
            pltpu.VMEM((2, height, width), BF),
            pltpu.VMEM((4, height, width), BF),
            dma((4,)),
            dma((4,)),
        ]
    if job:
        job_width = operands[0].shape[-1]
        scratch += [pltpu.VMEM((2, height, job_width), BF), dma((2,)), dma((2,)), dma((2,))]
    if job == "far":
        in_specs += [anywhere]
        out_shapes += [jax.ShapeDtypeStruct((2, height, job_width), BF)]
        out_specs += [whole]
    if job == "near":
        in_specs += [anywhere, anywhere]
        out_shapes += [jax.ShapeDtypeStruct((height, job_width), F32)]
        out_specs += [whole]
        scratch += [pltpu.VMEM((height, job_width), BF)]
    if residual is not None:
        own = residual.shape[0]
        in_specs += [whole]
        operands = (*operands, residual)
        out_shapes[2] = jax.ShapeDtypeStruct((own, depth), BF)
        out_specs[2] = whole
        scratch += [
            pltpu.VMEM((4, own, depth), BF),
            pltpu.VMEM((3, own, depth), BF),
            dma((3,)),
            dma((3,)),
        ]
    remote = cores or job
    return pl.pallas_call(
        functools.partial(chunk_kernel, (steps, slabs, first, last, cores, job, residual is not None)),
        name="chunk_pass",
        out_shape=tuple(out_shapes),
        grid=(steps + slabs,),
        in_specs=in_specs,
        out_specs=tuple(out_specs),
        scratch_shapes=scratch,
        input_output_aliases={} if first or last else {3: 1, 4: 2},
        compiler_params=pltpu.CompilerParams(
            vmem_limit_bytes=60 << 20,
            collective_id=number if remote else None,
            has_side_effects=bool(remote),
        ),
        cost_estimate=pl.CostEstimate(
            flops=6 * count * depth * width,
            bytes_accessed=8 * count * depth + 4 * depth * width + 16 * count * depth,
            transcendentals=count * chunk,
        ),
    )(rows, cot, full, *(() if first else sums), *operands)


def pair_kernel(left_ref, first_ref, other_ref, second_ref, out_ref):
    width = first_ref.shape[1]
    out_ref[:, :width] = dot_tn(left_ref[...], first_ref[...]).astype(BF)
    out_ref[:, width:] = dot_tn(other_ref[...], second_ref[...]).astype(BF)


def pair_grads(left, first, other, second):
    count, depth = left.shape
    width = first.shape[1] + second.shape[1]
    height = 256
    whole = pl.BlockSpec(memory_space=pltpu.VMEM)
    column = pl.BlockSpec((count, height), lambda i: (0, i))
    return pl.pallas_call(
        pair_kernel,
        name="pair_grads",
        out_shape=jax.ShapeDtypeStruct((depth, width), BF),
        grid=(depth // height,),
        in_specs=[column, whole, column, whole],
        out_specs=pl.BlockSpec((height, width), lambda i: (i, 0)),
        compiler_params=pltpu.CompilerParams(vmem_limit_bytes=32 << 20),
        cost_estimate=LIGHT,
    )(left, first, other, second)


def pair_hops_kernel(
    left_ref, first_ref, other_ref, second_ref, out_ref, mine_ref, theirs_ref, core_send, core_recv
):
    step = pl.program_id(0)
    z, core, peers = line_peers()
    width = first_ref.shape[1]
    height = out_ref.shape[1]

    def write(slab, target_ref, added_ref):
        at = pl.ds(pl.multiple_of(slab * height, height), height)
        grad = dot_tn(left_ref[:, at], first_ref[...])
        more = dot_tn(other_ref[:, at], second_ref[...])
        if added_ref is not None:
            grad = grad.astype(BF).astype(F32) + added_ref[:, :width].astype(F32)
            more = more.astype(BF).astype(F32) + added_ref[:, width:].astype(F32)
        target_ref[:, :width] = grad.astype(BF)
        target_ref[:, width:] = more.astype(BF)

    @pl.when(step == 0)
    def _():
        greet(peers[:1])

    copies = [
        pltpu.make_async_remote_copy(
            src_ref=mine_ref.at[at],
            dst_ref=theirs_ref.at[at],
            send_sem=core_send.at[at],
            recv_sem=core_recv.at[at],
            device_id=peers[0],
            device_id_type=MESH,
        )
        for at in range(4)
    ]
    for at, slot in enumerate(SLOTS):
        chip = (z + 4 - slot) % 4

        @pl.when(step == at)
        def _():
            write(2 * chip + 1 - core, mine_ref.at[at], None)
            copies[at].start()

        @pl.when(step == 4 + at)
        def _():
            copies[at].wait_recv()
            write(2 * chip + core, out_ref.at[0], theirs_ref.at[at])

    @pl.when(step == 7)
    def _():
        for copy in copies:
            copy.wait_send()


def pair_hops(left, first, other, second):
    count, depth = left.shape
    width = first.shape[1] + second.shape[1]
    height = depth // 8
    return pl.pallas_call(
        pair_hops_kernel,
        name="pair_hops",
        out_shape=jax.ShapeDtypeStruct((4, height, width), BF),
        grid=(8,),
        in_specs=[VMEM] * 4,
        out_specs=pl.BlockSpec((1, height, width), lambda i: (jnp.maximum(i - 4, 0), 0, 0)),
        scratch_shapes=[
            pltpu.VMEM((4, height, width), BF),
            pltpu.VMEM((4, height, width), BF),
            pltpu.SemaphoreType.DMA((4,)),
            pltpu.SemaphoreType.DMA((4,)),
        ],
        compiler_params=pltpu.CompilerParams(
            collective_id=7, has_side_effects=True, vmem_limit_bytes=48 << 20
        ),
        cost_estimate=pl.CostEstimate(
            flops=2 * count * depth * width,
            bytes_accessed=4 * count * depth + 2 * depth * width,
            transcendentals=0,
        ),
    )(left, first, other, second)


X_SWAP = [(i, i ^ 1) for i in range(4)]
Y_SWAP = [(i, i ^ 2) for i in range(4)]


def by_tp(value, pairs):
    return lax.ppermute(value, "tp", pairs)


def after(value, *earlier):
    return lax.optimization_barrier((value, *earlier))[0]


def sum_pieces(part_ref, make, half_ref, whole_ref, send_sem, recv_sem, peers, meanwhile):
    half = part_ref.shape[1] // 2
    make(3)
    copies = [
        send(
            part_ref.at[3, pl.ds(axis * half, half)],
            half_ref.at[axis],
            send_sem.at[axis],
            recv_sem.at[axis],
            peers[axis],
        )
        for axis in range(2)
    ]
    for piece in (1, 2, 0):
        make(piece)
    meanwhile(0)
    for copy in copies:
        copy.wait()
    part_ref[2, :half] = (part_ref[2, :half].astype(F32) + half_ref[0].astype(F32)).astype(BF)
    part_ref[1, half:] = (part_ref[1, half:].astype(F32) + half_ref[1].astype(F32)).astype(BF)
    copies = [
        send(
            part_ref.at[1 + axis],
            whole_ref.at[axis],
            send_sem.at[2 + axis],
            recv_sem.at[2 + axis],
            peers[axis],
        )
        for axis in range(2)
    ]
    meanwhile(1)
    for copy in copies:
        copy.wait()
    return part_ref[0].astype(F32) + whole_ref[0].astype(F32) + whole_ref[1].astype(F32)


def gather_pieces(all_ref, send_sem, recv_sem, peers, meanwhile):
    half = all_ref.shape[1] // 2
    copies = [
        send(all_ref.at[0], all_ref.at[1 + axis], send_sem.at[axis], recv_sem.at[axis], peers[axis])
        for axis in range(2)
    ]
    meanwhile(2)
    for copy in copies:
        copy.wait()
    copies = []
    for axis in range(2):
        rows = pl.ds(axis * half, half)
        copies.append(
            send(
                all_ref.at[1 + axis, rows],
                all_ref.at[3, rows],
                send_sem.at[2 + axis],
                recv_sem.at[2 + axis],
                peers[1 - axis],
            )
        )
    meanwhile(3)
    for copy in copies:
        copy.wait()


def idle(stage):
    return None


def row_scale(values):
    return lax.rsqrt(jnp.mean(values * values, axis=-1, keepdims=True) + EPSILON)


def mid_forward_kernel(
    attended_ref, weight_ref, input_ref, gain_ref,
    residual_ref, all_ref,
    part_ref, half_ref, whole_ref, sems,
):
    peers = swap_peers()
    rows = input_ref.shape[0]
    greet(peers)

    def make(piece):
        part_ref[piece] = dot_nt(
            attended_ref[piece * rows : (piece + 1) * rows], weight_ref[...]
        ).astype(BF)

    summed = sum_pieces(part_ref, make, half_ref, whole_ref, sems.at[0], sems.at[1], peers, idle)
    residual = input_ref[...].astype(F32) + summed
    residual_ref[...] = residual
    all_ref[0] = (residual * row_scale(residual) * gain_ref[...].astype(F32)).astype(BF)
    gather_pieces(all_ref, sems.at[2], sems.at[3], peers, idle)


def mid_forward(attended, weight, inputs, gain):
    rows, width = inputs.shape
    return pl.pallas_call(
        mid_forward_kernel,
        name="mid_forward",
        out_shape=(
            jax.ShapeDtypeStruct((rows, width), F32),
            jax.ShapeDtypeStruct((4, rows, width), BF),
        ),
        in_specs=[VMEM] * 4,
        out_specs=(VMEM,) * 2,
        scratch_shapes=[
            pltpu.VMEM((4, rows, width), BF),
            pltpu.VMEM((2, rows // 2, width), BF),
            pltpu.VMEM((2, rows, width), BF),
            pltpu.SemaphoreType.DMA((4, 4)),
        ],
        compiler_params=pltpu.CompilerParams(
            collective_id=1, has_side_effects=True, vmem_limit_bytes=56 << 20
        ),
        cost_estimate=pl.CostEstimate(
            flops=80_000_000_000, bytes_accessed=20_000_000, transcendentals=0
        ),
    )(attended, weight, inputs, gain)


def row_grads(values, gain, back):
    scale = row_scale(values)
    scaled = back * gain
    return scale * scaled - values * (scale * scale * scale) * jnp.mean(
        scaled * values, axis=-1, keepdims=True
    )


def mid_backward_kernel(
    back_ref, residual_ref, cot_ref, gain_ref, slabs_ref,
    out_ref, all_ref, total_ref,
    part_ref, half_ref, whole_ref, sems, load_sem, *hop_refs,
):
    peers = swap_peers()
    hops = Hops(slabs_ref, total_ref, *hop_refs)
    greet(peers + hops.line[1:])
    hops.begin()

    def meanwhile(stage):
        if stage == 1:
            hops.onward()

    order = (3, 1, 2, 0)
    loads = [
        pltpu.make_async_copy(back_ref.at[piece], part_ref.at[piece], load_sem.at[piece])
        for piece in range(4)
    ]
    for piece in order:
        loads[piece].start()
    summed = sum_pieces(
        part_ref, lambda piece: loads[piece].wait(), half_ref, whole_ref,
        sems.at[0], sems.at[1], peers, meanwhile,
    )
    grads = cot_ref[...].astype(F32) + row_grads(
        residual_ref[...], gain_ref[...].astype(F32), summed
    )
    out_ref[...] = grads
    all_ref[0] = grads.astype(BF)
    gather_pieces(all_ref, sems.at[2], sems.at[3], peers, idle)
    hops.finish()


def mid_backward(back, residual, cot, gain, slabs):
    rows, width = residual.shape
    _, height, job_width = slabs.shape
    return pl.pallas_call(
        mid_backward_kernel,
        name="mid_backward",
        out_shape=(
            jax.ShapeDtypeStruct((rows, width), F32),
            jax.ShapeDtypeStruct((4, rows, width), BF),
            jax.ShapeDtypeStruct((height, job_width), F32),
        ),
        in_specs=[
            pl.BlockSpec(memory_space=pl.ANY), VMEM, VMEM, VMEM, pl.BlockSpec(memory_space=pl.ANY)
        ],
        out_specs=(VMEM,) * 3,
        scratch_shapes=[
            pltpu.VMEM((4, rows, width), BF),
            pltpu.VMEM((2, rows // 2, width), BF),
            pltpu.VMEM((2, rows, width), BF),
            pltpu.SemaphoreType.DMA((4, 4)),
            pltpu.SemaphoreType.DMA((4,)),
            *hop_scratch(height, job_width),
        ],
        compiler_params=pltpu.CompilerParams(
            collective_id=2, has_side_effects=True, vmem_limit_bytes=48 << 20
        ),
        cost_estimate=pl.CostEstimate(
            flops=80_000_000_000, bytes_accessed=20_000_000, transcendentals=0
        ),
    )(back.reshape(4, rows, width), residual, cot, gain, slabs)


def end_backward_kernel(
    grads_ref, weight_ref, input_ref, gain_ref, later_ref, slabs_ref,
    out_ref, total_ref, part_ref, half_ref, whole_ref, sems, *hop_refs,
):
    peers = swap_peers()
    rows = input_ref.shape[0]
    hops = Hops(slabs_ref, total_ref, *hop_refs)
    greet(peers + hops.line[1:])
    hops.begin()

    def meanwhile(stage):
        if stage == 1:
            hops.onward()

    def make(piece):
        part_ref[piece] = dot_nt(
            grads_ref[piece * rows : (piece + 1) * rows], weight_ref[...]
        ).astype(BF)

    summed = sum_pieces(
        part_ref, make, half_ref, whole_ref, sems.at[0], sems.at[1], peers, meanwhile
    )
    out_ref[...] = later_ref[...] + row_grads(
        input_ref[...].astype(F32), gain_ref[...].astype(F32), summed
    )
    hops.finish()


def end_backward(grads, weight, inputs, gain, later, slabs):
    rows, width = inputs.shape
    _, height, job_width = slabs.shape
    return pl.pallas_call(
        end_backward_kernel,
        name="end_backward",
        out_shape=(
            jax.ShapeDtypeStruct((rows, width), F32),
            jax.ShapeDtypeStruct((height, job_width), F32),
        ),
        in_specs=[VMEM] * 5 + [pl.BlockSpec(memory_space=pl.ANY)],
        out_specs=(VMEM, VMEM),
        scratch_shapes=[
            pltpu.VMEM((4, rows, width), BF),
            pltpu.VMEM((2, rows // 2, width), BF),
            pltpu.VMEM((2, rows, width), BF),
            pltpu.SemaphoreType.DMA((2, 4)),
            *hop_scratch(height, job_width),
        ],
        compiler_params=pltpu.CompilerParams(
            collective_id=3, has_side_effects=True, vmem_limit_bytes=48 << 20
        ),
        cost_estimate=pl.CostEstimate(
            flops=40_000_000_000, bytes_accessed=20_000_000, transcendentals=0
        ),
    )(grads, weight, inputs, gain, later, slabs)


class Line:
    def __init__(self):
        self.rank = lax.axis_index("tp")

    def row_order(self, values):
        count = values.shape[0] // 4
        return jnp.concatenate(
            [lax.dynamic_slice_in_dim(values, (self.rank ^ p) * count, count, 0) for p in range(4)]
        )

    def trunk_base(self):
        return self.rank * TRUNK

    def gather_rows(self, rows):
        half = rows.shape[0] // 2
        beside = by_tp(rows, X_SWAP)
        above = by_tp(rows, Y_SWAP)
        return jnp.concatenate(
            [rows, beside, above, by_tp(beside[:half], Y_SWAP), by_tp(above[half:], X_SWAP)]
        )

    def mid_forward(self, attended, weight, inputs, gain):
        residual, normed = mid_forward(attended, weight, inputs, gain)
        return residual, normed.reshape(-1, normed.shape[-1])

    def mid_backward(self, back, residual, cot, gain, slabs):
        grads, gathered, total = mid_backward(back, residual, cot, gain, slabs)
        return grads, gathered.reshape(-1, gathered.shape[-1]), total

    def chunks(self, rows, cot, blocks, residual):
        (full, at, width), second, third = blocks
        slabs, *sums = chunk_pass(rows, cot, full, at, width, None, False, True, None, (), 4)
        first = slabs
        full, at, width = second
        slabs, *sums, moved = chunk_pass(
            rows, cot, full, at, width, sums, False, True, "far", (first,), 5
        )
        full, at, width = third
        grads, *sums, total = chunk_pass(
            rows, cot, full, at, width, sums, True, False, "near", (first, moved), 6, residual
        )
        return sums, [total, None, grads], slabs

    def end_backward(self, grads, weight, inputs, gain, later, operands):
        return end_backward(grads, weight, inputs, gain, later, pair_hops(*operands))


class Plain:
    def row_order(self, values):
        return values

    def trunk_base(self):
        return jnp.int32(0)

    def gather_rows(self, rows):
        return lax.all_gather(rows, "tp", axis=0, tiled=True)

    def scatter_rows(self, partial):
        return lax.psum_scatter(partial.astype(F32), "tp", scatter_dimension=0, tiled=True)

    def mid_forward(self, attended, weight, inputs, gain):
        residual = inputs.astype(F32) + self.scatter_rows(dot_nt(attended, weight))
        normed = residual * row_scale(residual) * gain.astype(F32)
        normed = self.gather_rows(normed.astype(BF))
        return residual, normed

    def chunks(self, rows, cot, blocks, residual):
        sums = None
        parts = []
        for full, at, width in blocks:
            grads, *sums = chunk_pass(rows, cot, full, at, width, sums, len(parts) == len(blocks) - 1)
            parts.append(scatter_slabs(grads))
        back, out = sums
        return (back, (residual + self.scatter_rows(out)).astype(BF)), parts, None

    def mid_backward(self, back, residual, cot, gain, slabs):
        grads = row_grads(residual, gain.astype(F32), self.scatter_rows(back))
        grads = cot.astype(F32) + grads
        return grads, self.gather_rows(grads.astype(BF)), None

    def end_backward(self, grads, weight, inputs, gain, later, operands):
        sums = scatter_slabs(pair_grads(*operands))
        back = self.scatter_rows(dot_nt(grads, weight))
        return later + row_grads(inputs.astype(F32), gain.astype(F32), back), sums


def gather_slabs(shard):
    return lax.all_gather(shard, "fsdp", axis=0, tiled=True)


def scatter_slabs(grads):
    return lax.psum_scatter(grads, "fsdp", scatter_dimension=0, tiled=True).astype(F32)


def body(
    make_links,
    layer_input,
    cotangent,
    segment_ids,
    path_positions,
    ancestor_masks,
    attn_gain,
    query_weight,
    key_weight,
    value_weight,
    out_weight,
    mlp_gain,
    gate_weight,
    up_weight,
    down_weight,
):
    links = make_links()
    heads = query_weight.shape[1] // HD
    groups = key_weight.shape[1] // HD
    q_width, kv_width = heads * HD, groups * HD
    qkv_width = q_width + 2 * kv_width
    units = gate_weight.shape[1]
    edges = [units * sum(PARTS[:i]) // sum(PARTS) for i in range(len(PARTS) + 1)]

    gain_rows = gather_slabs(jnp.stack([attn_gain, mlp_gain], axis=1))
    first_gain, second_gain = gain_rows[:, 0][None, :], gain_rows[:, 1][None, :]
    own_qkv = jnp.concatenate([query_weight, key_weight, value_weight], axis=1)
    attn_full = gather_slabs(jnp.concatenate([own_qkv, out_weight.T], axis=1))
    qkv_full, out_full = attn_full[:, :qkv_width], attn_full[:, qkv_width:]
    own_down = down_weight.T
    own_mlp = [
        jnp.concatenate([gate_weight[:, cut], up_weight[:, cut], own_down[:, cut]], axis=1)
        for cut in map(slice, edges[:-1], edges[1:])
    ]
    early = gather_slabs(jnp.concatenate(own_mlp[:EARLY], axis=1))
    mlp_full = [(early, place) for place in range(EARLY)]
    mlp_full += [(gather_slabs(own), 0) for own in own_mlp[EARLY:]]

    positions = links.row_order(path_positions)
    angles = positions.astype(F32)[:, None] * jnp.asarray(inverse_freq(HD))[None, :]
    cosine, sine = jnp.cos(angles), jnp.sin(angles)
    cosine = jnp.concatenate([cosine] * 4, axis=1)
    sine = jnp.concatenate([-sine, sine] * 2, axis=1)
    segs = links.row_order(segment_ids)[::SEG]
    masks = ancestor_masks.reshape(SEGS * SEGS)
    base = jnp.reshape(links.trunk_base(), (1,)).astype(jnp.int32)

    inputs = layer_input.astype(F32)
    cot_all = links.gather_rows(cotangent)
    first_rows = (inputs * row_scale(inputs) * first_gain.astype(F32)).astype(BF)
    first_normed = after(links.gather_rows(first_rows), cot_all)

    qkv_pre = dot_nn(first_normed, qkv_full)
    attended, queries, keys, vals = attention_forward(
        heads, groups, masks, segs, base, qkv_pre, cosine, sine
    )
    residual, second_normed = links.mid_forward(attended, out_full, layer_input, second_gain)

    widths = [own.shape[1] for own in own_mlp]
    (back_sum, output), mlp_sums, slabs = links.chunks(
        second_normed,
        cot_all,
        [(*pair, width) for pair, width in zip(mlp_full, widths)],
        residual,
    )
    residual_back, branch_back, total = links.mid_backward(
        back_sum, residual, cotangent, second_gain, slabs
    )
    if total is not None:
        mlp_sums = [mlp_sums[0], total, scatter_slabs(after(mlp_sums[2], branch_back))]
    attended_back = dot_nn(branch_back, out_full).astype(BF)
    qkv_back = attention_backward(
        heads, groups, masks, segs, base, queries, keys, vals, attended_back, cosine, sine
    )
    input_grad, attn_sum = links.end_backward(
        qkv_back,
        qkv_full,
        layer_input,
        first_gain,
        residual_back,
        (first_normed, qkv_back, branch_back, attended),
    )
    qkv_sum = attn_sum[:, :qkv_width]

    thirds = [
        [part[:, at * part.shape[1] // 3 : (at + 1) * part.shape[1] // 3] for part in mlp_sums]
        for at in range(3)
    ]
    gate_sum, up_sum = jnp.concatenate(thirds[0], axis=1), jnp.concatenate(thirds[1], axis=1)
    down_sum = jnp.concatenate(thirds[2], axis=1).T
    attn_part = jnp.sum(own_qkv.astype(F32) * qkv_sum, axis=1)
    mlp_part = jnp.sum(
        gate_weight.astype(F32) * gate_sum + up_weight.astype(F32) * up_sum, axis=1
    )
    attn_total, mlp_total = lax.psum((attn_part, mlp_part), "tp")
    return (
        output,
        input_grad,
        attn_total / attn_gain.astype(F32),
        qkv_sum[:, :q_width],
        qkv_sum[:, q_width : q_width + kv_width],
        qkv_sum[:, q_width + kv_width :],
        attn_sum[:, qkv_width:].T,
        mlp_total / mlp_gain.astype(F32),
        gate_sum,
        up_sum,
        down_sum,
    )


def solution(mesh):
    fits = mesh.shape["fsdp"] == 8 and mesh.shape["tp"] == 4
    return jax.shard_map(
        functools.partial(body, Line if fits else Plain),
        mesh=mesh,
        in_specs=(
            P(("fsdp", "tp"), None),
            P(("fsdp", "tp"), None),
            P("fsdp"),
            P("fsdp"),
            P("fsdp", None, None),
            P("fsdp"),
            P("fsdp", "tp"),
            P("fsdp", "tp"),
            P("fsdp", "tp"),
            P("tp", "fsdp"),
            P("fsdp"),
            P("fsdp", "tp"),
            P("fsdp", "tp"),
            P("tp", "fsdp"),
        ),
        out_specs=(
            P(("fsdp", "tp"), None),
            P(("fsdp", "tp"), None),
            P("fsdp"),
            P("fsdp", "tp"),
            P("fsdp", "tp"),
            P("fsdp", "tp"),
            P("tp", "fsdp"),
            P("fsdp"),
            P("fsdp", "tp"),
            P("fsdp", "tp"),
            P("tp", "fsdp"),
        ),
        check_vma=False,
    )
```

```python
import functools
import math

import jax
import jax.numpy as jnp
import numpy as np
from jax import lax
from jax.experimental import pallas as pl
from jax.experimental.pallas import tpu as pltpu
from jax.sharding import PartitionSpec as P

HD = 64
SEGS = 13
SEG = 64
TRUNK = 256
BRANCHES = 4
EPSILON = 1e-05
PARTS = (2, 3, 3)
NEG = -1e30
BF = jnp.bfloat16
F32 = jnp.float32


def inverse_freq(head_size):
    base_freq = 1.0 / 500000.0 ** (np.arange(0, head_size, 2) / head_size)
    wavelen = 2.0 * math.pi / base_freq
    smooth = (8192.0 / wavelen - 1.0) / 3.0
    blended = (1.0 - smooth) * base_freq / 32.0 + smooth * base_freq
    scaled = np.where(
        wavelen > 8192.0, base_freq / 32.0, np.where(wavelen < 2048.0, base_freq, blended)
    )
    return scaled.astype(np.float32)


def dot_nn(left, right):
    return lax.dot_general(
        left, right, (((1,), (0,)), ((), ())), preferred_element_type=F32
    )


def dot_nt(left, right):
    return lax.dot_general(
        left, right, (((1,), (1,)), ((), ())), preferred_element_type=F32
    )


def dot_tn(left, right):
    return lax.dot_general(
        left, right, (((0,), (0,)), ((), ())), preferred_element_type=F32
    )


def rope_lanes(values, cosine, signed_sine, low_half):
    rolled = jnp.where(low_half, pltpu.roll(values, 96, 1), pltpu.roll(values, 32, 1))
    return values * cosine + rolled * signed_sine


def rope_lanes_back(grads, cosine, signed_sine, low_half):
    scaled = grads * signed_sine
    rolled = jnp.where(low_half, pltpu.roll(scaled, 96, 1), pltpu.roll(scaled, 32, 1))
    return grads * cosine + rolled


def low_half_mask(rows):
    lane = lax.broadcasted_iota(jnp.int32, (rows, 128), 1)
    return lax.rem(lane, HD) < HD // 2


def parent_block(mask_ref, seg_ref, segment, block_count):
    parent = jnp.int32(0)
    for branch in range(1, BRANCHES + 1):
        parent = parent + branch * mask_ref[segment * SEGS + branch]
    parent = jnp.where(segment > BRANCHES, parent, segment)
    found = jnp.int32(0)
    for block in range(block_count):
        found = found + block * (seg_ref[block] == parent).astype(jnp.int32)
    return found


def block_mask(has_parent, members):
    shape = (members * SEG, 2 * SEG)
    row = lax.rem(lax.broadcasted_iota(jnp.int32, shape, 0), SEG)
    col = lax.broadcasted_iota(jnp.int32, shape, 1)
    return ((col < SEG) & has_parent) | ((col >= SEG) & (col - SEG <= row))


def trunk_mask(index, members):
    shape = (members * SEG, TRUNK)
    row = lax.rem(lax.broadcasted_iota(jnp.int32, shape, 0), SEG) + index * SEG
    col = lax.broadcasted_iota(jnp.int32, shape, 1)
    return col <= row


def softmax_rows(scores):
    row_max = jnp.max(scores, axis=-1, keepdims=True)
    exponent = jnp.exp(scores - row_max)
    return exponent / jnp.sum(exponent, axis=-1, keepdims=True)


def attn_fwd_kernel(
    heads, groups, mask_ref, seg_ref, base_ref, pre_ref, cos_ref, sin_ref,
    att_ref, q_ref, k_ref, v_ref,
):
    rows = pre_ref.shape[0]
    blocks = rows // SEG
    members = heads // groups
    score_scale = HD ** (-0.5)
    low_half = low_half_mask(rows)
    cosine = cos_ref[...]
    sine = sin_ref[...]
    q_width = heads * HD
    kv_width = groups * HD

    def put_heads(dest, first, wide, count):
        for half in range(count):
            head = first + half
            part = wide[:, half * HD : (half + 1) * HD].reshape(blocks, SEG, HD)
            group, member = head // members, head % members
            dest[group, :, member * SEG : (member + 1) * SEG, :] = part

    for pair in range(q_width // 128):
        lanes = pre_ref[:, pair * 128 : (pair + 1) * 128]
        put_heads(q_ref, 2 * pair, rope_lanes(lanes, cosine, sine, low_half).astype(BF), 2)
    if kv_width % 128 == 0:
        for pair in range(kv_width // 128):
            at = q_width + pair * 128
            wide = rope_lanes(pre_ref[:, at : at + 128], cosine, sine, low_half).astype(BF)
            at = q_width + kv_width + pair * 128
            plain = pre_ref[:, at : at + 128].astype(BF)
            for half in range(2):
                k_ref[2 * pair + half] = wide[:, half * HD : (half + 1) * HD]
                v_ref[2 * pair + half] = plain[:, half * HD : (half + 1) * HD]
    else:
        both = pre_ref[:, q_width : q_width + 128]
        k_ref[0] = rope_lanes(both, cosine, sine, low_half).astype(BF)[:, :HD]
        v_ref[0] = both.astype(BF)[:, HD:]

    base = base_ref[0]
    trunk_block = base // SEG
    trunk_rows = pl.ds(pl.multiple_of(base, TRUNK), TRUNK)

    def store(group, block, mixed):
        at = pl.ds(pl.multiple_of(block * SEG, SEG), SEG)
        for member in range(members):
            head = group * members + member
            att_ref[at, head * HD : (head + 1) * HD] = mixed[
                member * SEG : (member + 1) * SEG
            ].astype(BF)

    for group in range(groups):
        def one_block(block, carry):
            inside = block - trunk_block
            is_trunk = (inside >= 0) & (inside < TRUNK // SEG)

            @pl.when(is_trunk)
            def _():
                queries = q_ref[group, block]
                scores = dot_nt(queries, k_ref[group, trunk_rows, :]) * score_scale
                scores = jnp.where(trunk_mask(inside, members), scores, NEG)
                probs = softmax_rows(scores).astype(BF)
                store(group, block, dot_nn(probs, v_ref[group, trunk_rows, :]))

            @pl.when(jnp.logical_not(is_trunk))
            def _():
                segment = seg_ref[block]
                parent = parent_block(mask_ref, seg_ref, segment, blocks)
                up = pl.ds(pl.multiple_of(parent * SEG, SEG), SEG)
                own = pl.ds(pl.multiple_of(block * SEG, SEG), SEG)
                queries = q_ref[group, block]
                keys = jnp.concatenate(
                    [k_ref[group, trunk_rows, :], k_ref[group, up, :], k_ref[group, own, :]], axis=0
                )
                vals = jnp.concatenate(
                    [v_ref[group, trunk_rows, :], v_ref[group, up, :], v_ref[group, own, :]], axis=0
                )
                scores = dot_nt(queries, keys) * score_scale
                tail = jnp.where(
                    block_mask(segment > BRANCHES, members), scores[:, TRUNK:], NEG
                )
                scores = jnp.concatenate([scores[:, :TRUNK], tail], axis=1)
                probs = softmax_rows(scores).astype(BF)
                store(group, block, dot_nn(probs, vals))

            return carry

        lax.fori_loop(0, blocks, one_block, 0)


def attn_bwd_kernel(
    heads, groups, mask_ref, seg_ref, base_ref, q_ref, k_ref, v_ref, grad_ref, cos_ref, sin_ref,
    out_ref, g_ref, dq_ref, dk_ref, dv_ref,
):
    rows = grad_ref.shape[0]
    blocks = rows // SEG
    members = heads // groups
    score_scale = HD ** (-0.5)
    low_half = low_half_mask(rows)
    cosine = cos_ref[...]
    sine = sin_ref[...]
    q_width = heads * HD
    kv_width = groups * HD
    for head in range(heads):
        part = grad_ref[:, head * HD : (head + 1) * HD].reshape(blocks, SEG, HD)
        group, member = head // members, head % members
        g_ref[group, :, member * SEG : (member + 1) * SEG, :] = part
    dk_ref[...] = jnp.zeros_like(dk_ref)
    dv_ref[...] = jnp.zeros_like(dv_ref)
    base = base_ref[0]
    trunk_block = base // SEG
    trunk_rows = pl.ds(pl.multiple_of(base, TRUNK), TRUNK)

    def store(group, block, d_query):
        at = pl.ds(pl.multiple_of(block * SEG, SEG), SEG)
        for member in range(members):
            head = group * members + member
            dq_ref[at, head * HD : (head + 1) * HD] = d_query[member * SEG : (member + 1) * SEG]

    for group in range(groups):
        lanes = slice(group * HD, (group + 1) * HD)

        def grads(queries, out_grads, keys, vals, scores):
            probs = softmax_rows(scores)
            prob_back = dot_nt(out_grads, vals)
            delta = jnp.sum(probs * prob_back, axis=-1, keepdims=True)
            score_back = (probs * (prob_back - delta)).astype(BF)
            d_query = dot_nn(score_back, keys) * score_scale
            d_key = dot_tn(score_back, queries) * score_scale
            d_val = dot_tn(probs.astype(BF), out_grads)
            return d_query, d_key, d_val

        def one_block(block, carry):
            inside = block - trunk_block
            is_trunk = (inside >= 0) & (inside < TRUNK // SEG)

            @pl.when(is_trunk)
            def _():
                queries = q_ref[group, block]
                keys = k_ref[group, trunk_rows, :]
                scores = dot_nt(queries, keys) * score_scale
                scores = jnp.where(trunk_mask(inside, members), scores, NEG)
                d_query, d_key, d_val = grads(
                    queries, g_ref[group, block], keys, v_ref[group, trunk_rows, :], scores
                )
                store(group, block, d_query)
                dk_ref[trunk_rows, lanes] += d_key
                dv_ref[trunk_rows, lanes] += d_val

            @pl.when(jnp.logical_not(is_trunk))
            def _():
                segment = seg_ref[block]
                parent = parent_block(mask_ref, seg_ref, segment, blocks)
                up = pl.ds(pl.multiple_of(parent * SEG, SEG), SEG)
                own = pl.ds(pl.multiple_of(block * SEG, SEG), SEG)
                queries = q_ref[group, block]
                keys = jnp.concatenate(
                    [k_ref[group, trunk_rows, :], k_ref[group, up, :], k_ref[group, own, :]], axis=0
                )
                vals = jnp.concatenate(
                    [v_ref[group, trunk_rows, :], v_ref[group, up, :], v_ref[group, own, :]], axis=0
                )
                scores = dot_nt(queries, keys) * score_scale
                tail = jnp.where(
                    block_mask(segment > BRANCHES, members), scores[:, TRUNK:], NEG
                )
                scores = jnp.concatenate([scores[:, :TRUNK], tail], axis=1)
                d_query, d_key, d_val = grads(queries, g_ref[group, block], keys, vals, scores)
                store(group, block, d_query)
                for ref, val in ((dk_ref, d_key), (dv_ref, d_val)):
                    ref[trunk_rows, lanes] += val[:TRUNK]
                    ref[up, lanes] += val[TRUNK : TRUNK + SEG]
                    ref[own, lanes] += val[TRUNK + SEG :]

            return carry

        lax.fori_loop(0, blocks, one_block, 0)
    for pair in range(q_width // 128):
        at = slice(pair * 128, (pair + 1) * 128)
        out_ref[:, at] = rope_lanes_back(dq_ref[:, at], cosine, sine, low_half).astype(BF)
    if kv_width % 128 == 0:
        for pair in range(kv_width // 128):
            at = slice(pair * 128, (pair + 1) * 128)
            turned = rope_lanes_back(dk_ref[:, at], cosine, sine, low_half)
            out_ref[:, q_width + pair * 128 : q_width + (pair + 1) * 128] = turned.astype(BF)
            first = q_width + kv_width + pair * 128
            out_ref[:, first : first + 128] = dv_ref[:, at].astype(BF)
    else:
        wide = jnp.concatenate([dk_ref[...], dv_ref[...]], axis=1)
        turned = rope_lanes_back(wide, cosine, sine, low_half)
        lane = lax.broadcasted_iota(jnp.int32, (rows, 128), 1)
        out_ref[:, q_width : q_width + 128] = jnp.where(lane < HD, turned, wide).astype(BF)


LIGHT = pl.CostEstimate(flops=1000, bytes_accessed=1000, transcendentals=0)
SMEM = pl.BlockSpec(memory_space=pltpu.SMEM)
VMEM = pl.BlockSpec(memory_space=pltpu.VMEM)


def attention_forward(heads, groups, masks, segs, base, pre, cosine, sine):
    rows = pre.shape[0]
    members = heads // groups
    blocks = rows // SEG
    return pl.pallas_call(
        functools.partial(attn_fwd_kernel, heads, groups),
        name="attn_fwd",
        out_shape=(
            jax.ShapeDtypeStruct((rows, heads * HD), BF),
            jax.ShapeDtypeStruct((groups, blocks, members * SEG, HD), BF),
            jax.ShapeDtypeStruct((groups, rows, HD), BF),
            jax.ShapeDtypeStruct((groups, rows, HD), BF),
        ),
        in_specs=[SMEM, SMEM, SMEM, VMEM, VMEM, VMEM],
        out_specs=(VMEM, VMEM, VMEM, VMEM),
        compiler_params=pltpu.CompilerParams(vmem_limit_bytes=40 << 20),
        cost_estimate=LIGHT,
    )(masks, segs, base, pre, cosine, sine)


def attention_backward(heads, groups, masks, segs, base, queries, keys, vals, grads, cosine, sine):
    rows = grads.shape[0]
    members = heads // groups
    blocks = rows // SEG
    return pl.pallas_call(
        functools.partial(attn_bwd_kernel, heads, groups),
        name="attn_bwd",
        out_shape=jax.ShapeDtypeStruct((rows, (heads + 2 * groups) * HD), BF),
        in_specs=[SMEM, SMEM, SMEM, VMEM, VMEM, VMEM, VMEM, VMEM, VMEM],
        out_specs=VMEM,
        scratch_shapes=[
            pltpu.VMEM((groups, blocks, members * SEG, HD), BF),
            pltpu.VMEM((rows, heads * HD), F32),
            pltpu.VMEM((rows, groups * HD), F32),
            pltpu.VMEM((rows, groups * HD), F32),
        ],
        compiler_params=pltpu.CompilerParams(vmem_limit_bytes=40 << 20),
        cost_estimate=LIGHT,
    )(masks, segs, base, queries, keys, vals, grads, cosine, sine)


MESH = pl.DeviceIdType.MESH


def swap_peers():
    rank = lax.axis_index("tp")
    place = lax.axis_index("fsdp")
    return [(place, rank + 1 - 2 * (rank % 2)), (place, (rank + 2) % 4)]


def greet(peers):
    barrier = pltpu.get_barrier_semaphore()
    for peer in peers:
        pl.semaphore_signal(barrier, inc=1, device_id=peer, device_id_type=MESH)
    pl.semaphore_wait(barrier, len(peers))


def send(source, target, send_sem, recv_sem, peer):
    copy = pltpu.make_async_remote_copy(
        src_ref=source,
        dst_ref=target,
        send_sem=send_sem,
        recv_sem=recv_sem,
        device_id=peer,
        device_id_type=MESH,
    )
    copy.start()
    return copy


def line_peers():
    place = lax.axis_index("fsdp")
    rank = lax.axis_index("tp")
    z, core = place // 2, place % 2
    up, down = (z + 1) % 4, (z + 3) % 4
    return z, core, [(2 * z + 1 - core, rank), (2 * up + core, rank), (2 * down + core, rank)]


def far_copies(far_ref, far_recv, send_sem, recv_sem, z, peers):
    heading = z // 2
    place = lax.axis_index("fsdp")
    target = (place + 2 - 4 * heading, lax.axis_index("tp"))
    return pltpu.make_async_remote_copy(
        src_ref=far_ref,
        dst_ref=far_recv.at[heading],
        send_sem=send_sem,
        recv_sem=recv_sem.at[heading],
        device_id=target,
        device_id_type=MESH,
    )


def far_add(pair_ref, far_recv, recv_sem, z, peers):
    @pl.when((z == 1) | (z == 2))
    def _():
        for heading in range(2):
            pltpu.make_async_remote_copy(
                src_ref=far_recv.at[heading],
                dst_ref=far_recv.at[heading],
                send_sem=recv_sem.at[heading],
                recv_sem=recv_sem.at[heading],
                device_id=peers[0],
                device_id_type=MESH,
            ).wait_recv()
        pair_ref[0] = (pair_ref[0].astype(F32) + far_recv[1].astype(F32)).astype(BF)
        pair_ref[1] = (pair_ref[1].astype(F32) + far_recv[0].astype(F32)).astype(BF)


def near_copies(pair_ref, near_recv, send_sem, recv_sem, peers):
    return [
        pltpu.make_async_remote_copy(
            src_ref=pair_ref.at[at],
            dst_ref=near_recv.at[at],
            send_sem=send_sem.at[at],
            recv_sem=recv_sem.at[at],
            device_id=peers[2 - at],
            device_id_type=MESH,
        )
        for at in range(2)
    ]


class Hops:
    def __init__(self, slabs_ref, total_ref, pair_ref, slab_ref, far_recv, near_recv, sends, recvs, loads):
        self.z, _, self.line = line_peers()
        self.total_ref, self.pair_ref, self.slab_ref = total_ref, pair_ref, slab_ref
        self.far_recv, self.near_recv, self.recvs = far_recv, near_recv, recvs
        self.far = far_copies(
            slabs_ref.at[0], far_recv, sends.at[0, 0], recvs.at[0], self.z, self.line
        )
        self.loads = [
            pltpu.make_async_copy(slabs_ref.at[1 + at], pair_ref.at[at], loads.at[at])
            for at in range(2)
        ] + [pltpu.make_async_copy(slabs_ref.at[3], slab_ref, loads.at[2])]
        self.near = near_copies(pair_ref, near_recv, sends.at[1], recvs.at[1], self.line)

    def begin(self):
        self.far.start()
        for load in self.loads:
            load.start()

    def onward(self):
        for load in self.loads:
            load.wait()
        self.far.wait_send()
        far_add(self.pair_ref, self.far_recv, self.recvs.at[0], self.z, self.line)
        for copy in self.near:
            copy.start()

    def finish(self):
        for copy in self.near:
            copy.wait()
        self.total_ref[...] = (
            self.slab_ref[...].astype(F32)
            + self.near_recv[0].astype(F32)
            + self.near_recv[1].astype(F32)
        )


def hop_scratch(height, width):
    return [
        pltpu.VMEM((2, height, width), BF),
        pltpu.VMEM((height, width), BF),
        pltpu.VMEM((2, height, width), BF),
        pltpu.VMEM((2, height, width), BF),
        pltpu.SemaphoreType.DMA((2, 2)),
        pltpu.SemaphoreType.DMA((2, 2)),
        pltpu.SemaphoreType.DMA((3,)),
    ]


SLOTS = (2, 1, 3, 0)


def chunk_kernel(cfg, *refs):
    steps, slabs, first, last, cores, job, offset = cfg
    refs = list(refs)
    take = lambda count: [refs.pop(0) for _ in range(count)]
    rows_ref, cot_ref, source_ref = take(3)
    if not first:
        back_in_ref, out_in_ref = take(2)
    if job == "far":
        (slabs_ref,) = take(1)
    if job == "near":
        slabs_ref, moved_ref = take(2)
    grad_ref, back_ref, out_ref = take(3)
    if job == "far":
        (moved_ref,) = take(1)
    if job == "near":
        (total_ref,) = take(1)
    pair_ref, hidden_ref, full_ref, full_sem = take(4)
    if cores:
        mine_ref, theirs_ref, core_send, core_recv = take(4)
    if job:
        job_recv, job_send_sem, job_recv_sem, load_sem = take(4)
    if job == "near":
        (slab_ref,) = take(1)

    step = pl.program_id(0)
    end = steps + slabs - 1
    chunk = hidden_ref.shape[1]
    tile = chunk // steps
    height = rows_ref.shape[1] // slabs
    fetches = [
        pltpu.make_async_copy(
            source_ref.at[:, pl.ds(offset + third * chunk, chunk)],
            full_ref.at[:, pl.ds(third * chunk, chunk)],
            full_sem.at[third],
        )
        for third in range(3)
    ]

    @pl.when(step == 0)
    def _():
        for fetch in fetches:
            fetch.start()

    def fetched(at, third):
        if at == 0:
            fetches[third].wait()

    if cores or job:
        z, core, peers = line_peers()
        far = None
        if job == "far":
            loads = [
                pltpu.make_async_copy(slabs_ref.at[1 + at], moved_ref.at[at], load_sem.at[at])
                for at in range(2)
            ]
            far = far_copies(slabs_ref.at[0], job_recv, job_send_sem.at[0], job_recv_sem, z, peers)
        if job == "near":
            loads = [pltpu.make_async_copy(slabs_ref.at[3], slab_ref, load_sem.at[0])]
            near = near_copies(moved_ref, job_recv, job_send_sem, job_recv_sem, peers)

        @pl.when(step == 0)
        def _():
            greet(peers)
            if job == "far":
                far.start()
            if job == "near":
                for copy in near:
                    copy.start()
            if job:
                for load in loads:
                    load.start()

    for at in range(steps):

        @pl.when(step == at)
        def _():
            cut = slice(at * tile, (at + 1) * tile)
            fetched(at, 0)
            gate = dot_nn(rows_ref[...], full_ref[:, cut])
            fetched(at, 1)
            up = dot_nn(rows_ref[...], full_ref[:, chunk + at * tile : chunk + (at + 1) * tile])
            fetched(at, 2)
            back = dot_nn(
                cot_ref[...], full_ref[:, 2 * chunk + at * tile : 2 * chunk + (at + 1) * tile]
            )
            sigmoid = 1.0 / (1.0 + jnp.exp(-gate))
            silu = gate * sigmoid
            hidden_ref[:, cut] = (silu * up).astype(BF)
            pair_ref[:, cut] = (back * up * sigmoid * (1.0 + gate * (1.0 - sigmoid))).astype(BF)
            pair_ref[:, chunk + at * tile : chunk + (at + 1) * tile] = (back * silu).astype(BF)

    def write(slab, target_ref, added_ref):
        at = pl.ds(pl.multiple_of(slab * height, height), height)
        grad = dot_tn(rows_ref[:, at], pair_ref[...])
        more = dot_tn(cot_ref[:, at], hidden_ref[...])
        if added_ref is not None:
            grad = grad.astype(BF).astype(F32) + added_ref[:, : 2 * chunk].astype(F32)
            more = more.astype(BF).astype(F32) + added_ref[:, 2 * chunk :].astype(F32)
        target_ref[:, : 2 * chunk] = grad.astype(BF)
        target_ref[:, 2 * chunk :] = more.astype(BF)

    @pl.when(step >= steps)
    def _():
        slab = pl.ds(pl.multiple_of((step - steps) * height, height), height)
        back = dot_nt(pair_ref[...], full_ref[slab, : 2 * chunk])
        out = dot_nt(hidden_ref[...], full_ref[slab, 2 * chunk :])
        back = back if first else back_in_ref[...] + back
        out = out if first else out_in_ref[...] + out
        back_ref[...] = back.astype(back_ref.dtype)
        out_ref[...] = out.astype(out_ref.dtype)
        if not cores:
            write(step - steps, grad_ref, None)

    if cores:
        copies = [
            pltpu.make_async_remote_copy(
                src_ref=mine_ref.at[at % 2],
                dst_ref=theirs_ref.at[at],
                send_sem=core_send.at[at],
                recv_sem=core_recv.at[at],
                device_id=peers[0],
                device_id_type=MESH,
            )
            for at in range(4)
        ]
        for at, slot in enumerate(SLOTS):
            chip = (z + 4 - slot) % 4

            @pl.when(step == steps + at)
            def _():
                if at >= 2:
                    copies[at - 2].wait_send()
                write(2 * chip + 1 - core, mine_ref.at[at % 2], None)
                copies[at].start()

            @pl.when(step == steps + 4 + at)
            def _():
                copies[at].wait_recv()
                write(2 * chip + core, grad_ref.at[0], theirs_ref.at[at])

        @pl.when(step == end)
        def _():
            copies[2].wait_send()
            copies[3].wait_send()

    if job == "far":

        @pl.when(step == end)
        def _():
            for load in loads:
                load.wait()
            far.wait_send()
            far_add(moved_ref, job_recv, job_recv_sem, z, peers)

    if job == "near":

        @pl.when(step == end)
        def _():
            loads[0].wait()
            for copy in near:
                copy.wait()
            total_ref[...] = (
                slab_ref[...].astype(F32) + job_recv[0].astype(F32) + job_recv[1].astype(F32)
            )


def chunk_pass(rows, cot, full, at, width, sums, last, cores=False, job=None, operands=(), number=None):
    count, depth = rows.shape
    chunk = width // 3
    slabs = 8
    height = depth // slabs
    steps = max(1, chunk // 256)
    first = sums is None
    whole = pl.BlockSpec(memory_space=pltpu.VMEM)
    anywhere = pl.BlockSpec(memory_space=pl.ANY)

    def place(i):
        return jnp.maximum(i - steps, 0)

    column = pl.BlockSpec((count, height), lambda i: (0, place(i)))
    total = jax.ShapeDtypeStruct((count, depth), BF if last else F32)
    if cores:
        grad_shape = jax.ShapeDtypeStruct((4, height, width), BF)
        grad_spec = pl.BlockSpec((1, height, width), lambda i: (jnp.maximum(place(i) - 4, 0), 0, 0))
    else:
        grad_shape = jax.ShapeDtypeStruct((depth, width), BF)
        grad_spec = pl.BlockSpec((height, width), lambda i: (place(i), 0))
    out_shapes, out_specs = [grad_shape, total, total], [grad_spec, column, column]
    in_specs = [whole, whole, anywhere] + ([] if first else [column, column])
    dma = pltpu.SemaphoreType.DMA
    scratch = [
        pltpu.VMEM((count, 2 * chunk), BF),
        pltpu.VMEM((count, chunk), BF),
        pltpu.VMEM((depth, width), BF),
        dma((3,)),
    ]
    if cores:
        scratch += [
            pltpu.VMEM((2, height, width), BF),
            pltpu.VMEM((4, height, width), BF),
            dma((4,)),
            dma((4,)),
        ]
    if job:
        job_width = operands[0].shape[-1]
        scratch += [pltpu.VMEM((2, height, job_width), BF), dma((2,)), dma((2,)), dma((2,))]
    if job == "far":
        in_specs += [anywhere]
        out_shapes += [jax.ShapeDtypeStruct((2, height, job_width), BF)]
        out_specs += [whole]
    if job == "near":
        in_specs += [anywhere, anywhere]
        out_shapes += [jax.ShapeDtypeStruct((height, job_width), F32)]
        out_specs += [whole]
        scratch += [pltpu.VMEM((height, job_width), BF)]
    remote = cores or job
    return pl.pallas_call(
        functools.partial(chunk_kernel, (steps, slabs, first, last, cores, job, at)),
        name="chunk_pass",
        out_shape=tuple(out_shapes),
        grid=(steps + slabs,),
        in_specs=in_specs,
        out_specs=tuple(out_specs),
        scratch_shapes=scratch,
        input_output_aliases={} if first or last else {3: 1, 4: 2},
        compiler_params=pltpu.CompilerParams(
            vmem_limit_bytes=60 << 20,
            collective_id=number if remote else None,
            has_side_effects=bool(remote),
        ),
        cost_estimate=pl.CostEstimate(
            flops=6 * count * depth * width,
            bytes_accessed=8 * count * depth + 4 * depth * width + 16 * count * depth,
            transcendentals=count * chunk,
        ),
    )(rows, cot, full, *(() if first else sums), *operands)


def pair_kernel(left_ref, first_ref, other_ref, second_ref, out_ref):
    width = first_ref.shape[1]
    out_ref[:, :width] = dot_tn(left_ref[...], first_ref[...]).astype(BF)
    out_ref[:, width:] = dot_tn(other_ref[...], second_ref[...]).astype(BF)


def pair_grads(left, first, other, second):
    count, depth = left.shape
    width = first.shape[1] + second.shape[1]
    height = 256
    whole = pl.BlockSpec(memory_space=pltpu.VMEM)
    column = pl.BlockSpec((count, height), lambda i: (0, i))
    return pl.pallas_call(
        pair_kernel,
        name="pair_grads",
        out_shape=jax.ShapeDtypeStruct((depth, width), BF),
        grid=(depth // height,),
        in_specs=[column, whole, column, whole],
        out_specs=pl.BlockSpec((height, width), lambda i: (i, 0)),
        compiler_params=pltpu.CompilerParams(vmem_limit_bytes=32 << 20),
        cost_estimate=LIGHT,
    )(left, first, other, second)


def pair_hops_kernel(
    left_ref, first_ref, other_ref, second_ref, out_ref, mine_ref, theirs_ref, core_send, core_recv
):
    step = pl.program_id(0)
    z, core, peers = line_peers()
    width = first_ref.shape[1]
    height = out_ref.shape[1]

    def write(slab, target_ref, added_ref):
        at = pl.ds(pl.multiple_of(slab * height, height), height)
        grad = dot_tn(left_ref[:, at], first_ref[...])
        more = dot_tn(other_ref[:, at], second_ref[...])
        if added_ref is not None:
            grad = grad.astype(BF).astype(F32) + added_ref[:, :width].astype(F32)
            more = more.astype(BF).astype(F32) + added_ref[:, width:].astype(F32)
        target_ref[:, :width] = grad.astype(BF)
        target_ref[:, width:] = more.astype(BF)

    @pl.when(step == 0)
    def _():
        greet(peers[:1])

    copies = [
        pltpu.make_async_remote_copy(
            src_ref=mine_ref.at[at],
            dst_ref=theirs_ref.at[at],
            send_sem=core_send.at[at],
            recv_sem=core_recv.at[at],
            device_id=peers[0],
            device_id_type=MESH,
        )
        for at in range(4)
    ]
    for at, slot in enumerate(SLOTS):
        chip = (z + 4 - slot) % 4

        @pl.when(step == at)
        def _():
            write(2 * chip + 1 - core, mine_ref.at[at], None)
            copies[at].start()

        @pl.when(step == 4 + at)
        def _():
            copies[at].wait_recv()
            write(2 * chip + core, out_ref.at[0], theirs_ref.at[at])

    @pl.when(step == 7)
    def _():
        for copy in copies:
            copy.wait_send()


def pair_hops(left, first, other, second):
    count, depth = left.shape
    width = first.shape[1] + second.shape[1]
    height = depth // 8
    return pl.pallas_call(
        pair_hops_kernel,
        name="pair_hops",
        out_shape=jax.ShapeDtypeStruct((4, height, width), BF),
        grid=(8,),
        in_specs=[VMEM] * 4,
        out_specs=pl.BlockSpec((1, height, width), lambda i: (jnp.maximum(i - 4, 0), 0, 0)),
        scratch_shapes=[
            pltpu.VMEM((4, height, width), BF),
            pltpu.VMEM((4, height, width), BF),
            pltpu.SemaphoreType.DMA((4,)),
            pltpu.SemaphoreType.DMA((4,)),
        ],
        compiler_params=pltpu.CompilerParams(
            collective_id=7, has_side_effects=True, vmem_limit_bytes=48 << 20
        ),
        cost_estimate=pl.CostEstimate(
            flops=2 * count * depth * width,
            bytes_accessed=4 * count * depth + 2 * depth * width,
            transcendentals=0,
        ),
    )(left, first, other, second)


X_SWAP = [(i, i ^ 1) for i in range(4)]
Y_SWAP = [(i, i ^ 2) for i in range(4)]


def by_tp(value, pairs):
    return lax.ppermute(value, "tp", pairs)


def after(value, *earlier):
    return lax.optimization_barrier((value, *earlier))[0]


def sum_pieces(part_ref, make, half_ref, whole_ref, send_sem, recv_sem, peers, meanwhile):
    half = part_ref.shape[1] // 2
    make(3)
    copies = [
        send(
            part_ref.at[3, pl.ds(axis * half, half)],
            half_ref.at[axis],
            send_sem.at[axis],
            recv_sem.at[axis],
            peers[axis],
        )
        for axis in range(2)
    ]
    for piece in (1, 2, 0):
        make(piece)
    meanwhile(0)
    for copy in copies:
        copy.wait()
    part_ref[2, :half] = (part_ref[2, :half].astype(F32) + half_ref[0].astype(F32)).astype(BF)
    part_ref[1, half:] = (part_ref[1, half:].astype(F32) + half_ref[1].astype(F32)).astype(BF)
    copies = [
        send(
            part_ref.at[1 + axis],
            whole_ref.at[axis],
            send_sem.at[2 + axis],
            recv_sem.at[2 + axis],
            peers[axis],
        )
        for axis in range(2)
    ]
    meanwhile(1)
    for copy in copies:
        copy.wait()
    return part_ref[0].astype(F32) + whole_ref[0].astype(F32) + whole_ref[1].astype(F32)


def gather_pieces(all_ref, send_sem, recv_sem, peers, meanwhile):
    half = all_ref.shape[1] // 2
    copies = [
        send(all_ref.at[0], all_ref.at[1 + axis], send_sem.at[axis], recv_sem.at[axis], peers[axis])
        for axis in range(2)
    ]
    meanwhile(2)
    for copy in copies:
        copy.wait()
    copies = []
    for axis in range(2):
        rows = pl.ds(axis * half, half)
        copies.append(
            send(
                all_ref.at[1 + axis, rows],
                all_ref.at[3, rows],
                send_sem.at[2 + axis],
                recv_sem.at[2 + axis],
                peers[1 - axis],
            )
        )
    meanwhile(3)
    for copy in copies:
        copy.wait()


def idle(stage):
    return None


def row_scale(values):
    return lax.rsqrt(jnp.mean(values * values, axis=-1, keepdims=True) + EPSILON)


def mid_forward_kernel(
    attended_ref, weight_ref, input_ref, gain_ref,
    residual_ref, all_ref,
    part_ref, half_ref, whole_ref, sems,
):
    peers = swap_peers()
    rows = input_ref.shape[0]
    greet(peers)

    def make(piece):
        part_ref[piece] = dot_nt(
            attended_ref[piece * rows : (piece + 1) * rows], weight_ref[...]
        ).astype(BF)

    summed = sum_pieces(part_ref, make, half_ref, whole_ref, sems.at[0], sems.at[1], peers, idle)
    residual = input_ref[...].astype(F32) + summed
    residual_ref[...] = residual
    all_ref[0] = (residual * row_scale(residual) * gain_ref[...].astype(F32)).astype(BF)
    gather_pieces(all_ref, sems.at[2], sems.at[3], peers, idle)


def mid_forward(attended, weight, inputs, gain):
    rows, width = inputs.shape
    return pl.pallas_call(
        mid_forward_kernel,
        name="mid_forward",
        out_shape=(
            jax.ShapeDtypeStruct((rows, width), F32),
            jax.ShapeDtypeStruct((4, rows, width), BF),
        ),
        in_specs=[VMEM] * 4,
        out_specs=(VMEM,) * 2,
        scratch_shapes=[
            pltpu.VMEM((4, rows, width), BF),
            pltpu.VMEM((2, rows // 2, width), BF),
            pltpu.VMEM((2, rows, width), BF),
            pltpu.SemaphoreType.DMA((4, 4)),
        ],
        compiler_params=pltpu.CompilerParams(
            collective_id=1, has_side_effects=True, vmem_limit_bytes=56 << 20
        ),
        cost_estimate=pl.CostEstimate(
            flops=80_000_000_000, bytes_accessed=20_000_000, transcendentals=0
        ),
    )(attended, weight, inputs, gain)


def row_grads(values, gain, back):
    scale = row_scale(values)
    scaled = back * gain
    return scale * scaled - values * (scale * scale * scale) * jnp.mean(
        scaled * values, axis=-1, keepdims=True
    )


def mid_backward_kernel(
    back_ref, residual_ref, cot_ref, gain_ref, slabs_ref,
    out_ref, all_ref, total_ref,
    part_ref, half_ref, whole_ref, sems, load_sem, *hop_refs,
):
    peers = swap_peers()
    hops = Hops(slabs_ref, total_ref, *hop_refs)
    greet(peers + hops.line[1:])
    hops.begin()

    def meanwhile(stage):
        if stage == 1:
            hops.onward()

    order = (3, 1, 2, 0)
    loads = [
        pltpu.make_async_copy(back_ref.at[piece], part_ref.at[piece], load_sem.at[piece])
        for piece in range(4)
    ]
    for piece in order:
        loads[piece].start()
    summed = sum_pieces(
        part_ref, lambda piece: loads[piece].wait(), half_ref, whole_ref,
        sems.at[0], sems.at[1], peers, meanwhile,
    )
    grads = cot_ref[...].astype(F32) + row_grads(
        residual_ref[...], gain_ref[...].astype(F32), summed
    )
    out_ref[...] = grads
    all_ref[0] = grads.astype(BF)
    gather_pieces(all_ref, sems.at[2], sems.at[3], peers, idle)
    hops.finish()


def mid_backward(back, residual, cot, gain, slabs):
    rows, width = residual.shape
    _, height, job_width = slabs.shape
    return pl.pallas_call(
        mid_backward_kernel,
        name="mid_backward",
        out_shape=(
            jax.ShapeDtypeStruct((rows, width), F32),
            jax.ShapeDtypeStruct((4, rows, width), BF),
            jax.ShapeDtypeStruct((height, job_width), F32),
        ),
        in_specs=[
            pl.BlockSpec(memory_space=pl.ANY), VMEM, VMEM, VMEM, pl.BlockSpec(memory_space=pl.ANY)
        ],
        out_specs=(VMEM,) * 3,
        scratch_shapes=[
            pltpu.VMEM((4, rows, width), BF),
            pltpu.VMEM((2, rows // 2, width), BF),
            pltpu.VMEM((2, rows, width), BF),
            pltpu.SemaphoreType.DMA((4, 4)),
            pltpu.SemaphoreType.DMA((4,)),
            *hop_scratch(height, job_width),
        ],
        compiler_params=pltpu.CompilerParams(
            collective_id=2, has_side_effects=True, vmem_limit_bytes=48 << 20
        ),
        cost_estimate=pl.CostEstimate(
            flops=80_000_000_000, bytes_accessed=20_000_000, transcendentals=0
        ),
    )(back.reshape(4, rows, width), residual, cot, gain, slabs)


def end_backward_kernel(
    grads_ref, weight_ref, input_ref, gain_ref, later_ref, residual_ref, rows_ref, slabs_ref,
    out_ref, sum_ref, total_ref,
    part_ref, half_ref, whole_ref, sems, rows_part_ref, rows_half_ref, rows_whole_ref, rows_sems,
    load_sem, *hop_refs,
):
    loads = [
        pltpu.make_async_copy(rows_ref.at[piece], rows_part_ref.at[piece], load_sem.at[piece])
        for piece in range(4)
    ]
    peers = swap_peers()
    rows = input_ref.shape[0]
    hops = Hops(slabs_ref, total_ref, *hop_refs)
    greet(peers + hops.line[1:])
    hops.begin()

    def meanwhile(stage):
        if stage == 0:
            for load in loads:
                load.start()
        if stage == 1:
            hops.onward()

    def make(piece):
        part_ref[piece] = dot_nt(
            grads_ref[piece * rows : (piece + 1) * rows], weight_ref[...]
        ).astype(BF)

    summed = sum_pieces(
        part_ref, make, half_ref, whole_ref, sems.at[0], sems.at[1], peers, meanwhile
    )

    def finish(stage):
        if stage == 0:
            out_ref[...] = later_ref[...] + row_grads(
                input_ref[...].astype(F32), gain_ref[...].astype(F32), summed
            )

    summed_rows = sum_pieces(
        rows_part_ref, lambda piece: loads[piece].wait(), rows_half_ref, rows_whole_ref,
        rows_sems.at[0], rows_sems.at[1], peers, finish,
    )
    sum_ref[...] = (residual_ref[...] + summed_rows).astype(BF)
    hops.finish()


def end_backward(grads, weight, inputs, gain, later, residual, out_part, slabs):
    rows, width = inputs.shape
    _, height, job_width = slabs.shape
    return pl.pallas_call(
        end_backward_kernel,
        name="end_backward",
        out_shape=(
            jax.ShapeDtypeStruct((rows, width), F32),
            jax.ShapeDtypeStruct((rows, width), BF),
            jax.ShapeDtypeStruct((height, job_width), F32),
        ),
        in_specs=[VMEM] * 6 + [pl.BlockSpec(memory_space=pl.ANY)] * 2,
        out_specs=(VMEM,) * 3,
        scratch_shapes=[
            pltpu.VMEM((4, rows, width), BF),
            pltpu.VMEM((2, rows // 2, width), BF),
            pltpu.VMEM((2, rows, width), BF),
            pltpu.SemaphoreType.DMA((2, 4)),
            pltpu.VMEM((4, rows, width), BF),
            pltpu.VMEM((2, rows // 2, width), BF),
            pltpu.VMEM((2, rows, width), BF),
            pltpu.SemaphoreType.DMA((2, 4)),
            pltpu.SemaphoreType.DMA((4,)),
            *hop_scratch(height, job_width),
        ],
        compiler_params=pltpu.CompilerParams(
            collective_id=3, has_side_effects=True, vmem_limit_bytes=48 << 20
        ),
        cost_estimate=pl.CostEstimate(
            flops=40_000_000_000, bytes_accessed=20_000_000, transcendentals=0
        ),
    )(
        grads, weight, inputs, gain, later, residual, out_part.reshape(4, rows, width), slabs
    )


class Line:
    def __init__(self):
        self.rank = lax.axis_index("tp")

    def row_order(self, values):
        count = values.shape[0] // 4
        return jnp.concatenate(
            [lax.dynamic_slice_in_dim(values, (self.rank ^ p) * count, count, 0) for p in range(4)]
        )

    def trunk_base(self):
        return self.rank * TRUNK

    def gather_rows(self, rows):
        half = rows.shape[0] // 2
        beside = by_tp(rows, X_SWAP)
        above = by_tp(rows, Y_SWAP)
        return jnp.concatenate(
            [rows, beside, above, by_tp(beside[:half], Y_SWAP), by_tp(above[half:], X_SWAP)]
        )

    def mid_forward(self, attended, weight, inputs, gain):
        residual, normed = mid_forward(attended, weight, inputs, gain)
        return residual, normed.reshape(-1, normed.shape[-1])

    def mid_backward(self, back, residual, cot, gain, slabs):
        grads, gathered, total = mid_backward(back, residual, cot, gain, slabs)
        return grads, gathered.reshape(-1, gathered.shape[-1]), total

    def chunks(self, rows, cot, blocks):
        (full, at, width), second, third = blocks
        slabs, *sums = chunk_pass(rows, cot, full, at, width, None, False, True, None, (), 4)
        first = slabs
        full, at, width = second
        slabs, *sums, moved = chunk_pass(
            rows, cot, full, at, width, sums, False, True, "far", (first,), 5
        )
        full, at, width = third
        grads, *sums, total = chunk_pass(
            rows, cot, full, at, width, sums, True, False, "near", (first, moved), 6
        )
        return sums, [total, None, grads], slabs

    def end_backward(self, grads, weight, inputs, gain, later, residual, out_part, operands):
        slabs = pair_hops(*operands)
        return end_backward(grads, weight, inputs, gain, later, residual, out_part, slabs)


class Plain:
    def row_order(self, values):
        return values

    def trunk_base(self):
        return jnp.int32(0)

    def gather_rows(self, rows):
        return lax.all_gather(rows, "tp", axis=0, tiled=True)

    def scatter_rows(self, partial):
        return lax.psum_scatter(partial.astype(F32), "tp", scatter_dimension=0, tiled=True)

    def mid_forward(self, attended, weight, inputs, gain):
        residual = inputs.astype(F32) + self.scatter_rows(dot_nt(attended, weight))
        normed = residual * row_scale(residual) * gain.astype(F32)
        normed = self.gather_rows(normed.astype(BF))
        return residual, normed

    def chunks(self, rows, cot, blocks):
        sums = None
        parts = []
        for full, at, width in blocks:
            grads, *sums = chunk_pass(rows, cot, full, at, width, sums, len(parts) == len(blocks) - 1)
            parts.append(scatter_slabs(grads))
        return sums, parts, None

    def mid_backward(self, back, residual, cot, gain, slabs):
        grads = row_grads(residual, gain.astype(F32), self.scatter_rows(back))
        grads = cot.astype(F32) + grads
        return grads, self.gather_rows(grads.astype(BF)), None

    def end_backward(self, grads, weight, inputs, gain, later, residual, out_part, operands):
        output = (residual + self.scatter_rows(out_part)).astype(BF)
        sums = scatter_slabs(pair_grads(*operands))
        back = self.scatter_rows(dot_nt(grads, weight))
        return later + row_grads(inputs.astype(F32), gain.astype(F32), back), output, sums


def gather_slabs(shard):
    return lax.all_gather(shard, "fsdp", axis=0, tiled=True)


def scatter_slabs(grads):
    return lax.psum_scatter(grads, "fsdp", scatter_dimension=0, tiled=True).astype(F32)


def body(
    make_links,
    layer_input,
    cotangent,
    segment_ids,
    path_positions,
    ancestor_masks,
    attn_gain,
    query_weight,
    key_weight,
    value_weight,
    out_weight,
    mlp_gain,
    gate_weight,
    up_weight,
    down_weight,
):
    links = make_links()
    heads = query_weight.shape[1] // HD
    groups = key_weight.shape[1] // HD
    q_width, kv_width = heads * HD, groups * HD
    qkv_width = q_width + 2 * kv_width
    units = gate_weight.shape[1]
    edges = [units * sum(PARTS[:i]) // sum(PARTS) for i in range(len(PARTS) + 1)]

    gain_rows = gather_slabs(jnp.stack([attn_gain, mlp_gain], axis=1))
    first_gain, second_gain = gain_rows[:, 0][None, :], gain_rows[:, 1][None, :]
    own_qkv = jnp.concatenate([query_weight, key_weight, value_weight], axis=1)
    attn_full = gather_slabs(jnp.concatenate([own_qkv, out_weight.T], axis=1))
    out_full = attn_full[:, qkv_width:]
    qkv_full = lax.optimization_barrier(attn_full[:, :qkv_width])
    own_down = down_weight.T
    own_mlp = [
        jnp.concatenate([gate_weight[:, cut], up_weight[:, cut], own_down[:, cut]], axis=1)
        for cut in map(slice, edges[:-1], edges[1:])
    ]
    early = gather_slabs(jnp.concatenate(own_mlp[:2], axis=1))
    mlp_full = [(early, 0), (early, own_mlp[0].shape[1]), (gather_slabs(own_mlp[2]), 0)]

    positions = links.row_order(path_positions)
    angles = positions.astype(F32)[:, None] * jnp.asarray(inverse_freq(HD))[None, :]
    cosine, sine = jnp.cos(angles), jnp.sin(angles)
    cosine = jnp.concatenate([cosine] * 4, axis=1)
    sine = jnp.concatenate([-sine, sine] * 2, axis=1)
    segs = links.row_order(segment_ids)[::SEG]
    masks = ancestor_masks.reshape(SEGS * SEGS)
    base = jnp.reshape(links.trunk_base(), (1,)).astype(jnp.int32)

    inputs = layer_input.astype(F32)
    cot_all = links.gather_rows(cotangent)
    first_rows = (inputs * row_scale(inputs) * first_gain.astype(F32)).astype(BF)
    first_normed = after(links.gather_rows(first_rows), cot_all)

    qkv_pre = dot_nn(first_normed, qkv_full)
    attended, queries, keys, vals = attention_forward(
        heads, groups, masks, segs, base, qkv_pre, cosine, sine
    )
    residual, second_normed = links.mid_forward(
        after(attended, qkv_full), out_full, layer_input, second_gain
    )

    widths = [own.shape[1] for own in own_mlp]
    (back_sum, out_part), mlp_sums, slabs = links.chunks(
        second_normed,
        cot_all,
        [(*pair, width) for pair, width in zip(mlp_full, widths)],
    )
    residual_back, branch_back, total = links.mid_backward(
        back_sum, residual, cotangent, second_gain, slabs
    )
    if total is not None:
        mlp_sums = [mlp_sums[0], total, scatter_slabs(after(mlp_sums[2], branch_back))]
    attended_back = dot_nn(branch_back, out_full).astype(BF)
    qkv_back = attention_backward(
        heads, groups, masks, segs, base, queries, keys, vals, attended_back, cosine, sine
    )
    thirds = [
        [part[:, at * part.shape[1] // 3 : (at + 1) * part.shape[1] // 3] for part in mlp_sums]
        for at in range(3)
    ]
    room = jnp.zeros_like(thirds[0][2])
    gate_sum, up_sum, down_sum = (
        jnp.concatenate([parts[0], parts[1], room], axis=1) for parts in thirds
    )
    down_sum = down_sum.T
    mlp_parts = [
        jnp.sum(
            (own * part)[:, : 2 * own.shape[1] // 3].astype(F32), axis=1
        )
        for own, part in zip([own.astype(F32) for own in own_mlp], mlp_sums)
    ]
    early_part = mlp_parts[0] + mlp_parts[1]
    residual_back, gate_sum, up_sum, down_sum, early_part = lax.optimization_barrier(
        (residual_back, gate_sum, up_sum, down_sum, early_part)
    )
    input_grad, output, attn_sum = links.end_backward(
        qkv_back,
        qkv_full,
        layer_input,
        first_gain,
        residual_back,
        residual,
        out_part,
        (first_normed, qkv_back, branch_back, attended),
    )
    qkv_sum = attn_sum[:, :qkv_width]

    gate_sum = lax.dynamic_update_slice(gate_sum, thirds[0][2], (0, edges[2]))
    up_sum = lax.dynamic_update_slice(up_sum, thirds[1][2], (0, edges[2]))
    down_sum = lax.dynamic_update_slice(down_sum, thirds[2][2].T, (edges[2], 0))
    attn_part = jnp.sum(own_qkv.astype(F32) * qkv_sum, axis=1)
    mlp_part = early_part + mlp_parts[2]
    attn_total, mlp_total = lax.psum((attn_part, mlp_part), "tp")
    return (
        output,
        input_grad,
        attn_total / attn_gain.astype(F32),
        qkv_sum[:, :q_width],
        qkv_sum[:, q_width : q_width + kv_width],
        qkv_sum[:, q_width + kv_width :],
        attn_sum[:, qkv_width:].T,
        mlp_total / mlp_gain.astype(F32),
        gate_sum,
        up_sum,
        down_sum,
    )


def solution(mesh):
    fits = mesh.shape["fsdp"] == 8 and mesh.shape["tp"] == 4
    return jax.shard_map(
        functools.partial(body, Line if fits else Plain),
        mesh=mesh,
        in_specs=(
            P(("fsdp", "tp"), None),
            P(("fsdp", "tp"), None),
            P("fsdp"),
            P("fsdp"),
            P("fsdp", None, None),
            P("fsdp"),
            P("fsdp", "tp"),
            P("fsdp", "tp"),
            P("fsdp", "tp"),
            P("tp", "fsdp"),
            P("fsdp"),
            P("fsdp", "tp"),
            P("fsdp", "tp"),
            P("tp", "fsdp"),
        ),
        out_specs=(
            P(("fsdp", "tp"), None),
            P(("fsdp", "tp"), None),
            P("fsdp"),
            P("fsdp", "tp"),
            P("fsdp", "tp"),
            P("fsdp", "tp"),
            P("tp", "fsdp"),
            P("fsdp"),
            P("fsdp", "tp"),
            P("fsdp", "tp"),
            P("tp", "fsdp"),
        ),
        check_vma=False,
    )
```

```python
import functools
import math

import jax
import jax.numpy as jnp
import numpy as np
from jax import lax
from jax.experimental import pallas as pl
from jax.experimental.pallas import tpu as pltpu
from jax.sharding import PartitionSpec as P

HD = 64
SEGS = 13
SEG = 64
TRUNK = 256
BRANCHES = 4
EPSILON = 1e-05
PARTS = (2, 3, 3)
NEG = -1e30
BF = jnp.bfloat16
F32 = jnp.float32


def inverse_freq(head_size):
    base_freq = 1.0 / 500000.0 ** (np.arange(0, head_size, 2) / head_size)
    wavelen = 2.0 * math.pi / base_freq
    smooth = (8192.0 / wavelen - 1.0) / 3.0
    blended = (1.0 - smooth) * base_freq / 32.0 + smooth * base_freq
    scaled = np.where(
        wavelen > 8192.0, base_freq / 32.0, np.where(wavelen < 2048.0, base_freq, blended)
    )
    return scaled.astype(np.float32)


def dot_nn(left, right):
    return lax.dot_general(
        left, right, (((1,), (0,)), ((), ())), preferred_element_type=F32
    )


def dot_nt(left, right):
    return lax.dot_general(
        left, right, (((1,), (1,)), ((), ())), preferred_element_type=F32
    )


def dot_tn(left, right):
    return lax.dot_general(
        left, right, (((0,), (0,)), ((), ())), preferred_element_type=F32
    )


def rope_lanes(values, cosine, signed_sine, low_half):
    rolled = jnp.where(low_half, pltpu.roll(values, 96, 1), pltpu.roll(values, 32, 1))
    return values * cosine + rolled * signed_sine


def rope_lanes_back(grads, cosine, signed_sine, low_half):
    scaled = grads * signed_sine
    rolled = jnp.where(low_half, pltpu.roll(scaled, 96, 1), pltpu.roll(scaled, 32, 1))
    return grads * cosine + rolled


def low_half_mask(rows):
    lane = lax.broadcasted_iota(jnp.int32, (rows, 128), 1)
    return lax.rem(lane, HD) < HD // 2


def parent_block(mask_ref, seg_ref, segment, block_count):
    parent = jnp.int32(0)
    for branch in range(1, BRANCHES + 1):
        parent = parent + branch * mask_ref[segment * SEGS + branch]
    parent = jnp.where(segment > BRANCHES, parent, segment)
    found = jnp.int32(0)
    for block in range(block_count):
        found = found + block * (seg_ref[block] == parent).astype(jnp.int32)
    return found


def block_mask(has_parent, members):
    shape = (members * SEG, 2 * SEG)
    row = lax.rem(lax.broadcasted_iota(jnp.int32, shape, 0), SEG)
    col = lax.broadcasted_iota(jnp.int32, shape, 1)
    return ((col < SEG) & has_parent) | ((col >= SEG) & (col - SEG <= row))


def trunk_mask(index, members):
    shape = (members * SEG, TRUNK)
    row = lax.rem(lax.broadcasted_iota(jnp.int32, shape, 0), SEG) + index * SEG
    col = lax.broadcasted_iota(jnp.int32, shape, 1)
    return col <= row


def softmax_rows(scores):
    row_max = jnp.max(scores, axis=-1, keepdims=True)
    exponent = jnp.exp(scores - row_max)
    return exponent / jnp.sum(exponent, axis=-1, keepdims=True)


def attn_fwd_kernel(
    heads, groups, mask_ref, seg_ref, base_ref, pre_ref, cos_ref, sin_ref,
    att_ref, q_ref, k_ref, v_ref,
):
    rows = pre_ref.shape[0]
    blocks = rows // SEG
    members = heads // groups
    score_scale = HD ** (-0.5)
    low_half = low_half_mask(rows)
    cosine = cos_ref[...]
    sine = sin_ref[...]
    q_width = heads * HD
    kv_width = groups * HD

    def put_heads(dest, first, wide, count):
        for half in range(count):
            head = first + half
            part = wide[:, half * HD : (half + 1) * HD].reshape(blocks, SEG, HD)
            group, member = head // members, head % members
            dest[group, :, member * SEG : (member + 1) * SEG, :] = part

    for pair in range(q_width // 128):
        lanes = pre_ref[:, pair * 128 : (pair + 1) * 128]
        put_heads(q_ref, 2 * pair, rope_lanes(lanes, cosine, sine, low_half).astype(BF), 2)
    if kv_width % 128 == 0:
        for pair in range(kv_width // 128):
            at = q_width + pair * 128
            wide = rope_lanes(pre_ref[:, at : at + 128], cosine, sine, low_half).astype(BF)
            at = q_width + kv_width + pair * 128
            plain = pre_ref[:, at : at + 128].astype(BF)
            for half in range(2):
                k_ref[2 * pair + half] = wide[:, half * HD : (half + 1) * HD]
                v_ref[2 * pair + half] = plain[:, half * HD : (half + 1) * HD]
    else:
        both = pre_ref[:, q_width : q_width + 128]
        k_ref[0] = rope_lanes(both, cosine, sine, low_half).astype(BF)[:, :HD]
        v_ref[0] = both.astype(BF)[:, HD:]

    base = base_ref[0]
    trunk_block = base // SEG
    trunk_rows = pl.ds(pl.multiple_of(base, TRUNK), TRUNK)

    def store(group, block, mixed):
        at = pl.ds(pl.multiple_of(block * SEG, SEG), SEG)
        for member in range(members):
            head = group * members + member
            att_ref[at, head * HD : (head + 1) * HD] = mixed[
                member * SEG : (member + 1) * SEG
            ].astype(BF)

    for group in range(groups):
        def one_block(block, carry):
            inside = block - trunk_block
            is_trunk = (inside >= 0) & (inside < TRUNK // SEG)

            @pl.when(is_trunk)
            def _():
                queries = q_ref[group, block]
                scores = dot_nt(queries, k_ref[group, trunk_rows, :]) * score_scale
                scores = jnp.where(trunk_mask(inside, members), scores, NEG)
                probs = softmax_rows(scores).astype(BF)
                store(group, block, dot_nn(probs, v_ref[group, trunk_rows, :]))

            @pl.when(jnp.logical_not(is_trunk))
            def _():
                segment = seg_ref[block]
                parent = parent_block(mask_ref, seg_ref, segment, blocks)
                up = pl.ds(pl.multiple_of(parent * SEG, SEG), SEG)
                own = pl.ds(pl.multiple_of(block * SEG, SEG), SEG)
                queries = q_ref[group, block]
                keys = jnp.concatenate(
                    [k_ref[group, trunk_rows, :], k_ref[group, up, :], k_ref[group, own, :]], axis=0
                )
                vals = jnp.concatenate(
                    [v_ref[group, trunk_rows, :], v_ref[group, up, :], v_ref[group, own, :]], axis=0
                )
                scores = dot_nt(queries, keys) * score_scale
                tail = jnp.where(
                    block_mask(segment > BRANCHES, members), scores[:, TRUNK:], NEG
                )
                scores = jnp.concatenate([scores[:, :TRUNK], tail], axis=1)
                probs = softmax_rows(scores).astype(BF)
                store(group, block, dot_nn(probs, vals))

            return carry

        lax.fori_loop(0, blocks, one_block, 0)


def attn_bwd_kernel(
    heads, groups, mask_ref, seg_ref, base_ref, q_ref, k_ref, v_ref, grad_ref, cos_ref, sin_ref,
    out_ref, g_ref, dq_ref, dk_ref, dv_ref,
):
    rows = grad_ref.shape[0]
    blocks = rows // SEG
    members = heads // groups
    score_scale = HD ** (-0.5)
    low_half = low_half_mask(rows)
    cosine = cos_ref[...]
    sine = sin_ref[...]
    q_width = heads * HD
    kv_width = groups * HD
    for head in range(heads):
        part = grad_ref[:, head * HD : (head + 1) * HD].reshape(blocks, SEG, HD)
        group, member = head // members, head % members
        g_ref[group, :, member * SEG : (member + 1) * SEG, :] = part
    dk_ref[...] = jnp.zeros_like(dk_ref)
    dv_ref[...] = jnp.zeros_like(dv_ref)
    base = base_ref[0]
    trunk_block = base // SEG
    trunk_rows = pl.ds(pl.multiple_of(base, TRUNK), TRUNK)

    def store(group, block, d_query):
        at = pl.ds(pl.multiple_of(block * SEG, SEG), SEG)
        for member in range(members):
            head = group * members + member
            dq_ref[at, head * HD : (head + 1) * HD] = d_query[member * SEG : (member + 1) * SEG]

    for group in range(groups):
        lanes = slice(group * HD, (group + 1) * HD)

        def grads(queries, out_grads, keys, vals, scores):
            probs = softmax_rows(scores)
            prob_back = dot_nt(out_grads, vals)
            delta = jnp.sum(probs * prob_back, axis=-1, keepdims=True)
            score_back = (probs * (prob_back - delta)).astype(BF)
            d_query = dot_nn(score_back, keys) * score_scale
            d_key = dot_tn(score_back, queries) * score_scale
            d_val = dot_tn(probs.astype(BF), out_grads)
            return d_query, d_key, d_val

        def one_block(block, carry):
            inside = block - trunk_block
            is_trunk = (inside >= 0) & (inside < TRUNK // SEG)

            @pl.when(is_trunk)
            def _():
                queries = q_ref[group, block]
                keys = k_ref[group, trunk_rows, :]
                scores = dot_nt(queries, keys) * score_scale
                scores = jnp.where(trunk_mask(inside, members), scores, NEG)
                d_query, d_key, d_val = grads(
                    queries, g_ref[group, block], keys, v_ref[group, trunk_rows, :], scores
                )
                store(group, block, d_query)
                dk_ref[trunk_rows, lanes] += d_key
                dv_ref[trunk_rows, lanes] += d_val

            @pl.when(jnp.logical_not(is_trunk))
            def _():
                segment = seg_ref[block]
                parent = parent_block(mask_ref, seg_ref, segment, blocks)
                up = pl.ds(pl.multiple_of(parent * SEG, SEG), SEG)
                own = pl.ds(pl.multiple_of(block * SEG, SEG), SEG)
                queries = q_ref[group, block]
                keys = jnp.concatenate(
                    [k_ref[group, trunk_rows, :], k_ref[group, up, :], k_ref[group, own, :]], axis=0
                )
                vals = jnp.concatenate(
                    [v_ref[group, trunk_rows, :], v_ref[group, up, :], v_ref[group, own, :]], axis=0
                )
                scores = dot_nt(queries, keys) * score_scale
                tail = jnp.where(
                    block_mask(segment > BRANCHES, members), scores[:, TRUNK:], NEG
                )
                scores = jnp.concatenate([scores[:, :TRUNK], tail], axis=1)
                d_query, d_key, d_val = grads(queries, g_ref[group, block], keys, vals, scores)
                store(group, block, d_query)
                for ref, val in ((dk_ref, d_key), (dv_ref, d_val)):
                    ref[trunk_rows, lanes] += val[:TRUNK]
                    ref[up, lanes] += val[TRUNK : TRUNK + SEG]
                    ref[own, lanes] += val[TRUNK + SEG :]

            return carry

        lax.fori_loop(0, blocks, one_block, 0)
    for pair in range(q_width // 128):
        at = slice(pair * 128, (pair + 1) * 128)
        out_ref[:, at] = rope_lanes_back(dq_ref[:, at], cosine, sine, low_half).astype(BF)
    if kv_width % 128 == 0:
        for pair in range(kv_width // 128):
            at = slice(pair * 128, (pair + 1) * 128)
            turned = rope_lanes_back(dk_ref[:, at], cosine, sine, low_half)
            out_ref[:, q_width + pair * 128 : q_width + (pair + 1) * 128] = turned.astype(BF)
            first = q_width + kv_width + pair * 128
            out_ref[:, first : first + 128] = dv_ref[:, at].astype(BF)
    else:
        wide = jnp.concatenate([dk_ref[...], dv_ref[...]], axis=1)
        turned = rope_lanes_back(wide, cosine, sine, low_half)
        lane = lax.broadcasted_iota(jnp.int32, (rows, 128), 1)
        out_ref[:, q_width : q_width + 128] = jnp.where(lane < HD, turned, wide).astype(BF)


LIGHT = pl.CostEstimate(flops=1000, bytes_accessed=1000, transcendentals=0)
SMEM = pl.BlockSpec(memory_space=pltpu.SMEM)
VMEM = pl.BlockSpec(memory_space=pltpu.VMEM)


def loaded(value):
    return pl.BlockSpec(
        value.shape, lambda i: (0,) * value.ndim, pipeline_mode=pl.Buffered(1)
    )


def attention_forward(heads, groups, masks, segs, base, pre, cosine, sine):
    rows = pre.shape[0]
    members = heads // groups
    blocks = rows // SEG
    return pl.pallas_call(
        functools.partial(attn_fwd_kernel, heads, groups),
        name="attn_fwd",
        out_shape=(
            jax.ShapeDtypeStruct((rows, heads * HD), BF),
            jax.ShapeDtypeStruct((groups, blocks, members * SEG, HD), BF),
            jax.ShapeDtypeStruct((groups, rows, HD), BF),
            jax.ShapeDtypeStruct((groups, rows, HD), BF),
        ),
        in_specs=[SMEM, SMEM, SMEM, VMEM, VMEM, VMEM],
        out_specs=(VMEM, VMEM, VMEM, VMEM),
        compiler_params=pltpu.CompilerParams(vmem_limit_bytes=40 << 20),
        cost_estimate=LIGHT,
    )(masks, segs, base, pre, cosine, sine)


def attention_backward(heads, groups, masks, segs, base, queries, keys, vals, grads, cosine, sine):
    rows = grads.shape[0]
    members = heads // groups
    blocks = rows // SEG
    return pl.pallas_call(
        functools.partial(attn_bwd_kernel, heads, groups),
        name="attn_bwd",
        out_shape=jax.ShapeDtypeStruct((rows, (heads + 2 * groups) * HD), BF),
        grid=(1,),
        in_specs=[SMEM, SMEM, SMEM]
        + [loaded(value) for value in (queries, keys, vals, grads, cosine, sine)],
        out_specs=VMEM,
        scratch_shapes=[
            pltpu.VMEM((groups, blocks, members * SEG, HD), BF),
            pltpu.VMEM((rows, heads * HD), F32),
            pltpu.VMEM((rows, groups * HD), F32),
            pltpu.VMEM((rows, groups * HD), F32),
        ],
        compiler_params=pltpu.CompilerParams(vmem_limit_bytes=40 << 20),
        cost_estimate=LIGHT,
    )(masks, segs, base, queries, keys, vals, grads, cosine, sine)


MESH = pl.DeviceIdType.MESH


def swap_peers():
    rank = lax.axis_index("tp")
    place = lax.axis_index("fsdp")
    return [(place, rank + 1 - 2 * (rank % 2)), (place, (rank + 2) % 4)]


def greet(peers):
    barrier = pltpu.get_barrier_semaphore()
    for peer in peers:
        pl.semaphore_signal(barrier, inc=1, device_id=peer, device_id_type=MESH)
    pl.semaphore_wait(barrier, len(peers))


def send(source, target, send_sem, recv_sem, peer):
    copy = pltpu.make_async_remote_copy(
        src_ref=source,
        dst_ref=target,
        send_sem=send_sem,
        recv_sem=recv_sem,
        device_id=peer,
        device_id_type=MESH,
    )
    copy.start()
    return copy


def line_peers():
    place = lax.axis_index("fsdp")
    rank = lax.axis_index("tp")
    z, core = place // 2, place % 2
    up, down = (z + 1) % 4, (z + 3) % 4
    return z, core, [(2 * z + 1 - core, rank), (2 * up + core, rank), (2 * down + core, rank)]


def far_copies(far_ref, far_recv, send_sem, recv_sem, z, peers):
    heading = z // 2
    place = lax.axis_index("fsdp")
    target = (place + 2 - 4 * heading, lax.axis_index("tp"))
    return pltpu.make_async_remote_copy(
        src_ref=far_ref,
        dst_ref=far_recv.at[heading],
        send_sem=send_sem,
        recv_sem=recv_sem.at[heading],
        device_id=target,
        device_id_type=MESH,
    )


def far_add(pair_ref, far_recv, recv_sem, z, peers):
    @pl.when((z == 1) | (z == 2))
    def _():
        for heading in range(2):
            pltpu.make_async_remote_copy(
                src_ref=far_recv.at[heading],
                dst_ref=far_recv.at[heading],
                send_sem=recv_sem.at[heading],
                recv_sem=recv_sem.at[heading],
                device_id=peers[0],
                device_id_type=MESH,
            ).wait_recv()
        pair_ref[0] = (pair_ref[0].astype(F32) + far_recv[1].astype(F32)).astype(BF)
        pair_ref[1] = (pair_ref[1].astype(F32) + far_recv[0].astype(F32)).astype(BF)


def near_copies(pair_ref, near_recv, send_sem, recv_sem, peers):
    return [
        pltpu.make_async_remote_copy(
            src_ref=pair_ref.at[at],
            dst_ref=near_recv.at[at],
            send_sem=send_sem.at[at],
            recv_sem=recv_sem.at[at],
            device_id=peers[2 - at],
            device_id_type=MESH,
        )
        for at in range(2)
    ]


class Hops:
    def __init__(self, slabs_ref, total_ref, pair_ref, slab_ref, far_recv, near_recv, sends, recvs, loads):
        self.z, _, self.line = line_peers()
        self.total_ref, self.pair_ref, self.slab_ref = total_ref, pair_ref, slab_ref
        self.far_recv, self.near_recv, self.recvs = far_recv, near_recv, recvs
        self.far = far_copies(
            slabs_ref.at[0], far_recv, sends.at[0, 0], recvs.at[0], self.z, self.line
        )
        self.loads = [
            pltpu.make_async_copy(slabs_ref.at[1 + at], pair_ref.at[at], loads.at[at])
            for at in range(2)
        ] + [pltpu.make_async_copy(slabs_ref.at[3], slab_ref, loads.at[2])]
        self.near = near_copies(pair_ref, near_recv, sends.at[1], recvs.at[1], self.line)

    def begin(self):
        self.far.start()
        for load in self.loads:
            load.start()

    def onward(self):
        for load in self.loads:
            load.wait()
        self.far.wait_send()
        far_add(self.pair_ref, self.far_recv, self.recvs.at[0], self.z, self.line)
        for copy in self.near:
            copy.start()

    def finish(self):
        for copy in self.near:
            copy.wait()
        self.total_ref[...] = (
            self.slab_ref[...].astype(F32)
            + self.near_recv[0].astype(F32)
            + self.near_recv[1].astype(F32)
        )


def hop_scratch(height, width):
    return [
        pltpu.VMEM((2, height, width), BF),
        pltpu.VMEM((height, width), BF),
        pltpu.VMEM((2, height, width), BF),
        pltpu.VMEM((2, height, width), BF),
        pltpu.SemaphoreType.DMA((2, 2)),
        pltpu.SemaphoreType.DMA((2, 2)),
        pltpu.SemaphoreType.DMA((3,)),
    ]


SLOTS = (2, 1, 3, 0)


def chunk_kernel(cfg, *refs):
    steps, slabs, first, last, cores, job, offset = cfg
    refs = list(refs)
    take = lambda count: [refs.pop(0) for _ in range(count)]
    rows_ref, cot_ref, source_ref = take(3)
    if not first:
        back_in_ref, out_in_ref = take(2)
    if job:
        (slabs_ref,) = take(1)
    grad_ref, back_ref, out_ref = take(3)
    if job:
        (total_ref,) = take(1)
    pair_ref, hidden_ref, full_ref, full_sem = take(4)
    if cores:
        mine_ref, theirs_ref, core_send, core_recv = take(4)
    if job:
        hops = Hops(slabs_ref, total_ref, *take(7))

    step = pl.program_id(0)
    end = steps + slabs - 1
    chunk = hidden_ref.shape[1]
    tile = chunk // steps
    height = rows_ref.shape[1] // slabs
    fetches = [
        pltpu.make_async_copy(
            source_ref.at[:, pl.ds(offset + third * chunk, chunk)],
            full_ref.at[:, pl.ds(third * chunk, chunk)],
            full_sem.at[third],
        )
        for third in range(3)
    ]

    @pl.when(step == 0)
    def _():
        for fetch in fetches:
            fetch.start()

    def fetched(at, third):
        if at == 0:
            fetches[third].wait()

    if cores or job:
        z, core, peers = line_peers()

        @pl.when(step == 0)
        def _():
            greet(peers)
            if job:
                hops.begin()

    if job:

        @pl.when(step == steps + 1)
        def _():
            hops.onward()

    for at in range(steps):

        @pl.when(step == at)
        def _():
            cut = slice(at * tile, (at + 1) * tile)
            fetched(at, 0)
            gate = dot_nn(rows_ref[...], full_ref[:, cut])
            fetched(at, 1)
            up = dot_nn(rows_ref[...], full_ref[:, chunk + at * tile : chunk + (at + 1) * tile])
            fetched(at, 2)
            back = dot_nn(
                cot_ref[...], full_ref[:, 2 * chunk + at * tile : 2 * chunk + (at + 1) * tile]
            )
            sigmoid = 1.0 / (1.0 + jnp.exp(-gate))
            silu = gate * sigmoid
            hidden_ref[:, cut] = (silu * up).astype(BF)
            pair_ref[:, cut] = (back * up * sigmoid * (1.0 + gate * (1.0 - sigmoid))).astype(BF)
            pair_ref[:, chunk + at * tile : chunk + (at + 1) * tile] = (back * silu).astype(BF)

    def write(slab, target_ref, added_ref):
        at = pl.ds(pl.multiple_of(slab * height, height), height)
        grad = dot_tn(rows_ref[:, at], pair_ref[...])
        more = dot_tn(cot_ref[:, at], hidden_ref[...])
        if added_ref is not None:
            grad = grad.astype(BF).astype(F32) + added_ref[:, : 2 * chunk].astype(F32)
            more = more.astype(BF).astype(F32) + added_ref[:, 2 * chunk :].astype(F32)
        target_ref[:, : 2 * chunk] = grad.astype(BF)
        target_ref[:, 2 * chunk :] = more.astype(BF)

    @pl.when(step >= steps)
    def _():
        slab = pl.ds(pl.multiple_of((step - steps) * height, height), height)
        back = dot_nt(pair_ref[...], full_ref[slab, : 2 * chunk])
        out = dot_nt(hidden_ref[...], full_ref[slab, 2 * chunk :])
        back = back if first else back_in_ref[...] + back
        out = out if first else out_in_ref[...] + out
        back_ref[...] = back.astype(back_ref.dtype)
        out_ref[...] = out.astype(out_ref.dtype)
        if not cores:
            write(step - steps, grad_ref, None)

    if cores:
        copies = [
            pltpu.make_async_remote_copy(
                src_ref=mine_ref.at[at % 2],
                dst_ref=theirs_ref.at[at],
                send_sem=core_send.at[at],
                recv_sem=core_recv.at[at],
                device_id=peers[0],
                device_id_type=MESH,
            )
            for at in range(4)
        ]
        for at, slot in enumerate(SLOTS):
            chip = (z + 4 - slot) % 4

            @pl.when(step == steps + at)
            def _():
                if at >= 2:
                    copies[at - 2].wait_send()
                write(2 * chip + 1 - core, mine_ref.at[at % 2], None)
                copies[at].start()

            @pl.when(step == steps + 4 + at)
            def _():
                copies[at].wait_recv()
                write(2 * chip + core, grad_ref.at[0], theirs_ref.at[at])

        @pl.when(step == end)
        def _():
            copies[2].wait_send()
            copies[3].wait_send()

    if job:

        @pl.when(step == end)
        def _():
            hops.finish()


def chunk_pass(rows, cot, full, at, width, sums, last, cores=False, job=False, operands=(), number=None):
    count, depth = rows.shape
    chunk = width // 3
    slabs = 8
    height = depth // slabs
    steps = max(1, chunk // 256)
    first = sums is None
    whole = pl.BlockSpec(memory_space=pltpu.VMEM)
    anywhere = pl.BlockSpec(memory_space=pl.ANY)

    def place(i):
        return jnp.maximum(i - steps, 0)

    column = pl.BlockSpec((count, height), lambda i: (0, place(i)))
    total = jax.ShapeDtypeStruct((count, depth), BF if last else F32)
    if cores:
        grad_shape = jax.ShapeDtypeStruct((4, height, width), BF)
        grad_spec = pl.BlockSpec((1, height, width), lambda i: (jnp.maximum(place(i) - 4, 0), 0, 0))
    else:
        grad_shape = jax.ShapeDtypeStruct((depth, width), BF)
        grad_spec = pl.BlockSpec((height, width), lambda i: (place(i), 0))
    out_shapes, out_specs = [grad_shape, total, total], [grad_spec, column, column]
    in_specs = [whole, whole, anywhere] + ([] if first else [column, column])
    dma = pltpu.SemaphoreType.DMA
    scratch = [
        pltpu.VMEM((count, 2 * chunk), BF),
        pltpu.VMEM((count, chunk), BF),
        pltpu.VMEM((depth, width), BF),
        dma((3,)),
    ]
    if cores:
        scratch += [
            pltpu.VMEM((2, height, width), BF),
            pltpu.VMEM((4, height, width), BF),
            dma((4,)),
            dma((4,)),
        ]
    if job:
        job_width = operands[0].shape[-1]
        in_specs += [anywhere]
        out_shapes += [jax.ShapeDtypeStruct((height, job_width), F32)]
        out_specs += [whole]
        scratch += hop_scratch(height, job_width)
    remote = cores or job
    return pl.pallas_call(
        functools.partial(chunk_kernel, (steps, slabs, first, last, cores, job, at)),
        name="chunk_pass",
        out_shape=tuple(out_shapes),
        grid=(steps + slabs,),
        in_specs=in_specs,
        out_specs=tuple(out_specs),
        scratch_shapes=scratch,
        input_output_aliases={} if first or last else {3: 1, 4: 2},
        compiler_params=pltpu.CompilerParams(
            vmem_limit_bytes=60 << 20,
            collective_id=number if remote else None,
            has_side_effects=bool(remote),
        ),
        cost_estimate=pl.CostEstimate(
            flops=6 * count * depth * width,
            bytes_accessed=8 * count * depth + 4 * depth * width + 16 * count * depth,
            transcendentals=count * chunk,
        ),
    )(rows, cot, full, *(() if first else sums), *operands)


def pair_kernel(left_ref, first_ref, other_ref, second_ref, out_ref):
    width = first_ref.shape[1]
    out_ref[:, :width] = dot_tn(left_ref[...], first_ref[...]).astype(BF)
    out_ref[:, width:] = dot_tn(other_ref[...], second_ref[...]).astype(BF)


def pair_grads(left, first, other, second):
    count, depth = left.shape
    width = first.shape[1] + second.shape[1]
    height = 256
    whole = pl.BlockSpec(memory_space=pltpu.VMEM)
    column = pl.BlockSpec((count, height), lambda i: (0, i))
    return pl.pallas_call(
        pair_kernel,
        name="pair_grads",
        out_shape=jax.ShapeDtypeStruct((depth, width), BF),
        grid=(depth // height,),
        in_specs=[column, whole, column, whole],
        out_specs=pl.BlockSpec((height, width), lambda i: (i, 0)),
        compiler_params=pltpu.CompilerParams(vmem_limit_bytes=32 << 20),
        cost_estimate=LIGHT,
    )(left, first, other, second)


def pair_hops_kernel(
    left_ref, first_ref, other_ref, second_ref, out_ref, mine_ref, theirs_ref, core_send, core_recv
):
    step = pl.program_id(0)
    z, core, peers = line_peers()
    width = first_ref.shape[1]
    height = out_ref.shape[1]

    def write(slab, target_ref, added_ref):
        at = pl.ds(pl.multiple_of(slab * height, height), height)
        grad = dot_tn(left_ref[:, at], first_ref[...])
        more = dot_tn(other_ref[:, at], second_ref[...])
        if added_ref is not None:
            grad = grad.astype(BF).astype(F32) + added_ref[:, :width].astype(F32)
            more = more.astype(BF).astype(F32) + added_ref[:, width:].astype(F32)
        target_ref[:, :width] = grad.astype(BF)
        target_ref[:, width:] = more.astype(BF)

    @pl.when(step == 0)
    def _():
        greet(peers[:1])

    copies = [
        pltpu.make_async_remote_copy(
            src_ref=mine_ref.at[at],
            dst_ref=theirs_ref.at[at],
            send_sem=core_send.at[at],
            recv_sem=core_recv.at[at],
            device_id=peers[0],
            device_id_type=MESH,
        )
        for at in range(4)
    ]
    for at, slot in enumerate(SLOTS):
        chip = (z + 4 - slot) % 4

        @pl.when(step == at)
        def _():
            write(2 * chip + 1 - core, mine_ref.at[at], None)
            copies[at].start()

        @pl.when(step == 4 + at)
        def _():
            copies[at].wait_recv()
            write(2 * chip + core, out_ref.at[0], theirs_ref.at[at])

    @pl.when(step == 7)
    def _():
        for copy in copies:
            copy.wait_send()


def pair_hops(left, first, other, second):
    count, depth = left.shape
    width = first.shape[1] + second.shape[1]
    height = depth // 8
    return pl.pallas_call(
        pair_hops_kernel,
        name="pair_hops",
        out_shape=jax.ShapeDtypeStruct((4, height, width), BF),
        grid=(8,),
        in_specs=[VMEM] * 4,
        out_specs=pl.BlockSpec((1, height, width), lambda i: (jnp.maximum(i - 4, 0), 0, 0)),
        scratch_shapes=[
            pltpu.VMEM((4, height, width), BF),
            pltpu.VMEM((4, height, width), BF),
            pltpu.SemaphoreType.DMA((4,)),
            pltpu.SemaphoreType.DMA((4,)),
        ],
        compiler_params=pltpu.CompilerParams(
            collective_id=7, has_side_effects=True, vmem_limit_bytes=48 << 20
        ),
        cost_estimate=pl.CostEstimate(
            flops=2 * count * depth * width,
            bytes_accessed=4 * count * depth + 2 * depth * width,
            transcendentals=0,
        ),
    )(left, first, other, second)


X_SWAP = [(i, i ^ 1) for i in range(4)]
Y_SWAP = [(i, i ^ 2) for i in range(4)]


def by_tp(value, pairs):
    return lax.ppermute(value, "tp", pairs)


def after(value, *earlier):
    return lax.optimization_barrier((value, *earlier))[0]


def sum_pieces(part_ref, make, half_ref, whole_ref, send_sem, recv_sem, peers, meanwhile):
    half = part_ref.shape[1] // 2
    make(3)
    copies = [
        send(
            part_ref.at[3, pl.ds(axis * half, half)],
            half_ref.at[axis],
            send_sem.at[axis],
            recv_sem.at[axis],
            peers[axis],
        )
        for axis in range(2)
    ]
    for piece in (1, 2, 0):
        make(piece)
    meanwhile(0)
    for copy in copies:
        copy.wait()
    part_ref[2, :half] = (part_ref[2, :half].astype(F32) + half_ref[0].astype(F32)).astype(BF)
    part_ref[1, half:] = (part_ref[1, half:].astype(F32) + half_ref[1].astype(F32)).astype(BF)
    copies = [
        send(
            part_ref.at[1 + axis],
            whole_ref.at[axis],
            send_sem.at[2 + axis],
            recv_sem.at[2 + axis],
            peers[axis],
        )
        for axis in range(2)
    ]
    meanwhile(1)
    for copy in copies:
        copy.wait()
    return part_ref[0].astype(F32) + whole_ref[0].astype(F32) + whole_ref[1].astype(F32)


def gather_pieces(all_ref, send_sem, recv_sem, peers, meanwhile):
    half = all_ref.shape[1] // 2
    copies = [
        send(all_ref.at[0], all_ref.at[1 + axis], send_sem.at[axis], recv_sem.at[axis], peers[axis])
        for axis in range(2)
    ]
    meanwhile(2)
    for copy in copies:
        copy.wait()
    copies = []
    for axis in range(2):
        rows = pl.ds(axis * half, half)
        copies.append(
            send(
                all_ref.at[1 + axis, rows],
                all_ref.at[3, rows],
                send_sem.at[2 + axis],
                recv_sem.at[2 + axis],
                peers[1 - axis],
            )
        )
    meanwhile(3)
    for copy in copies:
        copy.wait()


def idle(stage):
    return None


def row_scale(values):
    return lax.rsqrt(jnp.mean(values * values, axis=-1, keepdims=True) + EPSILON)


def mid_forward_kernel(
    attended_ref, weight_ref, input_ref, gain_ref,
    residual_ref, all_ref,
    part_ref, half_ref, whole_ref, sems,
):
    peers = swap_peers()
    rows = input_ref.shape[0]
    greet(peers)

    def make(piece):
        part_ref[piece] = dot_nt(
            attended_ref[piece * rows : (piece + 1) * rows], weight_ref[...]
        ).astype(BF)

    summed = sum_pieces(part_ref, make, half_ref, whole_ref, sems.at[0], sems.at[1], peers, idle)
    residual = input_ref[...].astype(F32) + summed
    residual_ref[...] = residual
    all_ref[0] = (residual * row_scale(residual) * gain_ref[...].astype(F32)).astype(BF)
    gather_pieces(all_ref, sems.at[2], sems.at[3], peers, idle)


def mid_forward(attended, weight, inputs, gain):
    rows, width = inputs.shape
    return pl.pallas_call(
        mid_forward_kernel,
        name="mid_forward",
        out_shape=(
            jax.ShapeDtypeStruct((rows, width), F32),
            jax.ShapeDtypeStruct((4, rows, width), BF),
        ),
        in_specs=[VMEM] * 4,
        out_specs=(VMEM,) * 2,
        scratch_shapes=[
            pltpu.VMEM((4, rows, width), BF),
            pltpu.VMEM((2, rows // 2, width), BF),
            pltpu.VMEM((2, rows, width), BF),
            pltpu.SemaphoreType.DMA((4, 4)),
        ],
        compiler_params=pltpu.CompilerParams(
            collective_id=1, has_side_effects=True, vmem_limit_bytes=56 << 20
        ),
        cost_estimate=pl.CostEstimate(
            flops=80_000_000_000, bytes_accessed=20_000_000, transcendentals=0
        ),
    )(attended, weight, inputs, gain)


def row_grads(values, gain, back):
    scale = row_scale(values)
    scaled = back * gain
    return scale * scaled - values * (scale * scale * scale) * jnp.mean(
        scaled * values, axis=-1, keepdims=True
    )


def mid_backward_kernel(
    back_ref, residual_ref, cot_ref, gain_ref, weight_ref, slabs_ref,
    out_ref, all_ref, attended_ref, total_ref,
    part_ref, half_ref, whole_ref, sems, load_sem, *hop_refs,
):
    peers = swap_peers()
    hops = Hops(slabs_ref, total_ref, *hop_refs)
    greet(peers + hops.line[1:])
    hops.begin()

    rows = residual_ref.shape[0]

    def project(piece):
        attended_ref[piece * rows : (piece + 1) * rows] = dot_nn(
            all_ref[piece], weight_ref[...]
        ).astype(BF)

    def meanwhile(stage):
        if stage == 1:
            hops.onward()
        if stage == 2:
            project(0)
        if stage == 3:
            project(1)
            project(2)

    order = (3, 1, 2, 0)
    loads = [
        pltpu.make_async_copy(back_ref.at[piece], part_ref.at[piece], load_sem.at[piece])
        for piece in range(4)
    ]
    for piece in order:
        loads[piece].start()
    summed = sum_pieces(
        part_ref, lambda piece: loads[piece].wait(), half_ref, whole_ref,
        sems.at[0], sems.at[1], peers, meanwhile,
    )
    grads = cot_ref[...].astype(F32) + row_grads(
        residual_ref[...], gain_ref[...].astype(F32), summed
    )
    out_ref[...] = grads
    all_ref[0] = grads.astype(BF)
    gather_pieces(all_ref, sems.at[2], sems.at[3], peers, meanwhile)
    project(3)
    hops.finish()


def mid_backward(back, residual, cot, gain, weight, slabs):
    rows, width = residual.shape
    _, height, job_width = slabs.shape
    return pl.pallas_call(
        mid_backward_kernel,
        name="mid_backward",
        out_shape=(
            jax.ShapeDtypeStruct((rows, width), F32),
            jax.ShapeDtypeStruct((4, rows, width), BF),
            jax.ShapeDtypeStruct((4 * rows, weight.shape[1]), BF),
            jax.ShapeDtypeStruct((height, job_width), F32),
        ),
        in_specs=[
            pl.BlockSpec(memory_space=pl.ANY),
            VMEM,
            VMEM,
            VMEM,
            VMEM,
            pl.BlockSpec(memory_space=pl.ANY),
        ],
        out_specs=(VMEM,) * 4,
        scratch_shapes=[
            pltpu.VMEM((4, rows, width), BF),
            pltpu.VMEM((2, rows // 2, width), BF),
            pltpu.VMEM((2, rows, width), BF),
            pltpu.SemaphoreType.DMA((4, 4)),
            pltpu.SemaphoreType.DMA((4,)),
            *hop_scratch(height, job_width),
        ],
        compiler_params=pltpu.CompilerParams(
            collective_id=2, has_side_effects=True, vmem_limit_bytes=36 << 20
        ),
        cost_estimate=pl.CostEstimate(
            flops=80_000_000_000, bytes_accessed=20_000_000, transcendentals=0
        ),
    )(back.reshape(4, rows, width), residual, cot, gain, weight, slabs)


def end_backward_kernel(
    grads_ref, weight_ref, input_ref, gain_ref, later_ref, residual_ref, rows_ref, slabs_ref,
    out_ref, sum_ref, total_ref,
    part_ref, half_ref, whole_ref, sems, rows_part_ref, rows_half_ref, rows_whole_ref, rows_sems,
    load_sem, *hop_refs,
):
    loads = [
        pltpu.make_async_copy(rows_ref.at[piece], rows_part_ref.at[piece], load_sem.at[piece])
        for piece in range(4)
    ]
    peers = swap_peers()
    rows = input_ref.shape[0]
    hops = Hops(slabs_ref, total_ref, *hop_refs)
    greet(peers + hops.line[1:])
    hops.begin()

    def meanwhile(stage):
        if stage == 0:
            for load in loads:
                load.start()
        if stage == 1:
            hops.onward()

    def make(piece):
        part_ref[piece] = dot_nt(
            grads_ref[piece * rows : (piece + 1) * rows], weight_ref[...]
        ).astype(BF)

    summed = sum_pieces(
        part_ref, make, half_ref, whole_ref, sems.at[0], sems.at[1], peers, meanwhile
    )

    def finish(stage):
        if stage == 0:
            out_ref[...] = later_ref[...] + row_grads(
                input_ref[...].astype(F32), gain_ref[...].astype(F32), summed
            )

    summed_rows = sum_pieces(
        rows_part_ref, lambda piece: loads[piece].wait(), rows_half_ref, rows_whole_ref,
        rows_sems.at[0], rows_sems.at[1], peers, finish,
    )
    sum_ref[...] = (residual_ref[...] + summed_rows).astype(BF)
    hops.finish()


def end_backward(grads, weight, inputs, gain, later, residual, out_part, slabs):
    rows, width = inputs.shape
    _, height, job_width = slabs.shape
    return pl.pallas_call(
        end_backward_kernel,
        name="end_backward",
        out_shape=(
            jax.ShapeDtypeStruct((rows, width), F32),
            jax.ShapeDtypeStruct((rows, width), BF),
            jax.ShapeDtypeStruct((height, job_width), F32),
        ),
        in_specs=[VMEM] * 6 + [pl.BlockSpec(memory_space=pl.ANY)] * 2,
        out_specs=(VMEM,) * 3,
        scratch_shapes=[
            pltpu.VMEM((4, rows, width), BF),
            pltpu.VMEM((2, rows // 2, width), BF),
            pltpu.VMEM((2, rows, width), BF),
            pltpu.SemaphoreType.DMA((2, 4)),
            pltpu.VMEM((4, rows, width), BF),
            pltpu.VMEM((2, rows // 2, width), BF),
            pltpu.VMEM((2, rows, width), BF),
            pltpu.SemaphoreType.DMA((2, 4)),
            pltpu.SemaphoreType.DMA((4,)),
            *hop_scratch(height, job_width),
        ],
        compiler_params=pltpu.CompilerParams(
            collective_id=3, has_side_effects=True, vmem_limit_bytes=48 << 20
        ),
        cost_estimate=pl.CostEstimate(
            flops=40_000_000_000, bytes_accessed=20_000_000, transcendentals=0
        ),
    )(
        grads, weight, inputs, gain, later, residual, out_part.reshape(4, rows, width), slabs
    )


class Line:
    def __init__(self):
        self.rank = lax.axis_index("tp")

    def row_order(self, values):
        count = values.shape[0] // 4
        return jnp.concatenate(
            [lax.dynamic_slice_in_dim(values, (self.rank ^ p) * count, count, 0) for p in range(4)]
        )

    def trunk_base(self):
        return self.rank * TRUNK

    def gather_begin(self, rows):
        return rows, by_tp(rows, X_SWAP), by_tp(rows, Y_SWAP)

    def gather_end(self, pieces, hold):
        rows, beside, above, _ = lax.optimization_barrier((*pieces, hold))
        half = rows.shape[0] // 2
        return jnp.concatenate(
            [rows, beside, above, by_tp(beside[:half], Y_SWAP), by_tp(above[half:], X_SWAP)]
        )

    def gather_rows(self, rows):
        half = rows.shape[0] // 2
        beside = by_tp(rows, X_SWAP)
        above = by_tp(rows, Y_SWAP)
        return jnp.concatenate(
            [rows, beside, above, by_tp(beside[:half], Y_SWAP), by_tp(above[half:], X_SWAP)]
        )

    def sum_rows(self, values):
        values = values + by_tp(values, X_SWAP)
        return values + by_tp(values, Y_SWAP)

    def mid_forward(self, attended, weight, inputs, gain):
        residual, normed = mid_forward(attended, weight, inputs, gain)
        return residual, normed.reshape(-1, normed.shape[-1])

    def mid_backward(self, back, residual, cot, gain, weight, slabs):
        grads, gathered, attended, total = mid_backward(back, residual, cot, gain, weight, slabs)
        return grads, gathered.reshape(-1, gathered.shape[-1]), attended, total

    def chunks(self, rows, cot, blocks):
        (full, at, width), second, third = blocks
        slabs, *sums = chunk_pass(rows, cot, full, at, width, None, False, True, False, (), 4)
        first = slabs
        full, at, width = second
        slabs, *sums = chunk_pass(rows, cot, full, at, width, sums, False, True, False, (), 5)
        full, at, width = third
        grads, *sums, total = chunk_pass(
            rows, cot, full, at, width, sums, True, False, True, (first,), 6
        )
        return sums, [total, None, grads], slabs

    def end_backward(self, grads, weight, inputs, gain, later, residual, out_part, operands):
        slabs = pair_hops(*operands)
        return end_backward(grads, weight, inputs, gain, later, residual, out_part, slabs)


class Plain:
    def row_order(self, values):
        return values

    def trunk_base(self):
        return jnp.int32(0)

    def gather_begin(self, rows):
        return rows

    def gather_end(self, rows, hold):
        return self.gather_rows(rows)

    def gather_rows(self, rows):
        return lax.all_gather(rows, "tp", axis=0, tiled=True)

    def scatter_rows(self, partial):
        return lax.psum_scatter(partial.astype(F32), "tp", scatter_dimension=0, tiled=True)

    def sum_rows(self, values):
        return lax.psum(values, "tp")

    def mid_forward(self, attended, weight, inputs, gain):
        residual = inputs.astype(F32) + self.scatter_rows(dot_nt(attended, weight))
        normed = residual * row_scale(residual) * gain.astype(F32)
        normed = self.gather_rows(normed.astype(BF))
        return residual, normed

    def chunks(self, rows, cot, blocks):
        sums = None
        parts = []
        for full, at, width in blocks:
            grads, *sums = chunk_pass(rows, cot, full, at, width, sums, len(parts) == len(blocks) - 1)
            parts.append(scatter_slabs(grads))
        return sums, parts, None

    def mid_backward(self, back, residual, cot, gain, weight, slabs):
        grads = row_grads(residual, gain.astype(F32), self.scatter_rows(back))
        grads = cot.astype(F32) + grads
        gathered = self.gather_rows(grads.astype(BF))
        return grads, gathered, dot_nn(gathered, weight).astype(BF), None

    def end_backward(self, grads, weight, inputs, gain, later, residual, out_part, operands):
        output = (residual + self.scatter_rows(out_part)).astype(BF)
        sums = scatter_slabs(pair_grads(*operands))
        back = self.scatter_rows(dot_nt(grads, weight))
        return later + row_grads(inputs.astype(F32), gain.astype(F32), back), output, sums


def gather_slabs(shard):
    return lax.all_gather(shard, "fsdp", axis=0, tiled=True)


def scatter_slabs(grads):
    return lax.psum_scatter(grads, "fsdp", scatter_dimension=0, tiled=True).astype(F32)


def body(
    make_links,
    layer_input,
    cotangent,
    segment_ids,
    path_positions,
    ancestor_masks,
    attn_gain,
    query_weight,
    key_weight,
    value_weight,
    out_weight,
    mlp_gain,
    gate_weight,
    up_weight,
    down_weight,
):
    links = make_links()
    heads = query_weight.shape[1] // HD
    groups = key_weight.shape[1] // HD
    q_width, kv_width = heads * HD, groups * HD
    qkv_width = q_width + 2 * kv_width
    units = gate_weight.shape[1]
    edges = [units * sum(PARTS[:i]) // sum(PARTS) for i in range(len(PARTS) + 1)]

    gain_rows = gather_slabs(jnp.stack([attn_gain, mlp_gain], axis=1))
    first_gain, second_gain = gain_rows[:, 0][None, :], gain_rows[:, 1][None, :]
    own_qkv = jnp.concatenate([query_weight, key_weight, value_weight], axis=1)
    attn_full = gather_slabs(jnp.concatenate([own_qkv, out_weight.T], axis=1))
    out_full = attn_full[:, qkv_width:]
    qkv_full = lax.optimization_barrier(attn_full[:, :qkv_width])
    own_down = down_weight.T
    own_mlp = [
        jnp.concatenate([gate_weight[:, cut], up_weight[:, cut], own_down[:, cut]], axis=1)
        for cut in map(slice, edges[:-1], edges[1:])
    ]
    early = gather_slabs(jnp.concatenate(own_mlp[:2], axis=1))
    mlp_full = [(early, 0), (early, own_mlp[0].shape[1]), (gather_slabs(own_mlp[2]), 0)]

    positions = links.row_order(path_positions)
    angles = positions.astype(F32)[:, None] * jnp.asarray(inverse_freq(HD))[None, :]
    cosine, sine = jnp.cos(angles), jnp.sin(angles)
    cosine = jnp.concatenate([cosine] * 4, axis=1)
    sine = jnp.concatenate([-sine, sine] * 2, axis=1)
    segs = links.row_order(segment_ids)[::SEG]
    masks = ancestor_masks.reshape(SEGS * SEGS)
    base = jnp.reshape(links.trunk_base(), (1,)).astype(jnp.int32)

    inputs = layer_input.astype(F32)
    first_rows = (inputs * row_scale(inputs) * first_gain.astype(F32)).astype(BF)
    first_normed = links.gather_rows(first_rows)

    qkv_pre = dot_nn(first_normed, qkv_full)
    cot_pieces = links.gather_begin(after(cotangent, qkv_pre))
    attended, queries, keys, vals = attention_forward(
        heads, groups, masks, segs, base, qkv_pre, cosine, sine
    )
    cot_all = links.gather_end(cot_pieces, attended)
    residual, second_normed = links.mid_forward(
        after(attended, qkv_full), out_full, layer_input, second_gain
    )

    widths = [own.shape[1] for own in own_mlp]
    (back_sum, out_part), mlp_sums, slabs = links.chunks(
        second_normed,
        cot_all,
        [(*pair, width) for pair, width in zip(mlp_full, widths)],
    )
    residual_back, branch_back, attended_back, total = links.mid_backward(
        back_sum, residual, cotangent, second_gain, out_full, slabs
    )
    if total is not None:
        mlp_sums = [mlp_sums[0], total, scatter_slabs(after(mlp_sums[2], branch_back))]
    qkv_back = attention_backward(
        heads, groups, masks, segs, base, queries, keys, vals, attended_back, cosine, sine
    )
    thirds = [
        [part[:, at * part.shape[1] // 3 : (at + 1) * part.shape[1] // 3] for part in mlp_sums]
        for at in range(3)
    ]
    room = jnp.zeros_like(thirds[0][2])
    gate_sum, up_sum, down_sum = (
        jnp.concatenate([parts[0], parts[1], room], axis=1) for parts in thirds
    )
    down_sum = down_sum.T
    mlp_parts = [
        jnp.sum(
            (own * part)[:, : 2 * own.shape[1] // 3].astype(F32), axis=1
        )
        for own, part in zip([own.astype(F32) for own in own_mlp], mlp_sums)
    ]
    early_part = mlp_parts[0] + mlp_parts[1]
    residual_back, gate_sum, up_sum, down_sum, early_part = lax.optimization_barrier(
        (residual_back, gate_sum, up_sum, down_sum, early_part)
    )
    input_grad, output, attn_sum = links.end_backward(
        qkv_back,
        qkv_full,
        layer_input,
        first_gain,
        residual_back,
        residual,
        out_part,
        (first_normed, qkv_back, branch_back, attended),
    )
    qkv_sum = attn_sum[:, :qkv_width]

    gate_sum = lax.dynamic_update_slice(gate_sum, thirds[0][2], (0, edges[2]))
    up_sum = lax.dynamic_update_slice(up_sum, thirds[1][2], (0, edges[2]))
    down_sum = lax.dynamic_update_slice(down_sum, thirds[2][2].T, (edges[2], 0))
    attn_part = jnp.sum(own_qkv.astype(F32) * qkv_sum, axis=1)
    mlp_part = early_part + mlp_parts[2]
    attn_total, mlp_total = links.sum_rows(jnp.stack([attn_part, mlp_part]))
    return (
        output,
        input_grad,
        attn_total / attn_gain.astype(F32),
        qkv_sum[:, :q_width],
        qkv_sum[:, q_width : q_width + kv_width],
        qkv_sum[:, q_width + kv_width :],
        attn_sum[:, qkv_width:].T,
        mlp_total / mlp_gain.astype(F32),
        gate_sum,
        up_sum,
        down_sum,
    )


def solution(mesh):
    fits = mesh.shape["fsdp"] == 8 and mesh.shape["tp"] == 4
    return jax.shard_map(
        functools.partial(body, Line if fits else Plain),
        mesh=mesh,
        in_specs=(
            P(("fsdp", "tp"), None),
            P(("fsdp", "tp"), None),
            P("fsdp"),
            P("fsdp"),
            P("fsdp", None, None),
            P("fsdp"),
            P("fsdp", "tp"),
            P("fsdp", "tp"),
            P("fsdp", "tp"),
            P("tp", "fsdp"),
            P("fsdp"),
            P("fsdp", "tp"),
            P("fsdp", "tp"),
            P("tp", "fsdp"),
        ),
        out_specs=(
            P(("fsdp", "tp"), None),
            P(("fsdp", "tp"), None),
            P("fsdp"),
            P("fsdp", "tp"),
            P("fsdp", "tp"),
            P("fsdp", "tp"),
            P("tp", "fsdp"),
            P("fsdp"),
            P("fsdp", "tp"),
            P("fsdp", "tp"),
            P("tp", "fsdp"),
        ),
        check_vma=False,
    )
```

```python
import functools
import math

import jax
import jax.numpy as jnp
import numpy as np
from jax import lax
from jax.experimental import pallas as pl
from jax.experimental.pallas import tpu as pltpu
from jax.sharding import PartitionSpec as P

HD = 64
SEGS = 13
SEG = 64
TRUNK = 256
BRANCHES = 4
EPSILON = 1e-05
PARTS = (2, 3, 3)
NEG = -1e30
BF = jnp.bfloat16
F32 = jnp.float32


def inverse_freq(head_size):
    base_freq = 1.0 / 500000.0 ** (np.arange(0, head_size, 2) / head_size)
    wavelen = 2.0 * math.pi / base_freq
    smooth = (8192.0 / wavelen - 1.0) / 3.0
    blended = (1.0 - smooth) * base_freq / 32.0 + smooth * base_freq
    scaled = np.where(
        wavelen > 8192.0, base_freq / 32.0, np.where(wavelen < 2048.0, base_freq, blended)
    )
    return scaled.astype(np.float32)


def dot_nn(left, right):
    return lax.dot_general(
        left, right, (((1,), (0,)), ((), ())), preferred_element_type=F32
    )


def dot_nt(left, right):
    return lax.dot_general(
        left, right, (((1,), (1,)), ((), ())), preferred_element_type=F32
    )


def dot_tn(left, right):
    return lax.dot_general(
        left, right, (((0,), (0,)), ((), ())), preferred_element_type=F32
    )


def rope_lanes(values, cosine, signed_sine, low_half):
    rolled = jnp.where(low_half, pltpu.roll(values, 96, 1), pltpu.roll(values, 32, 1))
    return values * cosine + rolled * signed_sine


def rope_lanes_back(grads, cosine, signed_sine, low_half):
    scaled = grads * signed_sine
    rolled = jnp.where(low_half, pltpu.roll(scaled, 96, 1), pltpu.roll(scaled, 32, 1))
    return grads * cosine + rolled


def low_half_mask(rows):
    lane = lax.broadcasted_iota(jnp.int32, (rows, 128), 1)
    return lax.rem(lane, HD) < HD // 2


def parent_block(mask_ref, seg_ref, segment, block_count):
    parent = jnp.int32(0)
    for branch in range(1, BRANCHES + 1):
        parent = parent + branch * mask_ref[segment * SEGS + branch]
    parent = jnp.where(segment > BRANCHES, parent, segment)
    found = jnp.int32(0)
    for block in range(block_count):
        found = found + block * (seg_ref[block] == parent).astype(jnp.int32)
    return found


def block_mask(has_parent, members):
    shape = (members * SEG, 2 * SEG)
    row = lax.rem(lax.broadcasted_iota(jnp.int32, shape, 0), SEG)
    col = lax.broadcasted_iota(jnp.int32, shape, 1)
    return ((col < SEG) & has_parent) | ((col >= SEG) & (col - SEG <= row))


def trunk_mask(index, members):
    shape = (members * SEG, TRUNK)
    row = lax.rem(lax.broadcasted_iota(jnp.int32, shape, 0), SEG) + index * SEG
    col = lax.broadcasted_iota(jnp.int32, shape, 1)
    return col <= row


def softmax_rows(scores):
    row_max = jnp.max(scores, axis=-1, keepdims=True)
    exponent = jnp.exp(scores - row_max)
    return exponent / jnp.sum(exponent, axis=-1, keepdims=True)


def attn_fwd_kernel(
    heads, groups, mask_ref, seg_ref, base_ref, pre_ref, cos_ref, sin_ref,
    att_ref, q_ref, k_ref, v_ref,
):
    rows = pre_ref.shape[0]
    blocks = rows // SEG
    members = heads // groups
    score_scale = HD ** (-0.5)
    low_half = low_half_mask(rows)
    cosine = cos_ref[...]
    sine = sin_ref[...]
    q_width = heads * HD
    kv_width = groups * HD

    def put_heads(dest, first, wide, count):
        for half in range(count):
            head = first + half
            part = wide[:, half * HD : (half + 1) * HD].reshape(blocks, SEG, HD)
            group, member = head // members, head % members
            dest[group, :, member * SEG : (member + 1) * SEG, :] = part

    for pair in range(q_width // 128):
        lanes = pre_ref[:, pair * 128 : (pair + 1) * 128]
        put_heads(q_ref, 2 * pair, rope_lanes(lanes, cosine, sine, low_half).astype(BF), 2)
    if kv_width % 128 == 0:
        for pair in range(kv_width // 128):
            at = q_width + pair * 128
            wide = rope_lanes(pre_ref[:, at : at + 128], cosine, sine, low_half).astype(BF)
            at = q_width + kv_width + pair * 128
            plain = pre_ref[:, at : at + 128].astype(BF)
            for half in range(2):
                k_ref[2 * pair + half] = wide[:, half * HD : (half + 1) * HD]
                v_ref[2 * pair + half] = plain[:, half * HD : (half + 1) * HD]
    else:
        both = pre_ref[:, q_width : q_width + 128]
        k_ref[0] = rope_lanes(both, cosine, sine, low_half).astype(BF)[:, :HD]
        v_ref[0] = both.astype(BF)[:, HD:]

    base = base_ref[0]
    trunk_block = base // SEG
    trunk_rows = pl.ds(pl.multiple_of(base, TRUNK), TRUNK)

    def store(group, block, mixed):
        at = pl.ds(pl.multiple_of(block * SEG, SEG), SEG)
        for member in range(members):
            head = group * members + member
            att_ref[at, head * HD : (head + 1) * HD] = mixed[
                member * SEG : (member + 1) * SEG
            ].astype(BF)

    for group in range(groups):
        def one_block(block, carry):
            inside = block - trunk_block
            is_trunk = (inside >= 0) & (inside < TRUNK // SEG)

            @pl.when(is_trunk)
            def _():
                queries = q_ref[group, block]
                scores = dot_nt(queries, k_ref[group, trunk_rows, :]) * score_scale
                scores = jnp.where(trunk_mask(inside, members), scores, NEG)
                probs = softmax_rows(scores).astype(BF)
                store(group, block, dot_nn(probs, v_ref[group, trunk_rows, :]))

            @pl.when(jnp.logical_not(is_trunk))
            def _():
                segment = seg_ref[block]
                parent = parent_block(mask_ref, seg_ref, segment, blocks)
                up = pl.ds(pl.multiple_of(parent * SEG, SEG), SEG)
                own = pl.ds(pl.multiple_of(block * SEG, SEG), SEG)
                queries = q_ref[group, block]
                keys = jnp.concatenate(
                    [k_ref[group, trunk_rows, :], k_ref[group, up, :], k_ref[group, own, :]], axis=0
                )
                vals = jnp.concatenate(
                    [v_ref[group, trunk_rows, :], v_ref[group, up, :], v_ref[group, own, :]], axis=0
                )
                scores = dot_nt(queries, keys) * score_scale
                tail = jnp.where(
                    block_mask(segment > BRANCHES, members), scores[:, TRUNK:], NEG
                )
                scores = jnp.concatenate([scores[:, :TRUNK], tail], axis=1)
                probs = softmax_rows(scores).astype(BF)
                store(group, block, dot_nn(probs, vals))

            return carry

        lax.fori_loop(0, blocks, one_block, 0)


def attn_bwd_kernel(
    heads, groups, mask_ref, seg_ref, base_ref, q_ref, k_ref, v_ref, grad_ref, cos_ref, sin_ref,
    out_ref, g_ref, dq_ref, dk_ref, dv_ref,
):
    rows = grad_ref.shape[0]
    blocks = rows // SEG
    members = heads // groups
    score_scale = HD ** (-0.5)
    low_half = low_half_mask(rows)
    cosine = cos_ref[...]
    sine = sin_ref[...]
    q_width = heads * HD
    kv_width = groups * HD
    for head in range(heads):
        part = grad_ref[:, head * HD : (head + 1) * HD].reshape(blocks, SEG, HD)
        group, member = head // members, head % members
        g_ref[group, :, member * SEG : (member + 1) * SEG, :] = part
    dk_ref[...] = jnp.zeros_like(dk_ref)
    dv_ref[...] = jnp.zeros_like(dv_ref)
    base = base_ref[0]
    trunk_block = base // SEG
    trunk_rows = pl.ds(pl.multiple_of(base, TRUNK), TRUNK)

    def store(group, block, d_query):
        at = pl.ds(pl.multiple_of(block * SEG, SEG), SEG)
        for member in range(members):
            head = group * members + member
            dq_ref[at, head * HD : (head + 1) * HD] = d_query[member * SEG : (member + 1) * SEG]

    for group in range(groups):
        lanes = slice(group * HD, (group + 1) * HD)

        def grads(queries, out_grads, keys, vals, scores):
            probs = softmax_rows(scores)
            prob_back = dot_nt(out_grads, vals)
            delta = jnp.sum(probs * prob_back, axis=-1, keepdims=True)
            score_back = (probs * (prob_back - delta)).astype(BF)
            d_query = dot_nn(score_back, keys) * score_scale
            d_key = dot_tn(score_back, queries) * score_scale
            d_val = dot_tn(probs.astype(BF), out_grads)
            return d_query, d_key, d_val

        def one_block(block, carry):
            inside = block - trunk_block
            is_trunk = (inside >= 0) & (inside < TRUNK // SEG)

            @pl.when(is_trunk)
            def _():
                queries = q_ref[group, block]
                keys = k_ref[group, trunk_rows, :]
                scores = dot_nt(queries, keys) * score_scale
                scores = jnp.where(trunk_mask(inside, members), scores, NEG)
                d_query, d_key, d_val = grads(
                    queries, g_ref[group, block], keys, v_ref[group, trunk_rows, :], scores
                )
                store(group, block, d_query)
                dk_ref[trunk_rows, lanes] += d_key
                dv_ref[trunk_rows, lanes] += d_val

            @pl.when(jnp.logical_not(is_trunk))
            def _():
                segment = seg_ref[block]
                parent = parent_block(mask_ref, seg_ref, segment, blocks)
                up = pl.ds(pl.multiple_of(parent * SEG, SEG), SEG)
                own = pl.ds(pl.multiple_of(block * SEG, SEG), SEG)
                queries = q_ref[group, block]
                keys = jnp.concatenate(
                    [k_ref[group, trunk_rows, :], k_ref[group, up, :], k_ref[group, own, :]], axis=0
                )
                vals = jnp.concatenate(
                    [v_ref[group, trunk_rows, :], v_ref[group, up, :], v_ref[group, own, :]], axis=0
                )
                scores = dot_nt(queries, keys) * score_scale
                tail = jnp.where(
                    block_mask(segment > BRANCHES, members), scores[:, TRUNK:], NEG
                )
                scores = jnp.concatenate([scores[:, :TRUNK], tail], axis=1)
                d_query, d_key, d_val = grads(queries, g_ref[group, block], keys, vals, scores)
                store(group, block, d_query)
                for ref, val in ((dk_ref, d_key), (dv_ref, d_val)):
                    ref[trunk_rows, lanes] += val[:TRUNK]
                    ref[up, lanes] += val[TRUNK : TRUNK + SEG]
                    ref[own, lanes] += val[TRUNK + SEG :]

            return carry

        lax.fori_loop(0, blocks, one_block, 0)
    for pair in range(q_width // 128):
        at = slice(pair * 128, (pair + 1) * 128)
        out_ref[:, at] = rope_lanes_back(dq_ref[:, at], cosine, sine, low_half).astype(BF)
    if kv_width % 128 == 0:
        for pair in range(kv_width // 128):
            at = slice(pair * 128, (pair + 1) * 128)
            turned = rope_lanes_back(dk_ref[:, at], cosine, sine, low_half)
            out_ref[:, q_width + pair * 128 : q_width + (pair + 1) * 128] = turned.astype(BF)
            first = q_width + kv_width + pair * 128
            out_ref[:, first : first + 128] = dv_ref[:, at].astype(BF)
    else:
        wide = jnp.concatenate([dk_ref[...], dv_ref[...]], axis=1)
        turned = rope_lanes_back(wide, cosine, sine, low_half)
        lane = lax.broadcasted_iota(jnp.int32, (rows, 128), 1)
        out_ref[:, q_width : q_width + 128] = jnp.where(lane < HD, turned, wide).astype(BF)


LIGHT = pl.CostEstimate(flops=1000, bytes_accessed=1000, transcendentals=0)
SMEM = pl.BlockSpec(memory_space=pltpu.SMEM)
VMEM = pl.BlockSpec(memory_space=pltpu.VMEM)


def loaded(value):
    return pl.BlockSpec(
        value.shape, lambda i: (0,) * value.ndim, pipeline_mode=pl.Buffered(1)
    )


def attention_forward(heads, groups, masks, segs, base, pre, cosine, sine):
    rows = pre.shape[0]
    members = heads // groups
    blocks = rows // SEG
    return pl.pallas_call(
        functools.partial(attn_fwd_kernel, heads, groups),
        name="attn_fwd",
        out_shape=(
            jax.ShapeDtypeStruct((rows, heads * HD), BF),
            jax.ShapeDtypeStruct((groups, blocks, members * SEG, HD), BF),
            jax.ShapeDtypeStruct((groups, rows, HD), BF),
            jax.ShapeDtypeStruct((groups, rows, HD), BF),
        ),
        in_specs=[SMEM, SMEM, SMEM, VMEM, VMEM, VMEM],
        out_specs=(VMEM, VMEM, VMEM, VMEM),
        compiler_params=pltpu.CompilerParams(vmem_limit_bytes=40 << 20),
        cost_estimate=LIGHT,
    )(masks, segs, base, pre, cosine, sine)


def attention_backward(heads, groups, masks, segs, base, queries, keys, vals, grads, cosine, sine):
    rows = grads.shape[0]
    members = heads // groups
    blocks = rows // SEG
    return pl.pallas_call(
        functools.partial(attn_bwd_kernel, heads, groups),
        name="attn_bwd",
        out_shape=jax.ShapeDtypeStruct((rows, (heads + 2 * groups) * HD), BF),
        grid=(1,),
        in_specs=[SMEM, SMEM, SMEM]
        + [loaded(value) for value in (queries, keys, vals, grads, cosine, sine)],
        out_specs=VMEM,
        scratch_shapes=[
            pltpu.VMEM((groups, blocks, members * SEG, HD), BF),
            pltpu.VMEM((rows, heads * HD), F32),
            pltpu.VMEM((rows, groups * HD), F32),
            pltpu.VMEM((rows, groups * HD), F32),
        ],
        compiler_params=pltpu.CompilerParams(vmem_limit_bytes=40 << 20),
        cost_estimate=LIGHT,
    )(masks, segs, base, queries, keys, vals, grads, cosine, sine)


MESH = pl.DeviceIdType.MESH


def swap_peers():
    rank = lax.axis_index("tp")
    place = lax.axis_index("fsdp")
    return [(place, rank + 1 - 2 * (rank % 2)), (place, (rank + 2) % 4)]


def greet(peers):
    barrier = pltpu.get_barrier_semaphore()
    for peer in peers:
        pl.semaphore_signal(barrier, inc=1, device_id=peer, device_id_type=MESH)
    pl.semaphore_wait(barrier, len(peers))


def send(source, target, send_sem, recv_sem, peer):
    copy = pltpu.make_async_remote_copy(
        src_ref=source,
        dst_ref=target,
        send_sem=send_sem,
        recv_sem=recv_sem,
        device_id=peer,
        device_id_type=MESH,
    )
    copy.start()
    return copy


def line_peers():
    place = lax.axis_index("fsdp")
    rank = lax.axis_index("tp")
    z, core = place // 2, place % 2
    up, down = (z + 1) % 4, (z + 3) % 4
    return z, core, [(2 * z + 1 - core, rank), (2 * up + core, rank), (2 * down + core, rank)]


def far_copies(far_ref, far_recv, send_sem, recv_sem, z, peers):
    heading = z // 2
    place = lax.axis_index("fsdp")
    target = (place + 2 - 4 * heading, lax.axis_index("tp"))
    return pltpu.make_async_remote_copy(
        src_ref=far_ref,
        dst_ref=far_recv.at[heading],
        send_sem=send_sem,
        recv_sem=recv_sem.at[heading],
        device_id=target,
        device_id_type=MESH,
    )


def far_add(pair_ref, far_recv, recv_sem, z, peers):
    @pl.when((z == 1) | (z == 2))
    def _():
        for heading in range(2):
            pltpu.make_async_remote_copy(
                src_ref=far_recv.at[heading],
                dst_ref=far_recv.at[heading],
                send_sem=recv_sem.at[heading],
                recv_sem=recv_sem.at[heading],
                device_id=peers[0],
                device_id_type=MESH,
            ).wait_recv()
        pair_ref[0] = (pair_ref[0].astype(F32) + far_recv[1].astype(F32)).astype(BF)
        pair_ref[1] = (pair_ref[1].astype(F32) + far_recv[0].astype(F32)).astype(BF)


def near_copies(pair_ref, near_recv, send_sem, recv_sem, peers):
    return [
        pltpu.make_async_remote_copy(
            src_ref=pair_ref.at[at],
            dst_ref=near_recv.at[at],
            send_sem=send_sem.at[at],
            recv_sem=recv_sem.at[at],
            device_id=peers[2 - at],
            device_id_type=MESH,
        )
        for at in range(2)
    ]


class Hops:
    def __init__(self, slabs_ref, total_ref, pair_ref, slab_ref, far_recv, near_recv, sends, recvs, loads):
        self.z, _, self.line = line_peers()
        self.total_ref, self.pair_ref, self.slab_ref = total_ref, pair_ref, slab_ref
        self.far_recv, self.near_recv, self.recvs = far_recv, near_recv, recvs
        self.far = far_copies(
            slabs_ref.at[0], far_recv, sends.at[0, 0], recvs.at[0], self.z, self.line
        )
        self.loads = [
            pltpu.make_async_copy(slabs_ref.at[1 + at], pair_ref.at[at], loads.at[at])
            for at in range(2)
        ] + [pltpu.make_async_copy(slabs_ref.at[3], slab_ref, loads.at[2])]
        self.near = near_copies(pair_ref, near_recv, sends.at[1], recvs.at[1], self.line)

    def begin(self):
        self.far.start()
        for load in self.loads:
            load.start()

    def onward(self):
        for load in self.loads:
            load.wait()
        self.far.wait_send()
        far_add(self.pair_ref, self.far_recv, self.recvs.at[0], self.z, self.line)
        for copy in self.near:
            copy.start()

    def finish(self):
        for copy in self.near:
            copy.wait()
        self.total_ref[...] = (
            self.slab_ref[...].astype(F32)
            + self.near_recv[0].astype(F32)
            + self.near_recv[1].astype(F32)
        )


def hop_scratch(height, width):
    return [
        pltpu.VMEM((2, height, width), BF),
        pltpu.VMEM((height, width), BF),
        pltpu.VMEM((2, height, width), BF),
        pltpu.VMEM((2, height, width), BF),
        pltpu.SemaphoreType.DMA((2, 2)),
        pltpu.SemaphoreType.DMA((2, 2)),
        pltpu.SemaphoreType.DMA((3,)),
    ]


SLOTS = (2, 1, 3, 0)


def chunk_kernel(cfg, *refs):
    steps, slabs, first, last, cores, job, offset = cfg
    refs = list(refs)
    take = lambda count: [refs.pop(0) for _ in range(count)]
    rows_ref, cot_ref, source_ref = take(3)
    if not first:
        back_in_ref, out_in_ref = take(2)
    if job:
        (slabs_ref,) = take(1)
    grad_ref, back_ref, out_ref = take(3)
    if job:
        (total_ref,) = take(1)
    pair_ref, hidden_ref, full_ref, full_sem = take(4)
    if cores:
        mine_ref, theirs_ref, core_send, core_recv = take(4)
    if job:
        hops = Hops(slabs_ref, total_ref, *take(7))

    step = pl.program_id(0)
    end = steps + slabs - 1
    chunk = hidden_ref.shape[1]
    tile = chunk // steps
    height = rows_ref.shape[1] // slabs
    fetches = [
        pltpu.make_async_copy(
            source_ref.at[:, pl.ds(offset + third * chunk, chunk)],
            full_ref.at[:, pl.ds(third * chunk, chunk)],
            full_sem.at[third],
        )
        for third in range(3)
    ]

    @pl.when(step == 0)
    def _():
        for fetch in fetches:
            fetch.start()

    def fetched(at, third):
        if at == 0:
            fetches[third].wait()

    if cores or job:
        z, core, peers = line_peers()

        @pl.when(step == 0)
        def _():
            greet(peers)
            if job:
                hops.begin()

    if job:

        @pl.when(step == steps + 1)
        def _():
            hops.onward()

    for at in range(steps):

        @pl.when(step == at)
        def _():
            cut = slice(at * tile, (at + 1) * tile)
            fetched(at, 0)
            gate = dot_nn(rows_ref[...], full_ref[:, cut])
            fetched(at, 1)
            up = dot_nn(rows_ref[...], full_ref[:, chunk + at * tile : chunk + (at + 1) * tile])
            fetched(at, 2)
            back = dot_nn(
                cot_ref[...], full_ref[:, 2 * chunk + at * tile : 2 * chunk + (at + 1) * tile]
            )
            sigmoid = 1.0 / (1.0 + jnp.exp(-gate))
            silu = gate * sigmoid
            hidden_ref[:, cut] = (silu * up).astype(BF)
            pair_ref[:, cut] = (back * up * sigmoid * (1.0 + gate * (1.0 - sigmoid))).astype(BF)
            pair_ref[:, chunk + at * tile : chunk + (at + 1) * tile] = (back * silu).astype(BF)

    def write(slab, target_ref, added_ref):
        at = pl.ds(pl.multiple_of(slab * height, height), height)
        grad = dot_tn(rows_ref[:, at], pair_ref[...])
        more = dot_tn(cot_ref[:, at], hidden_ref[...])
        if added_ref is not None:
            grad = grad.astype(BF).astype(F32) + added_ref[:, : 2 * chunk].astype(F32)
            more = more.astype(BF).astype(F32) + added_ref[:, 2 * chunk :].astype(F32)
        target_ref[:, : 2 * chunk] = grad.astype(BF)
        target_ref[:, 2 * chunk :] = more.astype(BF)

    @pl.when(step >= steps)
    def _():
        slab = pl.ds(pl.multiple_of((step - steps) * height, height), height)
        back = dot_nt(pair_ref[...], full_ref[slab, : 2 * chunk])
        out = dot_nt(hidden_ref[...], full_ref[slab, 2 * chunk :])
        back = back if first else back_in_ref[...] + back
        out = out if first else out_in_ref[...] + out
        back_ref[...] = back.astype(back_ref.dtype)
        out_ref[...] = out.astype(out_ref.dtype)
        if not cores:
            write(step - steps, grad_ref, None)

    if cores:
        copies = [
            pltpu.make_async_remote_copy(
                src_ref=mine_ref.at[at % 2],
                dst_ref=theirs_ref.at[at],
                send_sem=core_send.at[at],
                recv_sem=core_recv.at[at],
                device_id=peers[0],
                device_id_type=MESH,
            )
            for at in range(4)
        ]
        for at, slot in enumerate(SLOTS):
            chip = (z + 4 - slot) % 4

            @pl.when(step == steps + at)
            def _():
                if at >= 2:
                    copies[at - 2].wait_send()
                write(2 * chip + 1 - core, mine_ref.at[at % 2], None)
                copies[at].start()

            @pl.when(step == steps + 4 + at)
            def _():
                copies[at].wait_recv()
                write(2 * chip + core, grad_ref.at[0], theirs_ref.at[at])

        @pl.when(step == end)
        def _():
            copies[2].wait_send()
            copies[3].wait_send()

    if job:

        @pl.when(step == end)
        def _():
            hops.finish()


def chunk_pass(rows, cot, full, at, width, sums, last, cores=False, job=False, operands=(), number=None):
    count, depth = rows.shape
    chunk = width // 3
    slabs = 8
    height = depth // slabs
    steps = max(1, chunk // 256)
    first = sums is None
    whole = pl.BlockSpec(memory_space=pltpu.VMEM)
    anywhere = pl.BlockSpec(memory_space=pl.ANY)

    def place(i):
        return jnp.maximum(i - steps, 0)

    column = pl.BlockSpec((count, height), lambda i: (0, place(i)))
    total = jax.ShapeDtypeStruct((count, depth), BF if last else F32)
    if cores:
        grad_shape = jax.ShapeDtypeStruct((4, height, width), BF)
        grad_spec = pl.BlockSpec((1, height, width), lambda i: (jnp.maximum(place(i) - 4, 0), 0, 0))
    else:
        grad_shape = jax.ShapeDtypeStruct((depth, width), BF)
        grad_spec = pl.BlockSpec((height, width), lambda i: (place(i), 0))
    out_shapes, out_specs = [grad_shape, total, total], [grad_spec, column, column]
    in_specs = [whole, whole, anywhere] + ([] if first else [column, column])
    dma = pltpu.SemaphoreType.DMA
    scratch = [
        pltpu.VMEM((count, 2 * chunk), BF),
        pltpu.VMEM((count, chunk), BF),
        pltpu.VMEM((depth, width), BF),
        dma((3,)),
    ]
    if cores:
        scratch += [
            pltpu.VMEM((2, height, width), BF),
            pltpu.VMEM((4, height, width), BF),
            dma((4,)),
            dma((4,)),
        ]
    if job:
        job_width = operands[0].shape[-1]
        in_specs += [anywhere]
        out_shapes += [jax.ShapeDtypeStruct((height, job_width), F32)]
        out_specs += [whole]
        scratch += hop_scratch(height, job_width)
    remote = cores or job
    return pl.pallas_call(
        functools.partial(chunk_kernel, (steps, slabs, first, last, cores, job, at)),
        name="chunk_pass",
        out_shape=tuple(out_shapes),
        grid=(steps + slabs,),
        in_specs=in_specs,
        out_specs=tuple(out_specs),
        scratch_shapes=scratch,
        input_output_aliases={} if first or last else {3: 1, 4: 2},
        compiler_params=pltpu.CompilerParams(
            vmem_limit_bytes=60 << 20,
            collective_id=number if remote else None,
            has_side_effects=bool(remote),
        ),
        cost_estimate=pl.CostEstimate(
            flops=6 * count * depth * width,
            bytes_accessed=8 * count * depth + 4 * depth * width + 16 * count * depth,
            transcendentals=count * chunk,
        ),
    )(rows, cot, full, *(() if first else sums), *operands)


def pair_kernel(left_ref, first_ref, other_ref, second_ref, out_ref):
    width = first_ref.shape[1]
    out_ref[:, :width] = dot_tn(left_ref[...], first_ref[...]).astype(BF)
    out_ref[:, width:] = dot_tn(other_ref[...], second_ref[...]).astype(BF)


def pair_grads(left, first, other, second):
    count, depth = left.shape
    width = first.shape[1] + second.shape[1]
    height = 256
    whole = pl.BlockSpec(memory_space=pltpu.VMEM)
    column = pl.BlockSpec((count, height), lambda i: (0, i))
    return pl.pallas_call(
        pair_kernel,
        name="pair_grads",
        out_shape=jax.ShapeDtypeStruct((depth, width), BF),
        grid=(depth // height,),
        in_specs=[column, whole, column, whole],
        out_specs=pl.BlockSpec((height, width), lambda i: (i, 0)),
        compiler_params=pltpu.CompilerParams(vmem_limit_bytes=32 << 20),
        cost_estimate=LIGHT,
    )(left, first, other, second)


def pair_hops_kernel(
    left_ref, first_ref, other_ref, second_ref, out_ref, mine_ref, theirs_ref, core_send, core_recv
):
    step = pl.program_id(0)
    z, core, peers = line_peers()
    width = first_ref.shape[1]
    height = out_ref.shape[1]

    def write(slab, target_ref, added_ref):
        at = pl.ds(pl.multiple_of(slab * height, height), height)
        grad = dot_tn(left_ref[:, at], first_ref[...])
        more = dot_tn(other_ref[:, at], second_ref[...])
        if added_ref is not None:
            grad = grad.astype(BF).astype(F32) + added_ref[:, :width].astype(F32)
            more = more.astype(BF).astype(F32) + added_ref[:, width:].astype(F32)
        target_ref[:, :width] = grad.astype(BF)
        target_ref[:, width:] = more.astype(BF)

    @pl.when(step == 0)
    def _():
        greet(peers[:1])

    copies = [
        pltpu.make_async_remote_copy(
            src_ref=mine_ref.at[at],
            dst_ref=theirs_ref.at[at],
            send_sem=core_send.at[at],
            recv_sem=core_recv.at[at],
            device_id=peers[0],
            device_id_type=MESH,
        )
        for at in range(4)
    ]
    for at, slot in enumerate(SLOTS):
        chip = (z + 4 - slot) % 4

        @pl.when(step == at)
        def _():
            write(2 * chip + 1 - core, mine_ref.at[at], None)
            copies[at].start()

        @pl.when(step == 4 + at)
        def _():
            copies[at].wait_recv()
            write(2 * chip + core, out_ref.at[0], theirs_ref.at[at])

    @pl.when(step == 7)
    def _():
        for copy in copies:
            copy.wait_send()


def pair_hops(left, first, other, second):
    count, depth = left.shape
    width = first.shape[1] + second.shape[1]
    height = depth // 8
    return pl.pallas_call(
        pair_hops_kernel,
        name="pair_hops",
        out_shape=jax.ShapeDtypeStruct((4, height, width), BF),
        grid=(8,),
        in_specs=[VMEM] * 4,
        out_specs=pl.BlockSpec((1, height, width), lambda i: (jnp.maximum(i - 4, 0), 0, 0)),
        scratch_shapes=[
            pltpu.VMEM((4, height, width), BF),
            pltpu.VMEM((4, height, width), BF),
            pltpu.SemaphoreType.DMA((4,)),
            pltpu.SemaphoreType.DMA((4,)),
        ],
        compiler_params=pltpu.CompilerParams(
            collective_id=7, has_side_effects=True, vmem_limit_bytes=48 << 20
        ),
        cost_estimate=pl.CostEstimate(
            flops=2 * count * depth * width,
            bytes_accessed=4 * count * depth + 2 * depth * width,
            transcendentals=0,
        ),
    )(left, first, other, second)


X_SWAP = [(i, i ^ 1) for i in range(4)]
Y_SWAP = [(i, i ^ 2) for i in range(4)]


def by_tp(value, pairs):
    return lax.ppermute(value, "tp", pairs)


def after(value, *earlier):
    return lax.optimization_barrier((value, *earlier))[0]


def sum_pieces(part_ref, make, half_ref, whole_ref, send_sem, recv_sem, peers, meanwhile):
    half = part_ref.shape[1] // 2
    make(3)
    copies = [
        send(
            part_ref.at[3, pl.ds(axis * half, half)],
            half_ref.at[axis],
            send_sem.at[axis],
            recv_sem.at[axis],
            peers[axis],
        )
        for axis in range(2)
    ]
    for piece in (1, 2, 0):
        make(piece)
    meanwhile(0)
    for copy in copies:
        copy.wait()
    part_ref[2, :half] = (part_ref[2, :half].astype(F32) + half_ref[0].astype(F32)).astype(BF)
    part_ref[1, half:] = (part_ref[1, half:].astype(F32) + half_ref[1].astype(F32)).astype(BF)
    copies = [
        send(
            part_ref.at[1 + axis],
            whole_ref.at[axis],
            send_sem.at[2 + axis],
            recv_sem.at[2 + axis],
            peers[axis],
        )
        for axis in range(2)
    ]
    meanwhile(1)
    for copy in copies:
        copy.wait()
    return part_ref[0].astype(F32) + whole_ref[0].astype(F32) + whole_ref[1].astype(F32)


def gather_pieces(all_ref, send_sem, recv_sem, peers, meanwhile):
    half = all_ref.shape[1] // 2
    copies = [
        send(all_ref.at[0], all_ref.at[1 + axis], send_sem.at[axis], recv_sem.at[axis], peers[axis])
        for axis in range(2)
    ]
    meanwhile(2)
    for copy in copies:
        copy.wait()
    copies = []
    for axis in range(2):
        rows = pl.ds(axis * half, half)
        copies.append(
            send(
                all_ref.at[1 + axis, rows],
                all_ref.at[3, rows],
                send_sem.at[2 + axis],
                recv_sem.at[2 + axis],
                peers[1 - axis],
            )
        )
    meanwhile(3)
    for copy in copies:
        copy.wait()


def idle(stage):
    return None


def row_scale(values):
    return lax.rsqrt(jnp.mean(values * values, axis=-1, keepdims=True) + EPSILON)


def mid_forward_kernel(
    attended_ref, weight_ref, input_ref, gain_ref,
    residual_ref, all_ref,
    part_ref, half_ref, whole_ref, sems,
):
    peers = swap_peers()
    rows = input_ref.shape[0]
    greet(peers)

    def make(piece):
        part_ref[piece] = dot_nt(
            attended_ref[piece * rows : (piece + 1) * rows], weight_ref[...]
        ).astype(BF)

    summed = sum_pieces(part_ref, make, half_ref, whole_ref, sems.at[0], sems.at[1], peers, idle)
    residual = input_ref[...].astype(F32) + summed
    residual_ref[...] = residual
    all_ref[0] = (residual * row_scale(residual) * gain_ref[...].astype(F32)).astype(BF)
    gather_pieces(all_ref, sems.at[2], sems.at[3], peers, idle)


def mid_forward(attended, weight, inputs, gain):
    rows, width = inputs.shape
    return pl.pallas_call(
        mid_forward_kernel,
        name="mid_forward",
        out_shape=(
            jax.ShapeDtypeStruct((rows, width), F32),
            jax.ShapeDtypeStruct((4, rows, width), BF),
        ),
        in_specs=[VMEM] * 4,
        out_specs=(VMEM,) * 2,
        scratch_shapes=[
            pltpu.VMEM((4, rows, width), BF),
            pltpu.VMEM((2, rows // 2, width), BF),
            pltpu.VMEM((2, rows, width), BF),
            pltpu.SemaphoreType.DMA((4, 4)),
        ],
        compiler_params=pltpu.CompilerParams(
            collective_id=1, has_side_effects=True, vmem_limit_bytes=56 << 20
        ),
        cost_estimate=pl.CostEstimate(
            flops=80_000_000_000, bytes_accessed=20_000_000, transcendentals=0
        ),
    )(attended, weight, inputs, gain)


def row_grads(values, gain, back):
    scale = row_scale(values)
    scaled = back * gain
    return scale * scaled - values * (scale * scale * scale) * jnp.mean(
        scaled * values, axis=-1, keepdims=True
    )


def mid_backward_kernel(
    back_ref, residual_ref, cot_ref, gain_ref, weight_ref, slabs_ref,
    out_ref, all_ref, attended_ref, total_ref,
    part_ref, half_ref, whole_ref, sems, load_sem, *hop_refs,
):
    peers = swap_peers()
    hops = Hops(slabs_ref, total_ref, *hop_refs)
    greet(peers + hops.line[1:])
    hops.begin()

    rows = residual_ref.shape[0]

    def project(piece):
        attended_ref[piece * rows : (piece + 1) * rows] = dot_nn(
            all_ref[piece], weight_ref[...]
        ).astype(BF)

    def meanwhile(stage):
        if stage == 1:
            hops.onward()
        if stage == 2:
            project(0)
        if stage == 3:
            project(1)
            project(2)

    order = (3, 1, 2, 0)
    loads = [
        pltpu.make_async_copy(back_ref.at[piece], part_ref.at[piece], load_sem.at[piece])
        for piece in range(4)
    ]
    for piece in order:
        loads[piece].start()
    summed = sum_pieces(
        part_ref, lambda piece: loads[piece].wait(), half_ref, whole_ref,
        sems.at[0], sems.at[1], peers, meanwhile,
    )
    grads = cot_ref[...].astype(F32) + row_grads(
        residual_ref[...], gain_ref[...].astype(F32), summed
    )
    out_ref[...] = grads
    all_ref[0] = grads.astype(BF)
    gather_pieces(all_ref, sems.at[2], sems.at[3], peers, meanwhile)
    project(3)
    hops.finish()


def mid_backward(back, residual, cot, gain, weight, slabs):
    rows, width = residual.shape
    _, height, job_width = slabs.shape
    return pl.pallas_call(
        mid_backward_kernel,
        name="mid_backward",
        out_shape=(
            jax.ShapeDtypeStruct((rows, width), F32),
            jax.ShapeDtypeStruct((4, rows, width), BF),
            jax.ShapeDtypeStruct((4 * rows, weight.shape[1]), BF),
            jax.ShapeDtypeStruct((height, job_width), F32),
        ),
        in_specs=[
            pl.BlockSpec(memory_space=pl.ANY),
            VMEM,
            VMEM,
            VMEM,
            VMEM,
            pl.BlockSpec(memory_space=pl.ANY),
        ],
        out_specs=(VMEM,) * 4,
        scratch_shapes=[
            pltpu.VMEM((4, rows, width), BF),
            pltpu.VMEM((2, rows // 2, width), BF),
            pltpu.VMEM((2, rows, width), BF),
            pltpu.SemaphoreType.DMA((4, 4)),
            pltpu.SemaphoreType.DMA((4,)),
            *hop_scratch(height, job_width),
        ],
        compiler_params=pltpu.CompilerParams(
            collective_id=2, has_side_effects=True, vmem_limit_bytes=48 << 20
        ),
        cost_estimate=pl.CostEstimate(
            flops=80_000_000_000, bytes_accessed=20_000_000, transcendentals=0
        ),
    )(back.reshape(4, rows, width), residual, cot, gain, weight, slabs)


def end_backward_kernel(
    grads_ref, weight_ref, input_ref, gain_ref, later_ref, residual_ref, rows_ref, slabs_ref,
    out_ref, sum_ref, total_ref,
    part_ref, half_ref, whole_ref, sems, rows_part_ref, rows_half_ref, rows_whole_ref, rows_sems,
    load_sem, *hop_refs,
):
    loads = [
        pltpu.make_async_copy(rows_ref.at[piece], rows_part_ref.at[piece], load_sem.at[piece])
        for piece in range(4)
    ]
    peers = swap_peers()
    rows = input_ref.shape[0]
    hops = Hops(slabs_ref, total_ref, *hop_refs)
    greet(peers + hops.line[1:])
    hops.begin()

    def meanwhile(stage):
        if stage == 0:
            for load in loads:
                load.start()
        if stage == 1:
            hops.onward()

    def make(piece):
        part_ref[piece] = dot_nt(
            grads_ref[piece * rows : (piece + 1) * rows], weight_ref[...]
        ).astype(BF)

    summed = sum_pieces(
        part_ref, make, half_ref, whole_ref, sems.at[0], sems.at[1], peers, meanwhile
    )

    def finish(stage):
        if stage == 0:
            out_ref[...] = later_ref[...] + row_grads(
                input_ref[...].astype(F32), gain_ref[...].astype(F32), summed
            )

    summed_rows = sum_pieces(
        rows_part_ref, lambda piece: loads[piece].wait(), rows_half_ref, rows_whole_ref,
        rows_sems.at[0], rows_sems.at[1], peers, finish,
    )
    sum_ref[...] = (residual_ref[...] + summed_rows).astype(BF)
    hops.finish()


def end_backward(grads, weight, inputs, gain, later, residual, out_part, slabs):
    rows, width = inputs.shape
    _, height, job_width = slabs.shape
    return pl.pallas_call(
        end_backward_kernel,
        name="end_backward",
        out_shape=(
            jax.ShapeDtypeStruct((rows, width), F32),
            jax.ShapeDtypeStruct((rows, width), BF),
            jax.ShapeDtypeStruct((height, job_width), F32),
        ),
        in_specs=[VMEM] * 6 + [pl.BlockSpec(memory_space=pl.ANY)] * 2,
        out_specs=(VMEM,) * 3,
        scratch_shapes=[
            pltpu.VMEM((4, rows, width), BF),
            pltpu.VMEM((2, rows // 2, width), BF),
            pltpu.VMEM((2, rows, width), BF),
            pltpu.SemaphoreType.DMA((2, 4)),
            pltpu.VMEM((4, rows, width), BF),
            pltpu.VMEM((2, rows // 2, width), BF),
            pltpu.VMEM((2, rows, width), BF),
            pltpu.SemaphoreType.DMA((2, 4)),
            pltpu.SemaphoreType.DMA((4,)),
            *hop_scratch(height, job_width),
        ],
        compiler_params=pltpu.CompilerParams(
            collective_id=3, has_side_effects=True, vmem_limit_bytes=48 << 20
        ),
        cost_estimate=pl.CostEstimate(
            flops=40_000_000_000, bytes_accessed=20_000_000, transcendentals=0
        ),
    )(
        grads, weight, inputs, gain, later, residual, out_part.reshape(4, rows, width), slabs
    )


class Line:
    def __init__(self):
        self.rank = lax.axis_index("tp")

    def row_order(self, values):
        count = values.shape[0] // 4
        return jnp.concatenate(
            [lax.dynamic_slice_in_dim(values, (self.rank ^ p) * count, count, 0) for p in range(4)]
        )

    def trunk_base(self):
        return self.rank * TRUNK

    def gather_begin(self, rows):
        return rows, by_tp(rows, X_SWAP), by_tp(rows, Y_SWAP)

    def gather_end(self, pieces, hold):
        rows, beside, above, _ = lax.optimization_barrier((*pieces, hold))
        half = rows.shape[0] // 2
        return jnp.concatenate(
            [rows, beside, above, by_tp(beside[:half], Y_SWAP), by_tp(above[half:], X_SWAP)]
        )

    def gather_rows(self, rows):
        half = rows.shape[0] // 2
        beside = by_tp(rows, X_SWAP)
        above = by_tp(rows, Y_SWAP)
        return jnp.concatenate(
            [rows, beside, above, by_tp(beside[:half], Y_SWAP), by_tp(above[half:], X_SWAP)]
        )

    def sum_rows(self, values):
        values = values + by_tp(values, X_SWAP)
        return values + by_tp(values, Y_SWAP)

    def mid_forward(self, attended, weight, inputs, gain):
        residual, normed = mid_forward(attended, weight, inputs, gain)
        return residual, normed.reshape(-1, normed.shape[-1])

    def mid_backward(self, back, residual, cot, gain, weight, slabs):
        grads, gathered, attended, total = mid_backward(back, residual, cot, gain, weight, slabs)
        return grads, gathered.reshape(-1, gathered.shape[-1]), attended, total

    def chunks(self, rows, cot, blocks):
        (full, at, width), second, third = blocks
        slabs, *sums = chunk_pass(rows, cot, full, at, width, None, False, True, False, (), 4)
        first = slabs
        full, at, width = second
        slabs, *sums = chunk_pass(rows, cot, full, at, width, sums, False, True, False, (), 5)
        full, at, width = third
        grads, *sums, total = chunk_pass(
            rows, cot, full, at, width, sums, True, False, True, (first,), 6
        )
        return sums, [total, None, grads], slabs

    def end_backward(self, grads, weight, inputs, gain, later, residual, out_part, operands):
        slabs = pair_hops(*operands)
        return end_backward(grads, weight, inputs, gain, later, residual, out_part, slabs)


class Plain:
    def row_order(self, values):
        return values

    def trunk_base(self):
        return jnp.int32(0)

    def gather_begin(self, rows):
        return rows

    def gather_end(self, rows, hold):
        return self.gather_rows(rows)

    def gather_rows(self, rows):
        return lax.all_gather(rows, "tp", axis=0, tiled=True)

    def scatter_rows(self, partial):
        return lax.psum_scatter(partial.astype(F32), "tp", scatter_dimension=0, tiled=True)

    def sum_rows(self, values):
        return lax.psum(values, "tp")

    def mid_forward(self, attended, weight, inputs, gain):
        residual = inputs.astype(F32) + self.scatter_rows(dot_nt(attended, weight))
        normed = residual * row_scale(residual) * gain.astype(F32)
        normed = self.gather_rows(normed.astype(BF))
        return residual, normed

    def chunks(self, rows, cot, blocks):
        sums = None
        parts = []
        for full, at, width in blocks:
            grads, *sums = chunk_pass(rows, cot, full, at, width, sums, len(parts) == len(blocks) - 1)
            parts.append(scatter_slabs(grads))
        return sums, parts, None

    def mid_backward(self, back, residual, cot, gain, weight, slabs):
        grads = row_grads(residual, gain.astype(F32), self.scatter_rows(back))
        grads = cot.astype(F32) + grads
        gathered = self.gather_rows(grads.astype(BF))
        return grads, gathered, dot_nn(gathered, weight).astype(BF), None

    def end_backward(self, grads, weight, inputs, gain, later, residual, out_part, operands):
        output = (residual + self.scatter_rows(out_part)).astype(BF)
        sums = scatter_slabs(pair_grads(*operands))
        back = self.scatter_rows(dot_nt(grads, weight))
        return later + row_grads(inputs.astype(F32), gain.astype(F32), back), output, sums


def gather_slabs(shard):
    return lax.all_gather(shard, "fsdp", axis=0, tiled=True)


def scatter_slabs(grads):
    return lax.psum_scatter(grads, "fsdp", scatter_dimension=0, tiled=True).astype(F32)


def body(
    make_links,
    layer_input,
    cotangent,
    segment_ids,
    path_positions,
    ancestor_masks,
    attn_gain,
    query_weight,
    key_weight,
    value_weight,
    out_weight,
    mlp_gain,
    gate_weight,
    up_weight,
    down_weight,
):
    links = make_links()
    heads = query_weight.shape[1] // HD
    groups = key_weight.shape[1] // HD
    q_width, kv_width = heads * HD, groups * HD
    qkv_width = q_width + 2 * kv_width
    units = gate_weight.shape[1]
    edges = [units * sum(PARTS[:i]) // sum(PARTS) for i in range(len(PARTS) + 1)]

    gain_rows = gather_slabs(jnp.stack([attn_gain, mlp_gain], axis=1))
    first_gain, second_gain = gain_rows[:, 0][None, :], gain_rows[:, 1][None, :]
    own_qkv = jnp.concatenate([query_weight, key_weight, value_weight], axis=1)
    attn_full = gather_slabs(jnp.concatenate([own_qkv, out_weight.T], axis=1))
    out_full = attn_full[:, qkv_width:]
    qkv_full = lax.optimization_barrier(attn_full[:, :qkv_width])
    own_down = down_weight.T
    own_mlp = [
        jnp.concatenate([gate_weight[:, cut], up_weight[:, cut], own_down[:, cut]], axis=1)
        for cut in map(slice, edges[:-1], edges[1:])
    ]
    early = gather_slabs(jnp.concatenate(own_mlp[:2], axis=1))
    mlp_full = [(early, 0), (early, own_mlp[0].shape[1]), (gather_slabs(own_mlp[2]), 0)]

    positions = links.row_order(path_positions)
    angles = positions.astype(F32)[:, None] * jnp.asarray(inverse_freq(HD))[None, :]
    cosine, sine = jnp.cos(angles), jnp.sin(angles)
    cosine = jnp.concatenate([cosine] * 4, axis=1)
    sine = jnp.concatenate([-sine, sine] * 2, axis=1)
    segs = links.row_order(segment_ids)[::SEG]
    masks = ancestor_masks.reshape(SEGS * SEGS)
    base = jnp.reshape(links.trunk_base(), (1,)).astype(jnp.int32)

    inputs = layer_input.astype(F32)
    first_rows = (inputs * row_scale(inputs) * first_gain.astype(F32)).astype(BF)
    first_normed = links.gather_rows(first_rows)

    qkv_pre = dot_nn(first_normed, qkv_full)
    cot_pieces = links.gather_begin(after(cotangent, qkv_pre))
    attended, queries, keys, vals = attention_forward(
        heads, groups, masks, segs, base, qkv_pre, cosine, sine
    )
    cot_all = links.gather_end(cot_pieces, attended)
    residual, second_normed = links.mid_forward(
        after(attended, qkv_full), out_full, layer_input, second_gain
    )

    widths = [own.shape[1] for own in own_mlp]
    (back_sum, out_part), mlp_sums, slabs = links.chunks(
        second_normed,
        cot_all,
        [(*pair, width) for pair, width in zip(mlp_full, widths)],
    )
    residual_back, branch_back, attended_back, total = links.mid_backward(
        back_sum, residual, cotangent, second_gain, out_full, slabs
    )
    if total is not None:
        mlp_sums = [mlp_sums[0], total, scatter_slabs(after(mlp_sums[2], branch_back))]
    qkv_back = attention_backward(
        heads, groups, masks, segs, base, queries, keys, vals, attended_back, cosine, sine
    )
    thirds = [
        [part[:, at * part.shape[1] // 3 : (at + 1) * part.shape[1] // 3] for part in mlp_sums]
        for at in range(3)
    ]
    room = jnp.zeros_like(thirds[0][2])
    gate_sum, up_sum, down_sum = (
        jnp.concatenate([parts[0], parts[1], room], axis=1) for parts in thirds
    )
    down_sum = down_sum.T
    mlp_parts = [
        jnp.sum(
            (own * part)[:, : 2 * own.shape[1] // 3].astype(F32), axis=1
        )
        for own, part in zip([own.astype(F32) for own in own_mlp], mlp_sums)
    ]
    early_part = mlp_parts[0] + mlp_parts[1]
    residual_back, gate_sum, up_sum, down_sum, early_part = lax.optimization_barrier(
        (residual_back, gate_sum, up_sum, down_sum, early_part)
    )
    input_grad, output, attn_sum = links.end_backward(
        qkv_back,
        qkv_full,
        layer_input,
        first_gain,
        residual_back,
        residual,
        out_part,
        (first_normed, qkv_back, branch_back, attended),
    )
    qkv_sum = attn_sum[:, :qkv_width]

    gate_sum = lax.dynamic_update_slice(gate_sum, thirds[0][2], (0, edges[2]))
    up_sum = lax.dynamic_update_slice(up_sum, thirds[1][2], (0, edges[2]))
    down_sum = lax.dynamic_update_slice(down_sum, thirds[2][2].T, (edges[2], 0))
    attn_part = jnp.sum(own_qkv.astype(F32) * qkv_sum, axis=1)
    mlp_part = early_part + mlp_parts[2]
    attn_total, mlp_total = links.sum_rows(jnp.stack([attn_part, mlp_part]))
    return (
        output,
        input_grad,
        attn_total / attn_gain.astype(F32),
        qkv_sum[:, :q_width],
        qkv_sum[:, q_width : q_width + kv_width],
        qkv_sum[:, q_width + kv_width :],
        attn_sum[:, qkv_width:].T,
        mlp_total / mlp_gain.astype(F32),
        gate_sum,
        up_sum,
        down_sum,
    )


def solution(mesh):
    fits = mesh.shape["fsdp"] == 8 and mesh.shape["tp"] == 4
    return jax.shard_map(
        functools.partial(body, Line if fits else Plain),
        mesh=mesh,
        in_specs=(
            P(("fsdp", "tp"), None),
            P(("fsdp", "tp"), None),
            P("fsdp"),
            P("fsdp"),
            P("fsdp", None, None),
            P("fsdp"),
            P("fsdp", "tp"),
            P("fsdp", "tp"),
            P("fsdp", "tp"),
            P("tp", "fsdp"),
            P("fsdp"),
            P("fsdp", "tp"),
            P("fsdp", "tp"),
            P("tp", "fsdp"),
        ),
        out_specs=(
            P(("fsdp", "tp"), None),
            P(("fsdp", "tp"), None),
            P("fsdp"),
            P("fsdp", "tp"),
            P("fsdp", "tp"),
            P("fsdp", "tp"),
            P("tp", "fsdp"),
            P("fsdp"),
            P("fsdp", "tp"),
            P("fsdp", "tp"),
            P("tp", "fsdp"),
        ),
        check_vma=False,
    )
```
